32 devices in a mesh: dp: 4 (over x, core), ctx: 8 (over z, y).
Axes of the slice: x: 2, y: 2, z: 4, core: 2. Of those that a mesh axis runs over, the one named last changes fastest.
Arguments:
- tokens: bfloat16 [16384, 1152], P(('dp', 'ctx')), may hold values from -6 to 6
- attention_gain: bfloat16 [1152], P(('dp', 'ctx')), may hold values from 0.099609375 to 1.8984375
- query_weight: bfloat16 [1152, 1024], P(('dp', 'ctx')), may hold values from -0.1875 to 0.1875
- key_weight: bfloat16 [1152, 256], P(('dp', 'ctx')), may hold values from -0.1875 to 0.1875
- value_weight: bfloat16 [1152, 256], P(('dp', 'ctx')), may hold values from -0.1875 to 0.1875
- query_gain: bfloat16 [256], P(('dp', 'ctx')), may hold values from 1 to 2
- key_gain: bfloat16 [256], P(('dp', 'ctx')), may hold values from 1 to 2
- output_weight: bfloat16 [1024, 1152], P(('dp', 'ctx')), may hold values from -0.1875 to 0.1875
- mixed_gain: bfloat16 [1152], P(('dp', 'ctx')), may hold values from 0.099609375 to 1.8984375
- feed_gain: bfloat16 [1152], P(('dp', 'ctx')), may hold values from 0.099609375 to 1.8984375
- gate_weight: bfloat16 [1152, 6912], P(('dp', 'ctx')), may hold values from -0.1875 to 0.1875
- up_weight: bfloat16 [1152, 6912], P(('dp', 'ctx')), may hold values from -0.1875 to 0.1875
- down_weight: bfloat16 [6912, 1152], P(('dp', 'ctx')), may hold values from -0.078125 to 0.078125
- final_gain: bfloat16 [1152], P(('dp', 'ctx')), may hold values from 0.099609375 to 1.8984375
- segment_ids: int32 [16384], P('dp'), may hold values from 0 to 4, as said below
- positions: int32 [16384], P('dp'), may hold values from 0 to 2559, as said below
- cotangent: bfloat16 [16384, 1152], P(('dp', 'ctx')), may hold values from -6 to 6
Outputs:
- layer_out: bfloat16 [16384, 1152], P(('dp', 'ctx'))
- tokens_grad: bfloat16 [16384, 1152], P(('dp', 'ctx'))
- attention_gain_grad: float32 [1152], P(('dp', 'ctx'))
- query_weight_grad: float32 [1152, 1024], P(('dp', 'ctx'))
- key_weight_grad: float32 [1152, 256], P(('dp', 'ctx'))
- value_weight_grad: float32 [1152, 256], P(('dp', 'ctx'))
- query_gain_grad: float32 [256], P(('dp', 'ctx'))
- key_gain_grad: float32 [256], P(('dp', 'ctx'))
- output_weight_grad: float32 [1024, 1152], P(('dp', 'ctx'))
- mixed_gain_grad: float32 [1152], P(('dp', 'ctx'))
- feed_gain_grad: float32 [1152], P(('dp', 'ctx'))
- gate_weight_grad: float32 [1152, 6912], P(('dp', 'ctx'))
- up_weight_grad: float32 [1152, 6912], P(('dp', 'ctx'))
- down_weight_grad: float32 [6912, 1152], P(('dp', 'ctx'))
- final_gain_grad: float32 [1152], P(('dp', 'ctx'))
The draws below stay inside these ranges and needn't reach their ends.
Inputs may be any that keep to these rules, and one draw needn't show every extreme that they name: `segment_ids`: each group's tokens form aligned blocks of 512. 2048 / 512 blocks, at places drawn from the seed, hold the prompt, segment id 0; each other block is one whole continuation, with its own id, and each id of 1 to 4 occurs in every group. `positions`: A prompt token's position is its place in the prompt, each of 0 to 2047 once a group; a continuation's token has 2048 plus its place in the continuation.
All inputs are finite; a program needn't handle non-finite values.
Results may differ from the reference program's by a relative error of at most 0.035.
Values may be sent and summed in bfloat16 or wider, within the bound.
A program may use at most 384 MiB of HBM per device.

```python
import jax
import jax.numpy as jnp
from jax import lax

D = 1152
FF = 6912
HQ = 4
HD = 256
CONT = 512
PROMPT = 2048
GROUP = 4096
TOKENS = 16384
N_DP = 4


def layout_blocks(key):
    count_blocks = GROUP // CONT
    group_keys = jax.random.split(jax.random.fold_in(key, 7), N_DP)
    return jax.vmap(lambda single_key: jax.random.permutation(single_key, count_blocks))(group_keys).astype(jnp.int32)


def draw_segment_ids(key, part):
    logical = layout_blocks(key)
    prompt_blocks = PROMPT // CONT
    block_ids = jnp.where(logical < prompt_blocks, 0, logical - prompt_blocks + 1)
    return jnp.repeat(block_ids, CONT, axis=1).reshape(-1).astype(jnp.int32)


def draw_positions(key, part):
    logical = layout_blocks(key)
    prompt_blocks = PROMPT // CONT
    offsets = jnp.arange(CONT, dtype=jnp.int32)
    starts = jnp.where(logical < prompt_blocks, logical * CONT, PROMPT)
    return (starts[:, :, None] + offsets[None, None, :]).reshape(-1).astype(jnp.int32)


def block_levels(key, extent, cuts, least, high):
    def one(dim, shards_of):
        draws = jax.random.uniform(jax.random.fold_in(jax.random.fold_in(key, 6), dim), (shards_of,), jnp.float32, least / len(cuts), high / len(cuts))
        return jnp.repeat(jnp.exp(draws), extent[dim] // shards_of).reshape((-1,) + (1,) * (len(extent) - dim - 1))

    loudness = one(*cuts[0])
    for cut in cuts[1:]:
        loudness = loudness * one(*cut)
    return loudness


def normal_values(own_key, dims, scale, bound, cuts=(), kind=jnp.bfloat16):
    array = scale * jax.random.normal(own_key, dims, jnp.float32)
    if cuts:
        array = array * block_levels(own_key, dims, cuts, -0.22, 0.18)
    return jnp.clip(array, -bound, bound).astype(kind)


def setup_inputs(seed: int = 0) -> dict:
    key_of = jax.random.split(jax.random.key(seed), 18)
    tokens = normal_values(key_of[0], (TOKENS, D), 1.0, 6.0, ((0, 32),))
    attention_gain = jnp.clip(1.0 + 0.18 * jax.random.normal(key_of[1], (D,), jnp.float32), 0.099609375, 1.8984375).astype(jnp.bfloat16)
    query_weight = normal_values(key_of[2], (D, HQ * HD), D ** -0.5, 0.1875, ((0, 32),))
    key_weight = normal_values(key_of[3], (D, HD), D ** -0.5, 0.1875, ((0, 32),))
    value_weight = normal_values(key_of[4], (D, HD), D ** -0.5, 0.1875, ((0, 32),))
    query_gain = jnp.clip(1.0 + 1.0 * jax.random.uniform(key_of[5], (HD,), jnp.float32) ** block_levels(key_of[5], (HD,), ((0, 32),), -0.2, 0.2), 1.0, 2.0).astype(jnp.bfloat16)
    key_gain = jnp.clip(1.0 + 1.0 * jax.random.uniform(key_of[6], (HD,), jnp.float32) ** block_levels(key_of[6], (HD,), ((0, 32),), -0.2, 0.2), 1.0, 2.0).astype(jnp.bfloat16)
    output_weight = normal_values(key_of[7], (HQ * HD, D), (HQ * HD) ** -0.5, 0.1875, ((0, 32),))
    mixed_gain = jnp.clip(1.0 + 0.18 * jax.random.normal(key_of[8], (D,), jnp.float32), 0.099609375, 1.8984375).astype(jnp.bfloat16)
    feed_gain = jnp.clip(1.0 + 0.18 * jax.random.normal(key_of[9], (D,), jnp.float32), 0.099609375, 1.8984375).astype(jnp.bfloat16)
    gate_weight = normal_values(key_of[10], (D, FF), D ** -0.5, 0.1875, ((0, 32),))
    up_weight = normal_values(key_of[11], (D, FF), D ** -0.5, 0.1875, ((0, 32),))
    down_weight = normal_values(key_of[12], (FF, D), FF ** -0.5, 0.078125, ((0, 32),))
    final_gain = jnp.clip(1.0 + 0.18 * jax.random.normal(key_of[13], (D,), jnp.float32), 0.099609375, 1.8984375).astype(jnp.bfloat16)
    segment_ids = draw_segment_ids(jax.random.fold_in(key_of[17], 71), 0)
    positions = draw_positions(jax.random.fold_in(key_of[17], 71), 0)
    cotangent = normal_values(key_of[16], (TOKENS, D), 1.0, 6.0, ((0, 32),))
    return dict(tokens=tokens, attention_gain=attention_gain, query_weight=query_weight, key_weight=key_weight, value_weight=value_weight, query_gain=query_gain, key_gain=key_gain, output_weight=output_weight, mixed_gain=mixed_gain, feed_gain=feed_gain, gate_weight=gate_weight, up_weight=up_weight, down_weight=down_weight, final_gain=final_gain, segment_ids=segment_ids, positions=positions, cotangent=cotangent)


EPSILON = 1e-06
THETA = 1000000.0
HIGH = lax.Precision.HIGHEST

@jax.custom_vjp
def low(v):
    return lax.optimization_barrier(v.astype(jnp.bfloat16)).astype(jnp.float32)

@jax.custom_vjp
def low_back(v):
    return v

def low_keep(v):
    return (low(v), None)

def low_pass(kept, grad):
    return (grad,)

def back_keep(v):
    return (v, None)

def back_low(kept, grad):
    return (low(grad),)
low.defvjp(low_keep, low_pass)
low_back.defvjp(back_keep, back_low)

def rms_scale(values, gain):
    return values * lax.rsqrt(lax.optimization_barrier(jnp.mean(values * values, axis=-1, keepdims=True)) + EPSILON) * gain

def angles_of(position_ids):
    half_width = HD // 2
    inverse = THETA ** (-(jnp.arange(half_width, dtype=jnp.float32) * 2.0) / HD)
    angle = position_ids.astype(jnp.float32)[:, None] * inverse[None, :]
    return (jnp.cos(angle), jnp.sin(angle))

def rotate(values, cosine, sine):
    half_width = values.shape[-1] // 2
    first_half = values[..., :half_width]
    second_half = values[..., half_width:]
    return jnp.concatenate([first_half * cosine - second_half * sine, second_half * cosine + first_half * sine], axis=-1)

def product(left, right):
    return jnp.dot(left, right, precision=HIGH)

def group_forward(rows_in, attention_gain, query_weight, key_weight, value_weight, query_gain, key_gain, output_weight, mixed_gain, feed_gain, gate_weight, up_weight, down_weight, final_gain, segment_ids, position_ids):
    count = rows_in.shape[0]
    normed = low(rms_scale(rows_in, attention_gain))
    query_raw = low_back(product(normed, query_weight))
    key_raw = low_back(product(normed, key_weight))
    value_rows = low(low_back(product(normed, value_weight)))
    cosine, sine = angles_of(position_ids)
    query_heads = rms_scale(query_raw.reshape(count, HQ, HD), query_gain)
    query_rows = low(rotate(query_heads, cosine[:, None, :], sine[:, None, :]))
    key_rows = low(rotate(rms_scale(key_raw, key_gain), cosine, sine))
    width = 512 if count % 512 == 0 else count
    blocks = count // width

    def attend(pieces):
        query_block, query_pos, query_seg = pieces
        scores = jnp.einsum('thd,kd->htk', query_block, key_rows, precision=HIGH)
        scores = low_back(scores) * HD ** (-0.5)
        allowed = (position_ids[None, :] <= query_pos[:, None]) & ((segment_ids[None, :] == 0) | (segment_ids[None, :] == query_seg[:, None]))
        scores = jnp.where(allowed[None], scores, -1e+30)
        probs = jax.nn.softmax(scores, axis=-1)
        return jnp.einsum('htk,kd->thd', low(probs), value_rows, precision=HIGH)
    attended = lax.map(jax.checkpoint(attend), (query_rows.reshape(blocks, width, HQ, HD), position_ids.reshape(blocks, width), segment_ids.reshape(blocks, width)))
    attended = low(low_back(attended.reshape(count, HQ * HD)))
    projected = low_back(product(attended, output_weight))
    mixed = rows_in + rms_scale(projected, mixed_gain)
    normed_two = low(rms_scale(mixed, feed_gain))
    gate_pre = low_back(product(normed_two, gate_weight))
    up_pre = low_back(product(normed_two, up_weight))
    hidden = low(jax.nn.gelu(gate_pre, approximate=True) * up_pre)
    branch = low_back(product(hidden, down_weight))
    return mixed + rms_scale(branch, final_gain)

def reference(tokens, attention_gain, query_weight, key_weight, value_weight, query_gain, key_gain, output_weight, mixed_gain, feed_gain, gate_weight, up_weight, down_weight, final_gain, segment_ids, positions, cotangent):
    params = tuple((weight.astype(jnp.float32) for weight in (attention_gain, query_weight, key_weight, value_weight, query_gain, key_gain, output_weight, mixed_gain, feed_gain, gate_weight, up_weight, down_weight, final_gain)))
    outputs = []
    input_grads = []
    totals = None
    for group_index in range(N_DP):
        first = group_index * GROUP
        rows_in = tokens[first:first + GROUP].astype(jnp.float32)
        group_segments = segment_ids[first:first + GROUP]
        group_positions = positions[first:first + GROUP]

        def forward(rows_arg, *weights):
            return group_forward(rows_arg, *weights, group_segments, group_positions)
        result, pullback = jax.vjp(forward, rows_in, *params)
        grads = pullback(cotangent[first:first + GROUP].astype(jnp.float32))
        outputs.append(result.astype(jnp.bfloat16))
        input_grads.append(grads[0].astype(jnp.bfloat16))
        totals = grads[1:] if totals is None else tuple((left + right for left, right in zip(totals, grads[1:])))
    layer_out = jnp.concatenate(outputs, axis=0)
    tokens_grad = jnp.concatenate(input_grads, axis=0)
    return (layer_out, tokens_grad, totals[0], totals[1], totals[2], totals[3], totals[4], totals[5], totals[6], totals[7], totals[8], totals[9], totals[10], totals[11], totals[12])
```

```python
import jax
import jax.numpy as jnp
import numpy as np
from jax import lax
from jax.experimental import pallas as pl
from jax.experimental.pallas import tpu as pltpu
from jax.sharding import Mesh, PartitionSpec as P

FF = 6912
HQ = 4
HD = 256
EPSILON = 1e-06
THETA = 1000000.0
BF = jnp.bfloat16
F32 = jnp.float32

AXES = ("x", "core", "w", "z", "y")
CTX_GRID = {8: (1, 4, 2), 32: (2, 4, 4)}


def grid_of(mesh):
    dp, ctx = mesh.shape["dp"], mesh.shape["ctx"]
    w, z, y = CTX_GRID.get(ctx, (1, ctx, 1))
    return (dp // 2, 2, w, z, y)


class Place:
    def __init__(self, sizes):
        self.size = dict(zip(AXES, sizes))
        self.at = {a: lax.axis_index(a) for a in AXES}

    def shift(self, value, axis, by):
        n = self.size[axis]
        return lax.ppermute(value, axis, [(i, (i + by) % n) for i in range(n)])

    def shift_wz(self, value, kw, kz):
        nw, nz = self.size["w"], self.size["z"]
        pairs = [
            (w * nz + z, ((w + kw) % nw) * nz + (z + kz) % nz) for w in range(nw) for z in range(nz)
        ]
        return lax.ppermute(value, ("w", "z"), pairs)

    def swap_core(self, value):
        return lax.ppermute(value, "core", [(0, 1), (1, 0)])

    def wz_steps(self):
        return [(kw, kz) for kw in range(self.size["w"]) for kz in range(self.size["z"])]

    def chip(self, spot):
        size = self.size
        return ((spot["x"] * size["w"] + spot["w"]) * size["z"] + spot["z"]) * size["y"] + spot["y"]

    def ctx_chip(self, spot):
        return (spot["w"] * self.size["z"] + spot["z"]) * self.size["y"] + spot["y"]

    def gather(self, own, orders, after=None):
        size, at = self.size, self.at
        rows = own.shape[0]
        chips = size["x"] * size["w"] * size["z"] * size["y"]
        full = jnp.zeros((chips * rows, own.shape[1]), own.dtype)
        came = []
        if after is not None:
            own, _ = lax.optimization_barrier((own, after))
        for number, (kw, kz) in enumerate(self.wz_steps()):
            block = own if kw == kz == 0 else self.shift_wz(own, kw, kz)
            if kw or kz:
                came.append(block)
            spot = {"w": (at["w"] - kw) % size["w"], "z": (at["z"] - kz) % size["z"]}
            first, second = orders[number % len(orders)]
            for ka in range(size[first]):
                block_a = block if ka == 0 else self.shift(block, first, ka)
                spot[first] = (at[first] - ka) % size[first]
                for kb in range(size[second]):
                    block_b = block_a if kb == 0 else self.shift(block_a, second, kb)
                    spot[second] = (at[second] - kb) % size[second]
                    full = lax.dynamic_update_slice(full, block_b, (self.chip(spot) * rows, 0))
        return full, came

    def gather_group(self, own):
        size, at = self.size, self.at
        rows = own.shape[0]
        full = jnp.zeros((size["w"] * size["z"] * size["y"] * rows, own.shape[1]), own.dtype)
        for kw, kz in self.wz_steps():
            block = own if kw == kz == 0 else self.shift_wz(own, kw, kz)
            spot = {"w": (at["w"] - kw) % size["w"], "z": (at["z"] - kz) % size["z"]}
            for ky in range(size["y"]):
                block_y = block if ky == 0 else self.shift(block, "y", ky)
                spot["y"] = (at["y"] - ky) % size["y"]
                full = lax.dynamic_update_slice(full, block_y, (self.ctx_chip(spot) * rows, 0))
        return full

    def scatter(self, full, orders):
        size, at = self.size, self.at
        lead = ("x", "w", "z", "y") if "x" in orders[0] else ("w", "z", "y")
        grid = tuple(size[a] for a in lead)
        full = full.reshape(grid + (-1, full.shape[-1]))
        total = None
        for number, (kw, kz) in reversed(list(enumerate(self.wz_steps()))):
            spot = {"w": (at["w"] + kw) % size["w"], "z": (at["z"] + kz) % size["z"]}
            names = [a for a in lead if a not in spot]
            part = lax.dynamic_slice(
                full,
                tuple(spot.get(a, 0) for a in lead) + (0, 0),
                tuple(1 if a in spot else size[a] for a in lead) + full.shape[-2:],
            ).reshape(tuple(size[a] for a in names) + full.shape[-2:])
            for axis in reversed(orders[number % len(orders)]):
                dim, n = names.index(axis), size[axis]
                names.remove(axis)

                def take(k):
                    return lax.dynamic_index_in_dim(part, (at[axis] + k) % n, dim, keepdims=False)

                acc = take(0).astype(F32)
                for k in range(1, n):
                    acc = acc + self.shift(take(k), axis, k).astype(F32)
                if names:
                    part = acc.astype(BF)
            if kw or kz:
                acc = self.shift_wz(acc.astype(BF), kw, kz).astype(F32)
            total = acc if total is None else total + acc
        return total


def rms_factor(values):
    return lax.rsqrt(jnp.mean(values * values, axis=-1, keepdims=True) + EPSILON)


def norm_back(incoming, values, factor, gain):
    scaled = incoming * gain
    gain_term = jnp.sum((incoming * values * factor).reshape(-1, values.shape[-1]), axis=0)
    inner = jnp.mean(scaled * values, axis=-1, keepdims=True)
    return (factor * scaled - values * (factor * factor * factor) * inner, gain_term)


def angles_of(position_ids):
    half_width = HD // 2
    inverse = THETA ** (-(jnp.arange(half_width, dtype=F32) * 2.0) / HD)
    angle = position_ids.astype(F32)[:, None] * inverse[None, :]
    return (jnp.cos(angle), jnp.sin(angle))


def rotate(values, cosine, sine):
    half_width = values.shape[-1] // 2
    first_half = values[..., :half_width]
    second_half = values[..., half_width:]
    return jnp.concatenate(
        [first_half * cosine - second_half * sine, second_half * cosine + first_half * sine],
        axis=-1,
    )


def matmul(left, right):
    return jnp.dot(left, right, preferred_element_type=F32)


def matmul_nt(left, right):
    return jnp.einsum("ij,kj->ik", left, right, preferred_element_type=F32)


def matmul_tn(left, right):
    return jnp.einsum("ji,jk->ik", left, right, preferred_element_type=F32)


def allowed_pairs(key_pos, key_seg, query_pos, query_seg):
    return (key_pos <= query_pos) & ((key_seg == 0) | (key_seg == query_seg))


def forward_kernel(
    live, q_ref, kv_ref, key_pos, key_seg, query_pos, query_seg, out_ref, log_ref, acc, total
):
    block = pl.program_id(0)
    local = q_ref.shape[0]

    @pl.when(block == 0)
    def _():
        acc[...] = jnp.zeros_like(acc)
        total[...] = jnp.zeros_like(total)

    @pl.when(live[block] != 0)
    def _():
        keys = kv_ref[:, :HD]
        values_t = kv_ref[:, HD:].T
        allowed = allowed_pairs(key_pos[...], key_seg[...], query_pos[...], query_seg[...])
        for head in range(HQ):
            mine = pl.ds(head * local, local)
            scores = matmul_nt(keys, q_ref[:, head * HD : (head + 1) * HD]) * HD ** (-0.5)
            weights = jnp.where(allowed, jnp.exp(scores), 0.0)
            total[:, mine] += jnp.sum(weights, axis=0, keepdims=True)
            acc[:, mine] += matmul(values_t, weights.astype(BF))

    @pl.when(block == pl.num_programs(0) - 1)
    def _():
        for head in range(HQ):
            mine = pl.ds(head * local, local)
            out_ref[:, head * HD : (head + 1) * HD] = (acc[:, mine] / total[:, mine]).T.astype(BF)
        log_ref[...] = jnp.log(total[...])


def backward_kernel(
    live,
    q_ref,
    grad_ref,
    log_ref,
    delta_ref,
    kv_ref,
    key_pos,
    key_seg,
    query_pos,
    query_seg,
    q_grad_ref,
    kv_grad_ref,
    acc,
):
    block = pl.program_id(0)
    local = q_ref.shape[0]

    @pl.when(block == 0)
    def _():
        acc[...] = jnp.zeros_like(acc)

    @pl.when(live[block] == 0)
    def _():
        kv_grad_ref[...] = jnp.zeros_like(kv_grad_ref)

    @pl.when(live[block] != 0)
    def _():
        keys = kv_ref[:, :HD]
        keys_t = keys.T
        values = kv_ref[:, HD:]
        allowed = allowed_pairs(key_pos[...], key_seg[...], query_pos[...], query_seg[...])
        key_grad = jnp.zeros(keys.shape, F32)
        value_grad = jnp.zeros(keys.shape, F32)
        for head in range(HQ):
            mine = pl.ds(head * local, local)
            queries = q_ref[:, head * HD : (head + 1) * HD]
            grads = grad_ref[:, head * HD : (head + 1) * HD]
            scores = matmul_nt(keys, queries) * HD ** (-0.5)
            probs = jnp.where(allowed, jnp.exp(scores - log_ref[:, mine]), 0.0)
            prob_grad = matmul_nt(values, grads)
            score_grad = (probs * (prob_grad - delta_ref[:, mine]) * HD ** (-0.5)).astype(BF)
            value_grad += matmul(probs.astype(BF), grads)
            key_grad += matmul(score_grad, queries)
            acc[:, mine] += matmul(keys_t, score_grad)
        kv_grad_ref[:, :HD] = key_grad.astype(BF)
        kv_grad_ref[:, HD:] = value_grad.astype(BF)

    @pl.when(block == pl.num_programs(0) - 1)
    def _():
        for head in range(HQ):
            mine = pl.ds(head * local, local)
            q_grad_ref[:, head * HD : (head + 1) * HD] = acc[:, mine].T


class Attention:
    def __init__(self, positions, segment_ids, query_pos, query_seg):
        local = query_pos.shape[0]
        self.local = local
        self.blocks = positions.shape[0] // local
        pos = positions.reshape(self.blocks, local)
        seg = segment_ids.reshape(self.blocks, local)
        seg_low, seg_high = jnp.min(seg, axis=1), jnp.max(seg, axis=1)
        late = jnp.min(pos, axis=1) > jnp.max(query_pos)
        foreign = (seg_low > 0) & (
            (seg_low > jnp.max(query_seg)) | (seg_high < jnp.min(query_seg))
        )
        self.live = jnp.where(late | foreign, 0, 1).astype(jnp.int32)
        self.marks = (
            positions.reshape(-1, 1),
            segment_ids.reshape(-1, 1),
            query_pos.reshape(1, -1),
            query_seg.reshape(1, -1),
        )

    def specs(self):
        local = self.local
        whole = lambda *shape: pl.BlockSpec(shape, lambda j, live: (0,) * len(shape))
        rows = lambda width: pl.BlockSpec((local, width), lambda j, live: (j, 0))
        marks = [rows(1), rows(1), whole(1, local), whole(1, local)]
        return whole, rows, marks

    def forward(self, queries, key_values):
        local, wide = queries.shape
        whole, rows, marks = self.specs()
        return pl.pallas_call(
            forward_kernel,
            out_shape=(
                jax.ShapeDtypeStruct((local, wide), BF),
                jax.ShapeDtypeStruct((1, HQ * local), F32),
            ),
            grid_spec=pltpu.PrefetchScalarGridSpec(
                num_scalar_prefetch=1,
                grid=(self.blocks,),
                in_specs=[whole(local, wide), rows(2 * HD)] + marks,
                out_specs=(whole(local, wide), whole(1, HQ * local)),
                scratch_shapes=[
                    pltpu.VMEM((HD, HQ * local), F32),
                    pltpu.VMEM((1, HQ * local), F32),
                ],
            ),
            cost_estimate=pl.CostEstimate(
                flops=20 * 4 * local * local * HD, bytes_accessed=8 << 20, transcendentals=0
            ),
        )(self.live, queries, key_values, *self.marks)

    def backward(self, queries, grads, logs, delta, key_values):
        local, wide = queries.shape
        whole, rows, marks = self.specs()
        return pl.pallas_call(
            backward_kernel,
            out_shape=(
                jax.ShapeDtypeStruct((local, wide), F32),
                jax.ShapeDtypeStruct(key_values.shape, BF),
            ),
            grid_spec=pltpu.PrefetchScalarGridSpec(
                num_scalar_prefetch=1,
                grid=(self.blocks,),
                in_specs=[
                    whole(local, wide),
                    whole(local, wide),
                    whole(1, HQ * local),
                    whole(1, HQ * local),
                    rows(2 * HD),
                ]
                + marks,
                out_specs=(whole(local, wide), rows(2 * HD)),
                scratch_shapes=[pltpu.VMEM((HD, HQ * local), F32)],
            ),
            cost_estimate=pl.CostEstimate(
                flops=20 * 10 * local * local * HD, bytes_accessed=16 << 20, transcendentals=0
            ),
        )(self.live, queries, grads, logs, delta, key_values, *self.marks)


def body(
    sizes,
    tokens,
    attention_gain,
    query_weight,
    key_weight,
    value_weight,
    query_gain,
    key_gain,
    output_weight,
    mixed_gain,
    feed_gain,
    gate_weight,
    up_weight,
    down_weight,
    final_gain,
    segment_ids,
    positions,
    cotangent,
):
    place = Place(sizes)
    nx, _, nw, nz, ny = sizes
    chips = nx * nw * nz * ny
    core = place.at["core"]
    local, model = tokens.shape
    rows = query_weight.shape[0]
    wide = HQ * HD
    half = FF // 2
    stretch = half // nx
    offset = place.ctx_chip(place.at) * local
    query_pos = lax.dynamic_slice_in_dim(positions, offset, local)
    query_seg = lax.dynamic_slice_in_dim(segment_ids, offset, local)
    both_ways = (("x", "y"), ("y", "x"))

    def pick(pair, which):
        return lax.dynamic_index_in_dim(pair, which, 0, keepdims=False)

    def cores_in_order(own, other):
        return jnp.where(core == 0, jnp.stack([own, other]), jnp.stack([other, own]))

    inside = np.arange(model).reshape(nx, 2, nw, nz, ny, rows).transpose(0, 2, 3, 4, 1, 5).reshape(-1)
    order = jnp.asarray(inside, jnp.int32)
    counting = lax.iota(jnp.int32, model)
    to_inside = (counting[:, None] == order[None, :]).astype(BF)
    to_outside = (order[:, None] == counting[None, :]).astype(BF)

    def reorder(values, matrix):
        if values.dtype == F32:
            return jnp.dot(values, matrix.astype(F32), precision=lax.Precision.HIGHEST)
        return matmul(values, matrix).astype(BF)

    def column_halves(query, key, value):
        cut = lambda m: m.reshape(m.shape[0], 2, -1)
        halves = jnp.concatenate([cut(query), cut(key), cut(value)], axis=2)
        return jnp.moveaxis(halves, 1, 0)

    head_width = wide // 2 + HD
    gains = jnp.concatenate(
        [attention_gain, mixed_gain, feed_gain, final_gain, query_gain, key_gain]
    )
    gain_count = gains.size
    projections = column_halves(query_weight, key_weight, value_weight)
    gain_rows = -(-gain_count // head_width) * 8
    gain_block = jnp.zeros((gain_rows * head_width,), BF).at[:gain_count].set(gains)
    small = jnp.concatenate(
        [gain_block.reshape(gain_rows, head_width), reorder(output_weight, to_inside).reshape(-1, head_width)]
    )
    first_own = jnp.concatenate(
        [
            cores_in_order(pick(projections, core), place.swap_core(pick(projections, 1 - core))).reshape(
                2 * rows, head_width
            ),
            small,
        ]
    )
    first_all, first_came = place.gather(first_own, both_ways)
    first_all = cores_in_order(first_all, place.swap_core(first_all)).reshape(
        2, chips, first_own.shape[0], head_width
    )
    projection_full = first_all[:, :, : 2 * rows].reshape(2, model, head_width)
    projection_full = jnp.concatenate([projection_full[0], projection_full[1]], axis=1)
    gains_all = first_all[:, :, 2 * rows].reshape(2, chips, head_width)[:, :, :gain_count]
    gains_all = jnp.moveaxis(gains_all.astype(F32), 0, 1)
    spans = np.cumsum([0, rows, rows, rows, rows, query_gain.size, key_gain.size])
    gain_one, mixed_scale, feed_scale, final_scale, query_scale, key_scale = (
        gains_all[:, :, a:b] for a, b in zip(spans[:-1], spans[1:])
    )
    gain_one, mixed_scale, feed_scale, final_scale = (
        g.reshape(model) for g in (gain_one, mixed_scale, feed_scale, final_scale)
    )

    def true_order(values):
        values = values.reshape(nx, nw, nz, ny, 2, -1)
        return jnp.transpose(values, (0, 4, 1, 2, 3, 5)).reshape(-1)

    query_scale, key_scale = true_order(query_scale), true_order(key_scale)
    output_full = first_all[:, :, 2 * rows + gain_rows :].reshape(2, nx, nw * nz * ny, -1, model)
    output_full = jnp.moveaxis(output_full, 0, 1).reshape(wide, model)

    gate_up = jnp.stack([gate_weight, up_weight], axis=1).reshape(rows, 2, nx, 2, stretch)

    def half_of(which):
        piece = lax.dynamic_index_in_dim(gate_up, which, 3, keepdims=False)
        return piece.reshape(rows, FF)

    gate_up_own = cores_in_order(half_of(core), place.swap_core(half_of(1 - core)))
    gate_up_full, gate_up_came = place.gather(
        gate_up_own.reshape(2 * rows, FF), both_ways, first_came
    )
    down_full, _ = place.gather(reorder(down_weight, to_inside), both_ways, gate_up_came)

    tokens_in = reorder(tokens, to_inside).astype(F32)
    out_grad = reorder(cotangent, to_inside).astype(F32)
    factor_one = rms_factor(tokens_in)
    normed = (tokens_in * factor_one * gain_one).astype(BF)
    raw = matmul(normed, projection_full)
    heads_half = wide // 2

    def both_halves(at, width):
        return [raw[:, at : at + width], raw[:, head_width + at : head_width + at + width]]

    query_raw = [
        piece[:, h * HD : (h + 1) * HD]
        for piece in both_halves(0, heads_half)
        for h in range(HQ // 2)
    ]
    key_raw = jnp.concatenate(both_halves(heads_half, HD // 2), axis=1)
    value_rows = jnp.concatenate(both_halves(heads_half + HD // 2, HD // 2), axis=1).astype(BF)
    cosine, sine = angles_of(query_pos)
    key_factor = rms_factor(key_raw)
    key_rows = rotate(key_raw * key_factor * key_scale, cosine, sine).astype(BF)
    key_values = place.gather_group(jnp.concatenate([key_rows, value_rows], axis=1))
    query_factor = [rms_factor(q) for q in query_raw]
    queries = jnp.concatenate(
        [
            rotate(q * f * query_scale, cosine, sine).astype(BF)
            for q, f in zip(query_raw, query_factor)
        ],
        axis=1,
    )
    attention = Attention(positions, segment_ids, query_pos, query_seg)
    attended, logs = attention.forward(queries, key_values)
    projected = matmul(attended, output_full)
    factor_three = rms_factor(projected)
    mixed = tokens_in + projected * factor_three * mixed_scale
    factor_two = rms_factor(mixed)
    normed_two = (mixed * factor_two * feed_scale).astype(BF)
    normed_both = jnp.concatenate([normed_two, place.swap_core(normed_two)])
    pre = matmul(normed_both, gate_up_full)
    gate_pre, up_pre = pre[:, :half], pre[:, half:]
    hidden = (jax.nn.gelu(gate_pre, approximate=True) * up_pre).astype(BF)
    branch_both = matmul(hidden, down_full)
    branch = branch_both[:local] + place.swap_core(branch_both[local:])
    factor_four = rms_factor(branch)
    layer_out = reorder((mixed + branch * factor_four * final_scale).astype(BF), to_outside)

    branch_grad, final_term = norm_back(out_grad, branch, factor_four, final_scale)
    branch_grad = branch_grad.astype(BF)
    branch_grad_both = jnp.concatenate([branch_grad, place.swap_core(branch_grad)])
    down_terms = matmul_tn(hidden, branch_grad_both).astype(BF)
    down_weight_grad = reorder(place.scatter(down_terms, both_ways), to_outside)
    hidden_grad = matmul_nt(branch_grad_both, down_full)
    _, geglu_back = jax.vjp(
        lambda gate_in, up_in: jax.nn.gelu(gate_in, approximate=True) * up_in, gate_pre, up_pre
    )
    gate_grad, up_grad = geglu_back(hidden_grad)
    gate_up_grad = jnp.concatenate([gate_grad.astype(BF), up_grad.astype(BF)], axis=1)
    gate_up_terms = matmul_tn(normed_both, gate_up_grad).astype(BF)
    gate_up_rows = place.scatter(gate_up_terms, both_ways).reshape(2, rows, FF)
    both = cores_in_order(pick(gate_up_rows, core), place.swap_core(pick(gate_up_rows, 1 - core)))
    both = both.reshape(2, rows, 2, nx, stretch)
    both = jnp.transpose(both, (2, 1, 3, 0, 4)).reshape(2, rows, FF)
    gate_weight_grad, up_weight_grad = both[0], both[1]

    normed_two_both = matmul_nt(gate_up_grad, gate_up_full)
    normed_two_grad = normed_two_both[:local] + place.swap_core(normed_two_both[local:])
    mixed_part, feed_term = norm_back(normed_two_grad, mixed, factor_two, feed_scale)
    mixed_grad = out_grad + mixed_part
    projected_grad, mixed_term = norm_back(mixed_grad, projected, factor_three, mixed_scale)
    projected_grad = projected_grad.astype(BF)
    output_terms = matmul_tn(attended, projected_grad).astype(BF)
    attended_grad = matmul_nt(projected_grad, output_full).astype(BF)
    delta = jnp.stack(
        [
            jnp.sum(
                attended_grad[:, h * HD : (h + 1) * HD].astype(F32)
                * attended[:, h * HD : (h + 1) * HD].astype(F32),
                axis=1,
            )
            for h in range(HQ)
        ]
    ).reshape(1, -1)
    queries_grad, key_value_terms = attention.backward(
        queries, attended_grad, logs, delta, key_values
    )
    key_value_grad = place.scatter(key_value_terms, (("y",),))
    key_grad_rows = key_value_grad[:, :HD]
    values_grad = key_value_grad[:, HD:].astype(BF)
    key_back = rotate(key_grad_rows, cosine, -sine)
    key_in_grad, key_term = norm_back(key_back, key_raw, key_factor, key_scale)
    key_in_grad = key_in_grad.astype(BF)
    query_in_grad, query_term = [], 0.0
    for h in range(HQ):
        query_back = rotate(queries_grad[:, h * HD : (h + 1) * HD], cosine, -sine)
        grad, term = norm_back(query_back, query_raw[h], query_factor[h], query_scale)
        query_in_grad.append(grad.astype(BF))
        query_term = query_term + term
    quarter = HD // 2
    raw_grad = []
    for c in range(2):
        raw_grad.append(
            jnp.concatenate(
                query_in_grad[c * HQ // 2 : (c + 1) * HQ // 2]
                + [
                    key_in_grad[:, c * quarter : (c + 1) * quarter],
                    values_grad[:, c * quarter : (c + 1) * quarter],
                ],
                axis=1,
            )
        )
    normed_grad = matmul_nt(jnp.concatenate(raw_grad, axis=1), projection_full)
    tokens_part, gain_one_term = norm_back(normed_grad, tokens_in, factor_one, gain_one)
    tokens_grad = reorder((mixed_grad + tokens_part).astype(BF), to_outside)

    def chip_order(values):
        values = values.reshape(nx, 2, nw, nz, ny, -1)
        return jnp.transpose(values, (0, 2, 3, 4, 1, 5)).reshape(chips, 2, -1)

    gain_terms = jnp.concatenate(
        [t.reshape(chips, 2, -1) for t in (gain_one_term, mixed_term, feed_term, final_term)]
        + [chip_order(query_term), chip_order(key_term)],
        axis=2,
    )
    gain_terms = jnp.moveaxis(gain_terms, 1, 0).astype(BF)
    gain_terms = jnp.pad(
        gain_terms, ((0, 0), (0, 0), (0, gain_rows * head_width - gain_count))
    ).reshape(2, chips, gain_rows, head_width)
    output_terms = output_terms.reshape(nx, 2, nw * nz * ny, -1, model)
    output_terms = jnp.moveaxis(output_terms, 1, 0).reshape(2, chips, -1, head_width)
    grads_pair = jnp.stack(raw_grad)

    def terms_of(which):
        return jnp.concatenate(
            [
                matmul_tn(normed, pick(grads_pair, which)).astype(BF).reshape(chips, 2 * rows, head_width),
                pick(gain_terms, which),
                pick(output_terms, which),
            ],
            axis=1,
        ).reshape(-1, head_width)

    first_terms = terms_of(core).astype(F32) + place.swap_core(terms_of(1 - core)).astype(F32)
    first_grad = place.scatter(first_terms.astype(BF), both_ways)
    projection_rows = first_grad[: 2 * rows].reshape(2, rows, head_width)
    projection_rows = cores_in_order(
        pick(projection_rows, core), place.swap_core(pick(projection_rows, 1 - core))
    )

    def whole_columns(a, b):
        return jnp.moveaxis(projection_rows[:, :, a:b], 0, 1).reshape(rows, -1)

    query_weight_grad = whole_columns(0, heads_half)
    key_weight_grad = whole_columns(heads_half, heads_half + quarter)
    value_weight_grad = whole_columns(heads_half + quarter, head_width)
    gain_grad = first_grad[2 * rows : 2 * rows + gain_rows].reshape(-1)
    (
        attention_gain_grad,
        mixed_gain_grad,
        feed_gain_grad,
        final_gain_grad,
        query_gain_grad,
        key_gain_grad,
    ) = (gain_grad[a:b] for a, b in zip(spans[:-1], spans[1:]))
    output_weight_grad = reorder(first_grad[2 * rows + gain_rows :].reshape(-1, model), to_outside)
    return (
        layer_out,
        tokens_grad,
        attention_gain_grad,
        query_weight_grad,
        key_weight_grad,
        value_weight_grad,
        query_gain_grad,
        key_gain_grad,
        output_weight_grad,
        mixed_gain_grad,
        feed_gain_grad,
        gate_weight_grad,
        up_weight_grad,
        down_weight_grad,
        final_gain_grad,
    )


def solution(mesh):
    sizes = grid_of(mesh)
    grid = Mesh(mesh.devices.reshape(sizes), AXES)
    matrix, vector, group = P(AXES, None), P(AXES), P(("x", "core"))
    return jax.shard_map(
        lambda *arrays: body(sizes, *arrays),
        mesh=grid,
        in_specs=(
            matrix,
            vector,
            matrix,
            matrix,
            matrix,
            vector,
            vector,
            matrix,
            vector,
            vector,
            matrix,
            matrix,
            matrix,
            vector,
            group,
            group,
            matrix,
        ),
        out_specs=(
            matrix,
            matrix,
            vector,
            matrix,
            matrix,
            matrix,
            vector,
            vector,
            matrix,
            vector,
            vector,
            matrix,
            matrix,
            matrix,
            vector,
        ),
        check_vma=False,
    )
```

```python
import jax
import jax.numpy as jnp
import numpy as np
from jax import lax
from jax.experimental import pallas as pl
from jax.experimental.pallas import tpu as pltpu
from jax.sharding import Mesh, PartitionSpec as P

FF = 6912
HQ = 4
HD = 256
EPSILON = 1e-06
THETA = 1000000.0
BF = jnp.bfloat16
F32 = jnp.float32

AXES = ("x", "core", "w", "z", "y")
CTX_GRID = {8: (1, 4, 2), 32: (2, 4, 4)}


def grid_of(mesh):
    dp, ctx = mesh.shape["dp"], mesh.shape["ctx"]
    w, z, y = CTX_GRID.get(ctx, (1, ctx, 1))
    return (dp // 2, 2, w, z, y)


class Place:
    def __init__(self, sizes):
        self.size = dict(zip(AXES, sizes))
        self.at = {a: lax.axis_index(a) for a in AXES}

    def shift(self, value, axis, by):
        n = self.size[axis]
        return lax.ppermute(value, axis, [(i, (i + by) % n) for i in range(n)])

    def shift_wz(self, value, kw, kz):
        nw, nz = self.size["w"], self.size["z"]
        pairs = [
            (w * nz + z, ((w + kw) % nw) * nz + (z + kz) % nz) for w in range(nw) for z in range(nz)
        ]
        return lax.ppermute(value, ("w", "z"), pairs)

    def swap_core(self, value):
        return lax.ppermute(value, "core", [(0, 1), (1, 0)])

    def wz_steps(self):
        return [(kw, kz) for kw in range(self.size["w"]) for kz in range(self.size["z"])]

    def gather_wz(self, own):
        return [own if kw == kz == 0 else self.shift_wz(own, kw, kz) for kw, kz in self.wz_steps()]

    def gather_line(self, own):
        return lax.all_gather(own, ("core", "w", "z"), axis=0, tiled=True)

    def cores_summed(self, full):
        full = full.reshape(2, -1, full.shape[-1])
        give = self.swap_core(lax.dynamic_index_in_dim(full, 1 - self.at["core"], 0, keepdims=False))
        keep = lax.dynamic_index_in_dim(full, self.at["core"], 0, keepdims=False)
        return (keep.astype(F32) + give.astype(F32)).astype(BF)

    def scatter_line(self, rows):
        return lax.psum_scatter(rows, ("w", "z"), scatter_dimension=0, tiled=True)

    def plane_steps(self):
        return [(dx, dy) for dx in range(self.size["x"]) for dy in range(self.size["y"])]

    def gather_near(self, own):
        blocks = {(0, 0): own}
        for dx in range(1, self.size["x"]):
            blocks[dx, 0] = self.shift(own, "x", dx)
        for dy in range(1, self.size["y"]):
            blocks[0, dy] = self.shift(own, "y", dy)
        return blocks

    def gather_far(self, near, *hold):
        blocks = {step: after(block, *hold) if hold else block for step, block in near.items()}
        cut = blocks[0, 0].shape[0] // 2
        for dx, dy in self.plane_steps():
            if dx and dy:
                top = self.shift(blocks[dx, 0][:cut], "y", dy)
                low = self.shift(blocks[0, dy][cut:], "x", dx)
                blocks[dx, dy] = jnp.concatenate([top, low])
        return [blocks[step] for step in self.plane_steps()]

    def scatter_plane(self, parts):
        parts = dict(zip(self.plane_steps(), parts))
        cut = parts[0, 0].shape[0] // 2
        tops = {d: parts[d, 0][:cut] for d in range(self.size["x"])}
        lows = {d: parts[0, d][cut:] for d in range(self.size["y"])}
        own_top, own_low = parts[0, 0][:cut], parts[0, 0][cut:]
        for dx in range(1, self.size["x"]):
            own_low = own_low + self.shift(parts[dx, 0][cut:].astype(BF), "x", -dx).astype(F32)
        for dy in range(1, self.size["y"]):
            own_top = own_top + self.shift(parts[0, dy][:cut].astype(BF), "y", -dy).astype(F32)
        for dx, dy in self.plane_steps():
            if dx and dy:
                part = parts[dx, dy].astype(BF)
                tops[dx] = tops[dx] + self.shift(part[:cut], "y", -dy).astype(F32)
                lows[dy] = lows[dy] + self.shift(part[cut:], "x", -dx).astype(F32)
        self.halfway = [tops[self.size["x"] - 1], lows[self.size["y"] - 1]]
        for dx in range(1, self.size["x"]):
            own_top = own_top + self.shift(tops[dx].astype(BF), "x", -dx).astype(F32)
        for dy in range(1, self.size["y"]):
            own_low = own_low + self.shift(lows[dy].astype(BF), "y", -dy).astype(F32)
        return jnp.concatenate([own_top, own_low])

    def deal_plane(self, pieces, hold=(), hold_end=()):
        for dim, axis in ((0, "x"), (1, "y")):
            n, here = self.size[axis], self.at[axis]
            dealt = []
            for d in range(n):
                piece = lax.dynamic_index_in_dim(pieces, (here + d) % n, dim)
                dealt.append(piece if d == 0 else self.shift(piece, axis, d))
            wait_for = hold if axis == "x" else hold_end
            if wait_for:
                dealt = [after(piece, *wait_for) for piece in dealt]
            if n == 2:
                own, other = dealt
                low = jnp.where(here == 0, own, other)
                pieces = jnp.concatenate([low, jnp.where(here == 0, other, own)], axis=dim)
            else:
                pieces = jnp.zeros_like(pieces)
                for d in range(n):
                    pieces = lax.dynamic_update_slice_in_dim(pieces, dealt[d], (here - d) % n, dim)
        return pieces

    def ctx_chip(self, spot):
        return (spot["w"] * self.size["z"] + spot["z"]) * self.size["y"] + spot["y"]

    def gather_chips(self, own):
        size, at = self.size, self.at
        rows, width = own.shape
        line = size["w"] * size["z"] * rows
        mine = jnp.zeros((line, width), own.dtype)
        for block, (kw, kz) in zip(self.gather_wz(own), self.wz_steps()):
            w, z = (at["w"] - kw) % size["w"], (at["z"] - kz) % size["z"]
            mine = lax.dynamic_update_slice(mine, block, ((w * size["z"] + z) * rows, 0))
        full = jnp.zeros((size["x"] * size["y"] * line, width), own.dtype)
        near = self.gather_near(mine)
        for block, (dx, dy) in zip(self.gather_far(near), self.plane_steps()):
            x, y = (at["x"] - dx) % size["x"], (at["y"] - dy) % size["y"]
            full = lax.dynamic_update_slice(full, block, ((x * size["y"] + y) * line, 0))
        return full, mine, list(near.values())

    def scatter_chips(self, full):
        size, at = self.size, self.at
        full = full.reshape((size["x"], size["y"], -1, full.shape[-1]))
        parts = [
            full[(at["x"] - dx) % size["x"], (at["y"] - dy) % size["y"]].astype(F32)
            for dx, dy in self.plane_steps()
        ]
        mine = self.scatter_plane(parts)
        mine = mine.reshape((size["w"], size["z"], -1, mine.shape[-1]))
        total = None
        for kw, kz in reversed(self.wz_steps()):
            part = mine[(at["w"] + kw) % size["w"], (at["z"] + kz) % size["z"]]
            if kw or kz:
                part = self.shift_wz(part.astype(BF), kw, kz).astype(F32)
            total = part if total is None else total + part
        return total

    def gather_group(self, own):
        size, at = self.size, self.at
        rows = own.shape[0]
        full = jnp.zeros((size["w"] * size["z"] * size["y"] * rows, own.shape[1]), own.dtype)
        for kw, kz in self.wz_steps():
            block = own if kw == kz == 0 else self.shift_wz(own, kw, kz)
            spot = {"w": (at["w"] - kw) % size["w"], "z": (at["z"] - kz) % size["z"]}
            for ky in range(size["y"]):
                block_y = block if ky == 0 else self.shift(block, "y", ky)
                came = block_y if kw == kz == 0 else came
                spot["y"] = (at["y"] - ky) % size["y"]
                full = lax.dynamic_update_slice(full, block_y, (self.ctx_chip(spot) * rows, 0))
        return full, came

    def scatter_group(self, full, meanwhile):
        size, at = self.size, self.at
        full = full.reshape((size["w"], size["z"], size["y"], -1, full.shape[-1]))
        steps = sorted(self.wz_steps(), key=lambda k: (k == (0, 0), abs(k[1] - size["z"] // 2)))
        total, came, gone = None, None, []
        for kw, kz in steps:
            part = full[(at["w"] + kw) % size["w"], (at["z"] + kz) % size["z"]]
            acc = part[at["y"]].astype(F32)
            for dy in range(1, size["y"]):
                other = self.shift(part[(at["y"] + dy) % size["y"]], "y", dy)
                if came is None:
                    came = other
                    done = meanwhile(came)
                acc = acc + after(other, *gone).astype(F32) if gone else acc + other.astype(F32)
            if kw or kz:
                acc = self.shift_wz(acc.astype(BF), kw, kz)
                gone = gone or [acc, done]
                acc = acc.astype(F32)
            total = acc if total is None else total + acc
        return total, came


def after(value, *others):
    return lax.optimization_barrier((value,) + others)[0]


def rms_factor(values):
    return lax.rsqrt(jnp.mean(values * values, axis=-1, keepdims=True) + EPSILON)


def norm_back(incoming, values, factor, gain):
    scaled = incoming * gain
    gain_term = jnp.sum((incoming * values * factor).reshape(-1, values.shape[-1]), axis=0)
    inner = jnp.mean(scaled * values, axis=-1, keepdims=True)
    return (factor * scaled - values * (factor * factor * factor) * inner, gain_term)


def angles_of(position_ids):
    half_width = HD // 2
    inverse = THETA ** (-(jnp.arange(half_width, dtype=F32) * 2.0) / HD)
    angle = position_ids.astype(F32)[:, None] * inverse[None, :]
    return (jnp.cos(angle), jnp.sin(angle))


def rotate(values, cosine, sine):
    half_width = values.shape[-1] // 2
    first_half = values[..., :half_width]
    second_half = values[..., half_width:]
    return jnp.concatenate(
        [first_half * cosine - second_half * sine, second_half * cosine + first_half * sine],
        axis=-1,
    )


def matmul(left, right):
    return jnp.dot(left, right, preferred_element_type=F32)


def matmul_nt(left, right):
    return jnp.einsum("ij,kj->ik", left, right, preferred_element_type=F32)


def matmul_tn(left, right):
    return jnp.einsum("ji,jk->ik", left, right, preferred_element_type=F32)


def allowed_pairs(key_pos, key_seg, query_pos, query_seg):
    return (key_pos <= query_pos) & ((key_seg == 0) | (key_seg == query_seg))


def forward_kernel(
    live, q_ref, kv_ref, key_pos, key_seg, query_pos, query_seg, out_ref, log_ref, acc, total
):
    block = pl.program_id(0)
    local = q_ref.shape[0]

    @pl.when(block == 0)
    def _():
        acc[...] = jnp.zeros_like(acc)
        total[...] = jnp.zeros_like(total)

    @pl.when(live[block] != 0)
    def _():
        keys = kv_ref[:, :HD]
        values_t = kv_ref[:, HD:].T
        allowed = allowed_pairs(key_pos[...], key_seg[...], query_pos[...], query_seg[...])
        for head in range(HQ):
            mine = pl.ds(head * local, local)
            scores = matmul_nt(keys, q_ref[:, head * HD : (head + 1) * HD]) * HD ** (-0.5)
            weights = jnp.where(allowed, jnp.exp(scores), 0.0)
            total[:, mine] += jnp.sum(weights, axis=0, keepdims=True)
            acc[:, mine] += matmul(values_t, weights.astype(BF))

    @pl.when(block == pl.num_programs(0) - 1)
    def _():
        for head in range(HQ):
            mine = pl.ds(head * local, local)
            out_ref[:, head * HD : (head + 1) * HD] = (acc[:, mine] / total[:, mine]).T.astype(BF)
        log_ref[...] = jnp.log(total[...])


def backward_kernel(
    live,
    q_ref,
    grad_ref,
    log_ref,
    delta_ref,
    kv_ref,
    key_pos,
    key_seg,
    query_pos,
    query_seg,
    q_grad_ref,
    kv_grad_ref,
    acc,
):
    block = pl.program_id(0)
    local = q_ref.shape[0]

    @pl.when(block == 0)
    def _():
        acc[...] = jnp.zeros_like(acc)

    @pl.when(live[block] == 0)
    def _():
        kv_grad_ref[...] = jnp.zeros_like(kv_grad_ref)

    @pl.when(live[block] != 0)
    def _():
        keys = kv_ref[:, :HD]
        keys_t = keys.T
        values = kv_ref[:, HD:]
        allowed = allowed_pairs(key_pos[...], key_seg[...], query_pos[...], query_seg[...])
        key_grad = jnp.zeros(keys.shape, F32)
        value_grad = jnp.zeros(keys.shape, F32)
        for head in range(HQ):
            mine = pl.ds(head * local, local)
            queries = q_ref[:, head * HD : (head + 1) * HD]
            grads = grad_ref[:, head * HD : (head + 1) * HD]
            scores = matmul_nt(keys, queries) * HD ** (-0.5)
            probs = jnp.where(allowed, jnp.exp(scores - log_ref[:, mine]), 0.0)
            prob_grad = matmul_nt(values, grads)
            score_grad = (probs * (prob_grad - delta_ref[:, mine]) * HD ** (-0.5)).astype(BF)
            value_grad += matmul(probs.astype(BF), grads)
            key_grad += matmul(score_grad, queries)
            acc[:, mine] += matmul(keys_t, score_grad)
        kv_grad_ref[:, :HD] = key_grad.astype(BF)
        kv_grad_ref[:, HD:] = value_grad.astype(BF)

    @pl.when(block == pl.num_programs(0) - 1)
    def _():
        for head in range(HQ):
            mine = pl.ds(head * local, local)
            q_grad_ref[:, head * HD : (head + 1) * HD] = acc[:, mine].T


class Attention:
    def __init__(self, positions, segment_ids, query_pos, query_seg):
        local = query_pos.shape[0]
        self.local = local
        self.blocks = positions.shape[0] // local
        pos = positions.reshape(self.blocks, local)
        seg = segment_ids.reshape(self.blocks, local)
        seg_low, seg_high = jnp.min(seg, axis=1), jnp.max(seg, axis=1)
        late = jnp.min(pos, axis=1) > jnp.max(query_pos)
        foreign = (seg_low > 0) & (
            (seg_low > jnp.max(query_seg)) | (seg_high < jnp.min(query_seg))
        )
        self.live = jnp.where(late | foreign, 0, 1).astype(jnp.int32)
        self.marks = (
            positions.reshape(-1, 1),
            segment_ids.reshape(-1, 1),
            query_pos.reshape(1, -1),
            query_seg.reshape(1, -1),
        )

    def specs(self):
        local = self.local
        whole = lambda *shape: pl.BlockSpec(shape, lambda j, live: (0,) * len(shape))
        rows = lambda width: pl.BlockSpec((local, width), lambda j, live: (j, 0))
        marks = [rows(1), rows(1), whole(1, local), whole(1, local)]
        return whole, rows, marks

    def forward(self, queries, key_values):
        local, wide = queries.shape
        whole, rows, marks = self.specs()
        return pl.pallas_call(
            forward_kernel,
            out_shape=(
                jax.ShapeDtypeStruct((local, wide), BF),
                jax.ShapeDtypeStruct((1, HQ * local), F32),
            ),
            grid_spec=pltpu.PrefetchScalarGridSpec(
                num_scalar_prefetch=1,
                grid=(self.blocks,),
                in_specs=[whole(local, wide), rows(2 * HD)] + marks,
                out_specs=(whole(local, wide), whole(1, HQ * local)),
                scratch_shapes=[
                    pltpu.VMEM((HD, HQ * local), F32),
                    pltpu.VMEM((1, HQ * local), F32),
                ],
            ),
            cost_estimate=pl.CostEstimate(
                flops=20 * 4 * local * local * HD, bytes_accessed=8 << 20, transcendentals=0
            ),
        )(self.live, queries, key_values, *self.marks)

    def backward(self, queries, grads, logs, delta, key_values):
        local, wide = queries.shape
        whole, rows, marks = self.specs()
        return pl.pallas_call(
            backward_kernel,
            out_shape=(
                jax.ShapeDtypeStruct((local, wide), F32),
                jax.ShapeDtypeStruct(key_values.shape, BF),
            ),
            grid_spec=pltpu.PrefetchScalarGridSpec(
                num_scalar_prefetch=1,
                grid=(self.blocks,),
                in_specs=[
                    whole(local, wide),
                    whole(local, wide),
                    whole(1, HQ * local),
                    whole(1, HQ * local),
                    rows(2 * HD),
                ]
                + marks,
                out_specs=(whole(local, wide), rows(2 * HD)),
                scratch_shapes=[pltpu.VMEM((HD, HQ * local), F32)],
            ),
            cost_estimate=pl.CostEstimate(
                flops=20 * 10 * local * local * HD, bytes_accessed=16 << 20, transcendentals=0
            ),
        )(self.live, queries, grads, logs, delta, key_values, *self.marks)


def body(
    sizes,
    tokens,
    attention_gain,
    query_weight,
    key_weight,
    value_weight,
    query_gain,
    key_gain,
    output_weight,
    mixed_gain,
    feed_gain,
    gate_weight,
    up_weight,
    down_weight,
    final_gain,
    segment_ids,
    positions,
    cotangent,
):
    place = Place(sizes)
    nx, _, nw, nz, ny = sizes
    chips = nx * nw * nz * ny
    core = place.at["core"]
    local, model = tokens.shape
    rows = query_weight.shape[0]
    wide = HQ * HD
    offset = place.ctx_chip(place.at) * local
    query_pos = lax.dynamic_slice_in_dim(positions, offset, local)
    query_seg = lax.dynamic_slice_in_dim(segment_ids, offset, local)

    def pick(pair, which):
        return lax.dynamic_index_in_dim(pair, which, 0, keepdims=False)

    def cores_in_order(own, other):
        return jnp.where(core == 0, jnp.stack([own, other]), jnp.stack([other, own]))

    outside = np.arange(model).reshape(nx, 2, nw, nz, ny, rows)
    inside = outside.transpose(1, 2, 3, 0, 4, 5).reshape(-1)
    first = outside.transpose(0, 4, 2, 3, 1, 5).reshape(-1)

    def order_change(source, target):
        at = jnp.asarray(np.argsort(source)[target], jnp.int32)
        return (lax.iota(jnp.int32, model)[:, None] == at[None, :]).astype(BF)

    outside = np.arange(model)
    to_inside = order_change(outside, inside)
    to_outside = order_change(inside, outside)
    to_first = order_change(outside, first)
    inside_from_first = order_change(inside, first)

    def reorder(values, matrix):
        if values.dtype == F32:
            return jnp.dot(values, matrix.astype(F32), precision=lax.Precision.HIGHEST)
        return matmul(values, matrix).astype(BF)

    def column_halves(query, key, value):
        cut = lambda m: m.reshape(m.shape[0], 2, -1)
        halves = jnp.concatenate([cut(query), cut(key), cut(value)], axis=2)
        return jnp.moveaxis(halves, 1, 0)

    head_width = wide // 2 + HD
    gains = jnp.concatenate(
        [mixed_gain, feed_gain, final_gain, query_gain, key_gain, attention_gain]
    )
    gain_count = gains.size
    projections = column_halves(query_weight, key_weight, value_weight)
    gain_rows = -(-gain_count // head_width) * 8
    gain_block = jnp.zeros((gain_rows * head_width,), BF).at[:gain_count].set(gains)
    small = jnp.concatenate(
        [gain_block.reshape(gain_rows, head_width), reorder(output_weight, to_inside).reshape(-1, head_width)]
    )
    first_own = jnp.concatenate(
        [
            cores_in_order(pick(projections, core), place.swap_core(pick(projections, 1 - core))).reshape(
                2 * rows, head_width
            ),
            small,
        ]
    )
    first_all, first_came, next_came = place.gather_chips(first_own)

    gate_weight, up_weight, down_weight, tokens, cotangent, _ = lax.optimization_barrier(
        (gate_weight, up_weight, down_weight, tokens, cotangent, first_own)
    )
    part = FF // (nx * ny)
    gate_up = jnp.stack([gate_weight, up_weight]).reshape(2, rows, nx, 2 * nw * nz, ny, -1)
    gate_up = jnp.transpose(gate_up, (2, 4, 0, 1, 3, 5)).reshape(nx, ny, 2, rows, part)
    down_own = reorder(down_weight, to_inside)
    gate_up = place.deal_plane(gate_up, [first_came], next_came)
    gate_own, up_own = (gate_up[:, :, i].reshape(-1, part) for i in range(2))
    gate_full = place.gather_line(gate_own)
    first_other = place.swap_core(first_all)

    def in_order(own, other):
        return jnp.where(core == 0, own, other), jnp.where(core == 0, other, own)

    first_all, first_other = (
        block.reshape(chips, first_own.shape[0], head_width) for block in (first_all, first_other)
    )
    projections = tuple(
        block[:, : 2 * rows].reshape(model, head_width) for block in (first_all, first_other)
    )
    gains_all = jnp.stack(
        in_order(*(block[:, 2 * rows, :gain_count] for block in (first_all, first_other)))
    )
    gains_all = jnp.moveaxis(gains_all.astype(F32), 0, 1)
    spans = np.cumsum([0, rows, rows, rows, query_gain.size, key_gain.size, rows])
    mixed_scale, feed_scale, final_scale, query_scale, key_scale, gain_one = (
        gains_all[:, :, a:b] for a, b in zip(spans[:-1], spans[1:])
    )
    gain_first = gain_one.reshape(model)

    def inside_order(values):
        values = values.reshape(nx, ny, nw, nz, 2, rows)
        return jnp.transpose(values, (4, 2, 3, 0, 1, 5)).reshape(-1)

    gain_one, mixed_scale, feed_scale, final_scale = (
        inside_order(g) for g in (gain_one, mixed_scale, feed_scale, final_scale)
    )

    def true_order(values):
        values = values.reshape(nx, ny, nw, nz, 2, -1)
        return jnp.transpose(values, (0, 4, 2, 3, 1, 5)).reshape(-1)

    query_scale, key_scale = true_order(query_scale), true_order(key_scale)

    tokens_in = reorder(tokens, to_inside).astype(F32)
    tokens_first = reorder(tokens, to_first).astype(F32)
    out_grad = reorder(cotangent, to_inside).astype(F32)
    factor_one = rms_factor(tokens_in)
    normed = (tokens_first * factor_one * gain_first).astype(BF)
    raw = in_order(*(matmul(normed, half) for half in projections))
    heads_half = wide // 2

    def both_halves(at, width):
        return [half[:, at : at + width] for half in raw]

    query_raw = [
        piece[:, h * HD : (h + 1) * HD]
        for piece in both_halves(0, heads_half)
        for h in range(HQ // 2)
    ]
    key_raw = jnp.concatenate(both_halves(heads_half, HD // 2), axis=1)
    value_rows = jnp.concatenate(both_halves(heads_half + HD // 2, HD // 2), axis=1).astype(BF)
    cosine, sine = angles_of(query_pos)
    key_factor = rms_factor(key_raw)
    key_rows = rotate(key_raw * key_factor * key_scale, cosine, sine).astype(BF)
    key_values, came = place.gather_group(jnp.concatenate([key_rows, value_rows], axis=1))
    query_raw = [after(q, came) for q in query_raw]
    positions, segment_ids, query_pos, query_seg, first_all, first_other, up_own, projections = (
        lax.optimization_barrier(
            (
                positions,
                segment_ids,
                query_pos,
                query_seg,
                first_all,
                first_other,
                up_own,
                projections,
                came,
            )
        )[:8]
    )
    output_full = jnp.stack(
        in_order(*(block[:, 2 * rows + gain_rows :] for block in (first_all, first_other)))
    )
    output_full = jnp.transpose(
        output_full.reshape(2, nx, ny, nw * nz, -1, model), (1, 0, 3, 2, 4, 5)
    ).reshape(wide, model)
    up_full = place.gather_line(after(up_own, key_values))
    query_factor = [rms_factor(q) for q in query_raw]
    queries = jnp.concatenate(
        [
            rotate(q * f * query_scale, cosine, sine).astype(BF)
            for q, f in zip(query_raw, query_factor)
        ],
        axis=1,
    )
    attention = Attention(positions, segment_ids, query_pos, query_seg)
    attended, logs = attention.forward(after(queries, gate_full), key_values)
    down_full = place.gather_line(after(down_own, attended))
    projected = matmul(attended, output_full)
    factor_three = rms_factor(projected)
    mixed = tokens_in + projected * factor_three * mixed_scale
    factor_two = rms_factor(mixed)
    normed_two = (mixed * factor_two * feed_scale).astype(BF)
    near_blocks = place.gather_near(normed_two)
    def gelu_parts(value):
        scale = (2.0 / np.pi) ** 0.5
        square = value * value
        bend = jnp.tanh(scale * (value + 0.044715 * (square * value)))
        rise = 0.5 * (1.0 + bend)
        slope = 0.5 * value * (1.0 - bend * bend) * (scale * (1.0 + 3 * 0.044715 * square))
        return value * rise, rise + slope

    kept, hidden_blocks, branch_parts = [], [], []
    normed_blocks = [normed_two]
    for number in range(nx * ny):
        if number == 1:
            normed_blocks = place.gather_far(near_blocks, branch_parts[0])
        block = normed_blocks[number]
        gate_pre, up_pre = matmul(block, gate_full), matmul(block, up_full)
        gelu, gelu_slope = gelu_parts(gate_pre)
        kept.append(((gelu_slope * up_pre).astype(BF), gelu.astype(BF)))
        hidden_blocks.append((gelu * up_pre).astype(BF))
        branch_parts.append(matmul(hidden_blocks[-1], down_full))
    branch = place.scatter_plane(branch_parts)
    factor_four = rms_factor(branch)
    layer_out = reorder((mixed + branch * factor_four * final_scale).astype(BF), to_outside)

    branch_grad, final_term = norm_back(out_grad, branch, factor_four, final_scale)
    branch_grad = branch_grad.astype(BF)
    near_blocks = place.gather_near(branch_grad)
    branch_grad_blocks = [branch_grad]
    gate_grads, up_grads, normed_two_parts = [], [], []
    for number, factors in enumerate(kept):
        if number == 1:
            branch_grad_blocks = place.gather_far(near_blocks, normed_two_parts[0])
        block = branch_grad_blocks[number]
        hidden_grad = matmul_nt(block, down_full)
        gate_grad, up_grad = ((hidden_grad * f.astype(F32)).astype(BF) for f in factors)
        gate_grads.append(gate_grad)
        up_grads.append(up_grad)
        normed_two_parts.append(matmul_nt(gate_grad, gate_full) + matmul_nt(up_grad, up_full))
    normed_two_grad = place.scatter_plane(normed_two_parts)
    halfway = place.halfway
    normed_all = jnp.concatenate(normed_blocks)
    hidden_all = jnp.concatenate(hidden_blocks)
    down_terms = matmul_tn(
        after(hidden_all, normed_two_parts[-1]), jnp.concatenate(branch_grad_blocks)
    ).astype(BF)
    down_terms = place.cores_summed(down_terms)
    gate_terms = matmul_tn(
        normed_all, after(jnp.concatenate(gate_grads), down_terms, *halfway)
    ).astype(BF)
    gate_terms = place.cores_summed(gate_terms)
    down_rows = place.scatter_line(down_terms)

    mixed_part, feed_term = norm_back(normed_two_grad, mixed, factor_two, feed_scale)
    mixed_grad = out_grad + mixed_part
    projected_grad, mixed_term = norm_back(mixed_grad, projected, factor_three, mixed_scale)
    projected_grad = projected_grad.astype(BF)
    output_terms = matmul_tn(attended, projected_grad).astype(BF)
    attended_grad = matmul_nt(projected_grad, output_full).astype(BF)
    attended_grad = after(attended_grad, gate_terms)
    delta = jnp.stack(
        [
            jnp.sum(
                attended_grad[:, h * HD : (h + 1) * HD].astype(F32)
                * attended[:, h * HD : (h + 1) * HD].astype(F32),
                axis=1,
            )
            for h in range(HQ)
        ]
    ).reshape(1, -1)
    queries_grad, key_value_terms = attention.backward(
        queries, attended_grad, logs, delta, key_values
    )
    up_terms = []

    def up_terms_after(came):
        grads = after(jnp.concatenate(up_grads), came)
        up_terms.append(place.cores_summed(matmul_tn(normed_all, grads).astype(BF)))
        return up_terms[0]

    key_value_grad, came = place.scatter_group(key_value_terms, up_terms_after)
    up_terms = up_terms[0]
    output_terms = after(output_terms, came)
    gate_rows = place.scatter_line(gate_terms)
    up_rows = place.scatter_line(after(up_terms, key_value_grad))
    down_weight_grad = matmul(down_rows, to_outside)
    gate_up_rows = jnp.stack(
        [rows_of.reshape(nx, ny, rows, part) for rows_of in (gate_rows, up_rows)], axis=2
    )
    gate_up_rows = place.deal_plane(gate_up_rows).reshape(nx, ny, 2, rows, 2 * nw * nz, -1)
    gate_up_rows = jnp.transpose(gate_up_rows, (2, 3, 0, 4, 1, 5)).reshape(2, rows, FF)
    gate_weight_grad = gate_up_rows[0].astype(F32)
    up_weight_grad = gate_up_rows[1].astype(F32)
    key_grad_rows = key_value_grad[:, :HD]
    values_grad = key_value_grad[:, HD:].astype(BF)
    key_back = rotate(key_grad_rows, cosine, -sine)
    key_in_grad, key_term = norm_back(key_back, key_raw, key_factor, key_scale)
    key_in_grad = key_in_grad.astype(BF)
    query_in_grad, query_term = [], 0.0
    for h in range(HQ):
        query_back = rotate(queries_grad[:, h * HD : (h + 1) * HD], cosine, -sine)
        grad, term = norm_back(query_back, query_raw[h], query_factor[h], query_scale)
        query_in_grad.append(grad.astype(BF))
        query_term = query_term + term
    quarter = HD // 2
    raw_grad = []
    for c in range(2):
        raw_grad.append(
            jnp.concatenate(
                query_in_grad[c * HQ // 2 : (c + 1) * HQ // 2]
                + [
                    key_in_grad[:, c * quarter : (c + 1) * quarter],
                    values_grad[:, c * quarter : (c + 1) * quarter],
                ],
                axis=1,
            )
        )
    def chip_order(values):
        values = values.reshape(nx, 2, nw, nz, ny, -1)
        return jnp.transpose(values, (0, 4, 2, 3, 1, 5)).reshape(chips, 2, -1)

    def chip_order_inside(values):
        values = values.reshape(2, nw, nz, nx, ny, rows)
        return jnp.transpose(values, (3, 4, 1, 2, 0, 5)).reshape(chips, 2, rows)

    gain_terms = jnp.concatenate(
        [chip_order_inside(t) for t in (mixed_term, feed_term, final_term)]
        + [chip_order(query_term), chip_order(key_term)],
        axis=2,
    )
    gain_terms = jnp.moveaxis(gain_terms, 1, 0).astype(BF)
    gain_terms = jnp.pad(
        gain_terms, ((0, 0), (0, 0), (0, gain_rows * head_width - gain_terms.shape[2]))
    ).reshape(2, chips, gain_rows, head_width)
    output_terms = output_terms.reshape(nx, 2, nw * nz, ny, -1, model)
    output_terms = jnp.transpose(output_terms, (1, 0, 3, 2, 4, 5)).reshape(2, chips, -1, head_width)
    grads_pair = jnp.stack(raw_grad)

    def terms_of(which):
        return jnp.concatenate(
            [
                matmul_tn(normed, pick(grads_pair, which)).astype(BF).reshape(chips, 2 * rows, head_width),
                pick(gain_terms, which),
                pick(output_terms, which),
            ],
            axis=1,
        ).reshape(-1, head_width)

    first_terms = terms_of(core).astype(F32) + place.swap_core(terms_of(1 - core)).astype(F32)
    first_terms = first_terms.astype(BF)
    normed_grad = 0.0
    for half, grad in zip(in_order(*projections), raw_grad):
        half = matmul(inside_from_first, half).astype(BF)
        normed_grad = normed_grad + matmul_nt(after(grad, first_terms), half)
    tokens_part, _ = norm_back(normed_grad, tokens_in, factor_one, gain_one)
    tokens_grad = reorder((mixed_grad + tokens_part).astype(BF), to_outside)

    first_grad = place.scatter_chips(first_terms)
    projection_rows = first_grad[: 2 * rows].reshape(2, rows, head_width)
    projection_rows = cores_in_order(
        pick(projection_rows, core), place.swap_core(pick(projection_rows, 1 - core))
    )

    def whole_columns(a, b):
        return jnp.moveaxis(projection_rows[:, :, a:b], 0, 1).reshape(rows, -1)

    query_weight_grad = whole_columns(0, heads_half)
    key_weight_grad = whole_columns(heads_half, heads_half + quarter)
    value_weight_grad = whole_columns(heads_half + quarter, head_width)
    gain_grad = first_grad[2 * rows : 2 * rows + gain_rows].reshape(-1)
    (
        mixed_gain_grad,
        feed_gain_grad,
        final_gain_grad,
        query_gain_grad,
        key_gain_grad,
    ) = (gain_grad[a:b] for a, b in zip(spans[:5], spans[1:6]))
    attention_gain_grad = sum(
        jnp.sum(grad * weight.astype(F32), axis=1)
        for grad, weight in (
            (query_weight_grad, query_weight),
            (key_weight_grad, key_weight),
            (value_weight_grad, value_weight),
        )
    ) / attention_gain.astype(F32)
    output_weight_grad = reorder(first_grad[2 * rows + gain_rows :].reshape(-1, model), to_outside)
    return (
        layer_out,
        tokens_grad,
        attention_gain_grad,
        query_weight_grad,
        key_weight_grad,
        value_weight_grad,
        query_gain_grad,
        key_gain_grad,
        output_weight_grad,
        mixed_gain_grad,
        feed_gain_grad,
        gate_weight_grad,
        up_weight_grad,
        down_weight_grad,
        final_gain_grad,
    )


def solution(mesh):
    sizes = grid_of(mesh)
    grid = Mesh(mesh.devices.reshape(sizes), AXES)
    matrix, vector, group = P(AXES, None), P(AXES), P(("x", "core"))
    return jax.shard_map(
        lambda *arrays: body(sizes, *arrays),
        mesh=grid,
        in_specs=(
            matrix,
            vector,
            matrix,
            matrix,
            matrix,
            vector,
            vector,
            matrix,
            vector,
            vector,
            matrix,
            matrix,
            matrix,
            vector,
            group,
            group,
            matrix,
        ),
        out_specs=(
            matrix,
            matrix,
            vector,
            matrix,
            matrix,
            matrix,
            vector,
            vector,
            matrix,
            vector,
            vector,
            matrix,
            matrix,
            matrix,
            vector,
        ),
        check_vma=False,
    )
```

```python
import functools

import jax
import jax.numpy as jnp
import numpy as np
from jax import lax
from jax.experimental import pallas as pl
from jax.experimental.pallas import tpu as pltpu
from jax.sharding import Mesh, PartitionSpec as P

FF = 6912
HQ = 4
HD = 256
EPSILON = 1e-06
THETA = 1000000.0
BF = jnp.bfloat16
F32 = jnp.float32

AXES = ("x", "core", "w", "z", "y")
CTX_GRID = {8: (1, 4, 2), 32: (2, 4, 4)}


def grid_of(mesh):
    dp, ctx = mesh.shape["dp"], mesh.shape["ctx"]
    w, z, y = CTX_GRID.get(ctx, (1, ctx, 1))
    return (dp // 2, 2, w, z, y)


class Place:
    def __init__(self, sizes):
        self.size = dict(zip(AXES, sizes))
        self.at = {a: lax.axis_index(a) for a in AXES}

    def shift(self, value, axis, by):
        n = self.size[axis]
        return lax.ppermute(value, axis, [(i, (i + by) % n) for i in range(n)])

    def shift_wz(self, value, kw, kz):
        nw, nz = self.size["w"], self.size["z"]
        pairs = [
            (w * nz + z, ((w + kw) % nw) * nz + (z + kz) % nz) for w in range(nw) for z in range(nz)
        ]
        return lax.ppermute(value, ("w", "z"), pairs)

    def swap_core(self, value):
        return lax.ppermute(value, "core", [(0, 1), (1, 0)])

    def wz_steps(self):
        return [(kw, kz) for kw in range(self.size["w"]) for kz in range(self.size["z"])]

    def gather_wz(self, own):
        return [own if kw == kz == 0 else self.shift_wz(own, kw, kz) for kw, kz in self.wz_steps()]

    def gather_line(self, own):
        return lax.all_gather(own, ("core", "w", "z"), axis=0, tiled=True)

    def cores_summed(self, full):
        full = full.reshape(2, -1, full.shape[-1])
        give = self.swap_core(lax.dynamic_index_in_dim(full, 1 - self.at["core"], 0, keepdims=False))
        keep = lax.dynamic_index_in_dim(full, self.at["core"], 0, keepdims=False)
        return (keep.astype(F32) + give.astype(F32)).astype(BF)

    def scatter_line(self, rows):
        return lax.psum_scatter(rows, ("w", "z"), scatter_dimension=0, tiled=True)

    def plane_steps(self):
        return [(dx, dy) for dx in range(self.size["x"]) for dy in range(self.size["y"])]

    def gather_near(self, own):
        blocks = {(0, 0): own}
        for dx in range(1, self.size["x"]):
            blocks[dx, 0] = self.shift(own, "x", dx)
        for dy in range(1, self.size["y"]):
            blocks[0, dy] = self.shift(own, "y", dy)
        return blocks

    def gather_far(self, near, *hold):
        blocks = {step: after(block, *hold) if hold else block for step, block in near.items()}
        cut = blocks[0, 0].shape[0] // 2
        for dx, dy in self.plane_steps():
            if dx and dy:
                top = self.shift(blocks[dx, 0][:cut], "y", dy)
                low = self.shift(blocks[0, dy][cut:], "x", dx)
                blocks[dx, dy] = jnp.concatenate([top, low])
        return [blocks[step] for step in self.plane_steps()]

    def scatter_plane(self, parts):
        parts = dict(zip(self.plane_steps(), parts))
        cut = parts[0, 0].shape[0] // 2
        tops = {d: parts[d, 0][:cut] for d in range(self.size["x"])}
        lows = {d: parts[0, d][cut:] for d in range(self.size["y"])}
        own_top, own_low = parts[0, 0][:cut], parts[0, 0][cut:]
        for dx in range(1, self.size["x"]):
            own_low = own_low + self.shift(parts[dx, 0][cut:].astype(BF), "x", -dx).astype(F32)
        for dy in range(1, self.size["y"]):
            own_top = own_top + self.shift(parts[0, dy][:cut].astype(BF), "y", -dy).astype(F32)
        for dx, dy in self.plane_steps():
            if dx and dy:
                part = parts[dx, dy].astype(BF)
                tops[dx] = tops[dx] + self.shift(part[:cut], "y", -dy).astype(F32)
                lows[dy] = lows[dy] + self.shift(part[cut:], "x", -dx).astype(F32)
        self.halfway = [tops[self.size["x"] - 1], lows[self.size["y"] - 1]]
        for dx in range(1, self.size["x"]):
            own_top = own_top + self.shift(tops[dx].astype(BF), "x", -dx).astype(F32)
        for dy in range(1, self.size["y"]):
            own_low = own_low + self.shift(lows[dy].astype(BF), "y", -dy).astype(F32)
        return jnp.concatenate([own_top, own_low])

    def deal_plane(self, pieces, hold=(), hold_end=()):
        for dim, axis in ((0, "x"), (1, "y")):
            n, here = self.size[axis], self.at[axis]
            dealt = []
            for d in range(n):
                piece = lax.dynamic_index_in_dim(pieces, (here + d) % n, dim)
                dealt.append(piece if d == 0 else self.shift(piece, axis, d))
            wait_for = hold if axis == "x" else hold_end
            if wait_for:
                dealt = [after(piece, *wait_for) for piece in dealt]
            if n == 2:
                own, other = dealt
                low = jnp.where(here == 0, own, other)
                pieces = jnp.concatenate([low, jnp.where(here == 0, other, own)], axis=dim)
            else:
                pieces = jnp.zeros_like(pieces)
                for d in range(n):
                    pieces = lax.dynamic_update_slice_in_dim(pieces, dealt[d], (here - d) % n, dim)
        return pieces

    def ctx_chip(self, spot):
        return (spot["w"] * self.size["z"] + spot["z"]) * self.size["y"] + spot["y"]

    def gather_chips(self, own):
        size, at = self.size, self.at
        rows, width = own.shape
        line = size["w"] * size["z"] * rows
        mine = jnp.zeros((line, width), own.dtype)
        for block, (kw, kz) in zip(self.gather_wz(own), self.wz_steps()):
            w, z = (at["w"] - kw) % size["w"], (at["z"] - kz) % size["z"]
            mine = lax.dynamic_update_slice(mine, block, ((w * size["z"] + z) * rows, 0))
        full = jnp.zeros((size["x"] * size["y"] * line, width), own.dtype)
        near = self.gather_near(mine)
        for block, (dx, dy) in zip(self.gather_far(near), self.plane_steps()):
            x, y = (at["x"] - dx) % size["x"], (at["y"] - dy) % size["y"]
            full = lax.dynamic_update_slice(full, block, ((x * size["y"] + y) * line, 0))
        return full, mine, list(near.values())

    def scatter_chips(self, full, hold):
        size, at = self.size, self.at
        full = full.reshape((size["x"], size["y"], -1, full.shape[-1]))
        parts = [
            full[(at["x"] - dx) % size["x"], (at["y"] - dy) % size["y"]].astype(F32)
            for dx, dy in self.plane_steps()
        ]
        mine = after(self.scatter_plane(parts), hold)
        mine = mine.reshape((size["w"], size["z"], -1, mine.shape[-1]))
        total = None
        for kw, kz in reversed(self.wz_steps()):
            part = mine[(at["w"] + kw) % size["w"], (at["z"] + kz) % size["z"]]
            if kw or kz:
                part = self.shift_wz(part.astype(BF), kw, kz).astype(F32)
            total = part if total is None else total + part
        return total

    def gather_group(self, own):
        size, at = self.size, self.at
        rows = own.shape[0]
        full = jnp.zeros((size["w"] * size["z"] * size["y"] * rows, own.shape[1]), own.dtype)
        for kw, kz in self.wz_steps():
            block = own if kw == kz == 0 else self.shift_wz(own, kw, kz)
            spot = {"w": (at["w"] - kw) % size["w"], "z": (at["z"] - kz) % size["z"]}
            for ky in range(size["y"]):
                block_y = block if ky == 0 else self.shift(block, "y", ky)
                spot["y"] = (at["y"] - ky) % size["y"]
                full = lax.dynamic_update_slice(full, block_y, (self.ctx_chip(spot) * rows, 0))
        return full

    def scatter_group(self, full):
        size, at = self.size, self.at
        full = full.reshape((size["w"], size["z"], size["y"], -1, full.shape[-1]))
        total = None
        for kw, kz in reversed(self.wz_steps()):
            part = full[(at["w"] + kw) % size["w"], (at["z"] + kz) % size["z"]]
            acc = part[at["y"]].astype(F32)
            for dy in range(1, size["y"]):
                acc = acc + self.shift(part[(at["y"] + dy) % size["y"]], "y", dy).astype(F32)
            if kw or kz:
                acc = self.shift_wz(acc.astype(BF), kw, kz).astype(F32)
            total = acc if total is None else total + acc
        return total


def after(value, *others):
    return lax.optimization_barrier((value,) + others)[0]


def rms_factor(values):
    return lax.rsqrt(jnp.mean(values * values, axis=-1, keepdims=True) + EPSILON)


def norm_back(incoming, values, factor, gain):
    scaled = incoming * gain
    gain_term = jnp.sum((incoming * values * factor).reshape(-1, values.shape[-1]), axis=0)
    inner = jnp.mean(scaled * values, axis=-1, keepdims=True)
    return (factor * scaled - values * (factor * factor * factor) * inner, gain_term)


def angles_of(position_ids):
    half_width = HD // 2
    inverse = THETA ** (-(jnp.arange(half_width, dtype=F32) * 2.0) / HD)
    angle = position_ids.astype(F32)[:, None] * inverse[None, :]
    return (jnp.cos(angle), jnp.sin(angle))


def rotate(values, cosine, sine):
    half_width = values.shape[-1] // 2
    first_half = values[..., :half_width]
    second_half = values[..., half_width:]
    return jnp.concatenate(
        [first_half * cosine - second_half * sine, second_half * cosine + first_half * sine],
        axis=-1,
    )


def matmul(left, right):
    return jnp.dot(left, right, preferred_element_type=F32)


def matmul_nt(left, right):
    return jnp.einsum("ij,kj->ik", left, right, preferred_element_type=F32)


def matmul_tn(left, right):
    return jnp.einsum("ji,jk->ik", left, right, preferred_element_type=F32)


def allowed_pairs(key_pos, key_seg, query_pos, query_seg):
    return (key_pos <= query_pos) & ((key_seg == 0) | (key_seg == query_seg))


def forward_kernel(
    live, q_ref, kv_ref, key_pos, key_seg, query_pos, query_seg, out_ref, log_ref, acc, total
):
    block = pl.program_id(0)
    local = q_ref.shape[0]

    @pl.when(block == 0)
    def _():
        acc[...] = jnp.zeros_like(acc)
        total[...] = jnp.zeros_like(total)

    @pl.when(live[block] != 0)
    def _():
        keys = kv_ref[:, :HD]
        values_t = kv_ref[:, HD:].T
        allowed = allowed_pairs(key_pos[...], key_seg[...], query_pos[...], query_seg[...])
        for head in range(HQ):
            mine = pl.ds(head * local, local)
            scores = matmul_nt(keys, q_ref[:, head * HD : (head + 1) * HD]) * HD ** (-0.5)
            weights = jnp.where(allowed, jnp.exp(scores), 0.0)
            total[:, mine] += jnp.sum(weights, axis=0, keepdims=True)
            acc[:, mine] += matmul(values_t, weights.astype(BF))

    @pl.when(block == pl.num_programs(0) - 1)
    def _():
        for head in range(HQ):
            mine = pl.ds(head * local, local)
            out_ref[:, head * HD : (head + 1) * HD] = (acc[:, mine] / total[:, mine]).T.astype(BF)
        log_ref[...] = jnp.log(total[...])


def backward_kernel(
    live,
    q_ref,
    grad_ref,
    log_ref,
    delta_ref,
    kv_ref,
    key_pos,
    key_seg,
    query_pos,
    query_seg,
    q_grad_ref,
    kv_grad_ref,
    acc,
):
    block = pl.program_id(0)
    local = q_ref.shape[0]

    @pl.when(block == 0)
    def _():
        acc[...] = jnp.zeros_like(acc)

    @pl.when(live[block] == 0)
    def _():
        kv_grad_ref[...] = jnp.zeros_like(kv_grad_ref)

    @pl.when(live[block] != 0)
    def _():
        keys = kv_ref[:, :HD]
        keys_t = keys.T
        values = kv_ref[:, HD:]
        allowed = allowed_pairs(key_pos[...], key_seg[...], query_pos[...], query_seg[...])
        key_grad = jnp.zeros(keys.shape, F32)
        value_grad = jnp.zeros(keys.shape, F32)
        for head in range(HQ):
            mine = pl.ds(head * local, local)
            queries = q_ref[:, head * HD : (head + 1) * HD]
            grads = grad_ref[:, head * HD : (head + 1) * HD]
            scores = matmul_nt(keys, queries) * HD ** (-0.5)
            probs = jnp.where(allowed, jnp.exp(scores - log_ref[:, mine]), 0.0)
            prob_grad = matmul_nt(values, grads)
            score_grad = (probs * (prob_grad - delta_ref[:, mine]) * HD ** (-0.5)).astype(BF)
            value_grad += matmul(probs.astype(BF), grads)
            key_grad += matmul(score_grad, queries)
            acc[:, mine] += matmul(keys_t, score_grad)
        kv_grad_ref[:, :HD] = key_grad.astype(BF)
        kv_grad_ref[:, HD:] = value_grad.astype(BF)

    @pl.when(block == pl.num_programs(0) - 1)
    def _():
        for head in range(HQ):
            mine = pl.ds(head * local, local)
            q_grad_ref[:, head * HD : (head + 1) * HD] = acc[:, mine].T


class Ring:
    def __init__(self, sizes):
        _, _, self.nw, self.nz, self.ny = sizes
        self.line = self.nw * self.nz
        self.w, self.z, self.y = (lax.axis_index(a) for a in ("w", "z", "y"))

    def spot(self, k, ky):
        w = lax.rem(self.w + k // self.nz + self.nw, self.nw)
        z = lax.rem(self.z + k % self.nz + self.nz, self.nz)
        return w, z, lax.rem(self.y + ky + self.ny, self.ny)

    def device(self, k, ky):
        w, z, y = self.spot(k, ky)
        return {"w": w, "z": z, "y": y}

    def block(self, k, ky):
        w, z, y = self.spot(k, ky)
        return (w * self.nz + z) * self.ny + y

    def source(self, k, ky):
        w = lax.rem(self.w - k // self.nz + self.nw, self.nw)
        z = lax.rem(self.z - k % self.nz + self.nz, self.nz)
        return (w * self.nz + z) * self.ny + lax.rem(self.y - ky + self.ny, self.ny)

    def meet(self):
        barrier = pltpu.get_barrier_semaphore()
        peers = [(k, 0) for k in range(1, self.line)] + [(0, ky) for ky in range(1, self.ny)]
        for step in peers:
            pl.semaphore_signal(
                barrier, inc=1, device_id=self.device(*step), device_id_type=pl.DeviceIdType.MESH
            )
        pl.semaphore_wait(barrier, len(peers))

    def copy(self, source, target, sems, k, ky, to):
        send, recv = sems
        return pltpu.make_async_remote_copy(
            src_ref=source,
            dst_ref=target,
            send_sem=send.at[k, ky],
            recv_sem=recv.at[k, ky],
            device_id=self.device(*to),
            device_id_type=pl.DeviceIdType.MESH,
        )


def gather_attend_kernel(
    sizes,
    own_ref,
    raw_ref,
    gain_ref,
    cos_ref,
    sin_ref,
    key_pos,
    key_seg,
    query_pos,
    query_seg,
    all_ref,
    q_ref,
    out_ref,
    log_ref,
    held,
    acc,
    total,
    send_sem,
    recv_sem,
    out_sem,
):
    ring = Ring(sizes)
    local = own_ref.shape[0]
    sems = (send_sem, recv_sem)

    def rows(block):
        return pl.ds(pl.multiple_of(block * local, local), local)

    mine = held.at[rows(ring.block(0, 0)), :]
    ring.meet()
    for ky in range(1, ring.ny):
        ring.copy(own_ref, mine, sems, 0, ky, (0, ky)).start()
    for k in range(1, ring.line):
        ring.copy(own_ref, mine, sems, k, 0, (k, 0)).start()
    held[rows(ring.block(0, 0)), :] = own_ref[...]
    acc[...] = jnp.zeros_like(acc)
    total[...] = jnp.zeros_like(total)
    for head in range(HQ):
        raw = raw_ref[:, head * HD : (head + 1) * HD]
        scaled = raw * rms_factor(raw) * gain_ref[...]
        q_ref[:, head * HD : (head + 1) * HD] = rotate(scaled, cos_ref[...], sin_ref[...]).astype(BF)

    def attend(block):
        here = rows(block)
        keys = held[here, :HD]
        values_t = held[here, HD:].T
        allowed = allowed_pairs(key_pos[here, :], key_seg[here, :], query_pos[...], query_seg[...])
        for head in range(HQ):
            place = pl.ds(head * local, local)
            scores = matmul_nt(keys, q_ref[:, head * HD : (head + 1) * HD]) * HD ** (-0.5)
            weights = jnp.where(allowed, jnp.exp(scores), 0.0)
            total[:, place] += jnp.sum(weights, axis=0, keepdims=True)
            acc[:, place] += matmul(values_t, weights.astype(BF))

    def came(k, ky):
        piece = held.at[rows(ring.source(k, ky)), :]
        ring.copy(piece, piece, sems, k, ky, (k, ky)).wait_recv()

    @pl.loop(0, ring.ny)
    def _(ky):
        @pl.when(ky > 0)
        def _():
            came(0, ky)

        attend(ring.source(0, ky))

    @pl.loop(1, ring.line)
    def _(k):
        came(k, 0)
        piece = held.at[rows(ring.source(k, 0)), :]
        for ky in range(1, ring.ny):
            ring.copy(piece, piece, sems, k, ky, (0, ky)).start()
        attend(ring.source(k, 0))

    for ky in range(1, ring.ny):

        @pl.loop(1, ring.line)
        def _(k, ky=ky):
            came(k, ky)
            attend(ring.source(k, ky))

    keep = pltpu.make_async_copy(held, all_ref, out_sem)
    keep.start()
    for head in range(HQ):
        place = pl.ds(head * local, local)
        out_ref[:, head * HD : (head + 1) * HD] = (acc[:, place] / total[:, place]).T.astype(BF)
    log_ref[...] = jnp.log(total[...])
    for ky in range(1, ring.ny):
        ring.copy(own_ref, mine, sems, 0, ky, (0, ky)).wait_send()
    for k in range(1, ring.line):
        ring.copy(own_ref, mine, sems, k, 0, (k, 0)).wait_send()
        for ky in range(1, ring.ny):
            ring.copy(own_ref, mine, sems, k, ky, (0, ky)).wait_send()
    keep.wait()


def attend_back_kernel(
    sizes,
    q_ref,
    grad_ref,
    log_ref,
    delta_ref,
    all_ref,
    key_pos,
    key_seg,
    query_pos,
    query_seg,
    q_grad_ref,
    own_grad_ref,
    acc,
    term,
    from_y,
    on_z,
    from_z,
    send_y,
    recv_y,
    send_z,
    recv_z,
):
    ring = Ring(sizes)
    local = q_ref.shape[0]
    along_y, along_z = (send_y, recv_y), (send_z, recv_z)

    def to_y(k, ky):
        return ring.copy(term.at[k, ky], from_y.at[k, ky], along_y, k, ky, (0, ky))

    def to_z(k):
        return ring.copy(on_z.at[k], from_z.at[k], along_z, k, 0, (k, 0))

    def terms(block):
        here = pl.ds(pl.multiple_of(block * local, local), local)
        keys = all_ref[here, :HD]
        keys_t = keys.T
        values = all_ref[here, HD:]
        allowed = allowed_pairs(key_pos[here, :], key_seg[here, :], query_pos[...], query_seg[...])
        key_grad = jnp.zeros(keys.shape, F32)
        value_grad = jnp.zeros(keys.shape, F32)
        for head in range(HQ):
            place = pl.ds(head * local, local)
            queries = q_ref[:, head * HD : (head + 1) * HD]
            grads = grad_ref[:, head * HD : (head + 1) * HD]
            scores = matmul_nt(keys, queries) * HD ** (-0.5)
            probs = jnp.where(allowed, jnp.exp(scores - log_ref[:, place]), 0.0)
            prob_grad = matmul_nt(values, grads)
            score_grad = (probs * (prob_grad - delta_ref[:, place]) * HD ** (-0.5)).astype(BF)
            value_grad += matmul(probs.astype(BF), grads)
            key_grad += matmul(score_grad, queries)
            acc[:, place] += matmul(keys_t, score_grad)
        return key_grad, value_grad

    def keep(ref, pair):
        ref[:, :HD] = pair[0].astype(ref.dtype)
        ref[:, HD:] = pair[1].astype(ref.dtype)

    ring.meet()
    acc[...] = jnp.zeros_like(acc)
    for ky in range(1, ring.ny):

        @pl.loop(1, ring.line)
        def _(k, ky=ky):
            keep(term.at[k, ky], terms(ring.block(k, ky)))
            to_y(k, ky).start()

    @pl.loop(1, ring.line)
    def _(k):
        keep(own_grad_ref, terms(ring.block(k, 0)))
        for ky in range(1, ring.ny):
            to_y(k, ky).wait_recv()
            own_grad_ref[...] += from_y[k, ky].astype(F32)
        on_z[k] = own_grad_ref[...].astype(BF)
        to_z(k).start()

    @pl.loop(0, ring.ny)
    def _(step):
        ky = lax.rem(step + 1, ring.ny)
        pair = terms(ring.block(0, ky))

        @pl.when(ky > 0)
        def _():
            keep(term.at[0, ky], pair)
            to_y(0, ky).start()

        @pl.when(ky == 0)
        def _():
            keep(own_grad_ref, pair)

    for head in range(HQ):
        place = pl.ds(head * local, local)
        q_grad_ref[:, head * HD : (head + 1) * HD] = acc[:, place].T
    for ky in range(1, ring.ny):
        to_y(0, ky).wait_recv()
        own_grad_ref[...] += from_y[0, ky].astype(F32)
    for k in range(1, ring.line):
        to_z(k).wait_recv()
        own_grad_ref[...] += from_z[k].astype(F32)
        to_z(k).wait_send()
    for k in range(ring.line):
        for ky in range(1, ring.ny):
            to_y(k, ky).wait_send()


IN_VMEM = pl.BlockSpec(memory_space=pltpu.VMEM)


def kernel_settings(number):
    return dict(
        compiler_params=pltpu.CompilerParams(
            collective_id=number, has_side_effects=True, vmem_limit_bytes=56 << 20
        ),
        cost_estimate=pl.CostEstimate(
            flops=5 * 10**10, bytes_accessed=16 << 20, transcendentals=0
        ),
    )


def gather_attend(sizes, own, raw, gain, cosine, sine, marks):
    local, wide = raw.shape
    _, _, nw, nz, ny = sizes
    line = nw * nz
    full = jax.ShapeDtypeStruct((line * ny * local, own.shape[1]), BF)
    return pl.pallas_call(
        functools.partial(gather_attend_kernel, sizes),
        out_shape=(
            full,
            jax.ShapeDtypeStruct((local, wide), BF),
            jax.ShapeDtypeStruct((local, wide), BF),
            jax.ShapeDtypeStruct((1, HQ * local), F32),
        ),
        in_specs=[IN_VMEM] * 9,
        out_specs=(pl.BlockSpec(memory_space=pl.ANY), IN_VMEM, IN_VMEM, IN_VMEM),
        scratch_shapes=[
            pltpu.VMEM(full.shape, BF),
            pltpu.VMEM((HD, HQ * local), F32),
            pltpu.VMEM((1, HQ * local), F32),
            pltpu.SemaphoreType.DMA((line, ny)),
            pltpu.SemaphoreType.DMA((line, ny)),
            pltpu.SemaphoreType.DMA,
        ],
        **kernel_settings(0),
    )(own, raw, gain, cosine, sine, *marks)


def attend_back(sizes, queries, grads, logs, delta, key_values, marks):
    local, wide = queries.shape
    _, _, nw, nz, ny = sizes
    line = nw * nz
    width = key_values.shape[1]
    return pl.pallas_call(
        functools.partial(attend_back_kernel, sizes),
        out_shape=(
            jax.ShapeDtypeStruct((local, wide), F32),
            jax.ShapeDtypeStruct((local, width), F32),
        ),
        in_specs=[IN_VMEM] * 9,
        out_specs=(IN_VMEM, IN_VMEM),
        scratch_shapes=[
            pltpu.VMEM((HD, HQ * local), F32),
            pltpu.VMEM((line, ny, local, width), BF),
            pltpu.VMEM((line, ny, local, width), BF),
            pltpu.VMEM((line, local, width), BF),
            pltpu.VMEM((line, local, width), BF),
            pltpu.SemaphoreType.DMA((line, ny)),
            pltpu.SemaphoreType.DMA((line, ny)),
            pltpu.SemaphoreType.DMA((line, 1)),
            pltpu.SemaphoreType.DMA((line, 1)),
        ],
        **kernel_settings(1),
    )(queries, grads, logs, delta, key_values, *marks)


class Attention:
    def __init__(self, positions, segment_ids, query_pos, query_seg):
        local = query_pos.shape[0]
        self.local = local
        self.blocks = positions.shape[0] // local
        pos = positions.reshape(self.blocks, local)
        seg = segment_ids.reshape(self.blocks, local)
        seg_low, seg_high = jnp.min(seg, axis=1), jnp.max(seg, axis=1)
        late = jnp.min(pos, axis=1) > jnp.max(query_pos)
        foreign = (seg_low > 0) & (
            (seg_low > jnp.max(query_seg)) | (seg_high < jnp.min(query_seg))
        )
        self.live = jnp.where(late | foreign, 0, 1).astype(jnp.int32)
        self.marks = (
            positions.reshape(-1, 1),
            segment_ids.reshape(-1, 1),
            query_pos.reshape(1, -1),
            query_seg.reshape(1, -1),
        )

    def specs(self):
        local = self.local
        whole = lambda *shape: pl.BlockSpec(shape, lambda j, live: (0,) * len(shape))
        rows = lambda width: pl.BlockSpec((local, width), lambda j, live: (j, 0))
        marks = [rows(1), rows(1), whole(1, local), whole(1, local)]
        return whole, rows, marks

    def forward(self, queries, key_values):
        local, wide = queries.shape
        whole, rows, marks = self.specs()
        return pl.pallas_call(
            forward_kernel,
            out_shape=(
                jax.ShapeDtypeStruct((local, wide), BF),
                jax.ShapeDtypeStruct((1, HQ * local), F32),
            ),
            grid_spec=pltpu.PrefetchScalarGridSpec(
                num_scalar_prefetch=1,
                grid=(self.blocks,),
                in_specs=[whole(local, wide), rows(2 * HD)] + marks,
                out_specs=(whole(local, wide), whole(1, HQ * local)),
                scratch_shapes=[
                    pltpu.VMEM((HD, HQ * local), F32),
                    pltpu.VMEM((1, HQ * local), F32),
                ],
            ),
            cost_estimate=pl.CostEstimate(
                flops=20 * 4 * local * local * HD, bytes_accessed=8 << 20, transcendentals=0
            ),
        )(self.live, queries, key_values, *self.marks)

    def backward(self, queries, grads, logs, delta, key_values):
        local, wide = queries.shape
        whole, rows, marks = self.specs()
        return pl.pallas_call(
            backward_kernel,
            out_shape=(
                jax.ShapeDtypeStruct((local, wide), F32),
                jax.ShapeDtypeStruct(key_values.shape, BF),
            ),
            grid_spec=pltpu.PrefetchScalarGridSpec(
                num_scalar_prefetch=1,
                grid=(self.blocks,),
                in_specs=[
                    whole(local, wide),
                    whole(local, wide),
                    whole(1, HQ * local),
                    whole(1, HQ * local),
                    rows(2 * HD),
                ]
                + marks,
                out_specs=(whole(local, wide), rows(2 * HD)),
                scratch_shapes=[pltpu.VMEM((HD, HQ * local), F32)],
            ),
            cost_estimate=pl.CostEstimate(
                flops=20 * 10 * local * local * HD, bytes_accessed=16 << 20, transcendentals=0
            ),
        )(self.live, queries, grads, logs, delta, key_values, *self.marks)


def body(
    sizes,
    tokens,
    attention_gain,
    query_weight,
    key_weight,
    value_weight,
    query_gain,
    key_gain,
    output_weight,
    mixed_gain,
    feed_gain,
    gate_weight,
    up_weight,
    down_weight,
    final_gain,
    segment_ids,
    positions,
    cotangent,
):
    place = Place(sizes)
    nx, _, nw, nz, ny = sizes
    chips = nx * nw * nz * ny
    core = place.at["core"]
    local, model = tokens.shape
    rows = query_weight.shape[0]
    wide = HQ * HD
    offset = place.ctx_chip(place.at) * local
    query_pos = lax.dynamic_slice_in_dim(positions, offset, local)
    query_seg = lax.dynamic_slice_in_dim(segment_ids, offset, local)

    def pick(pair, which):
        return lax.dynamic_index_in_dim(pair, which, 0, keepdims=False)

    def cores_in_order(own, other):
        return jnp.where(core == 0, jnp.stack([own, other]), jnp.stack([other, own]))

    outside = np.arange(model).reshape(nx, 2, nw, nz, ny, rows)
    inside = outside.transpose(1, 2, 3, 0, 4, 5).reshape(-1)
    first = outside.transpose(0, 4, 2, 3, 1, 5).reshape(-1)

    def order_change(source, target):
        at = jnp.asarray(np.argsort(source)[target], jnp.int32)
        return (lax.iota(jnp.int32, model)[:, None] == at[None, :]).astype(BF)

    outside = np.arange(model)
    to_inside = order_change(outside, inside)
    to_outside = order_change(inside, outside)
    to_first = order_change(outside, first)
    inside_from_first = order_change(inside, first)

    def reorder(values, matrix):
        if values.dtype == F32:
            return jnp.dot(values, matrix.astype(F32), precision=lax.Precision.HIGHEST)
        return matmul(values, matrix).astype(BF)

    def column_halves(query, key, value):
        cut = lambda m: m.reshape(m.shape[0], 2, -1)
        halves = jnp.concatenate([cut(query), cut(key), cut(value)], axis=2)
        return jnp.moveaxis(halves, 1, 0)

    head_width = wide // 2 + HD
    gains = jnp.concatenate(
        [mixed_gain, feed_gain, final_gain, query_gain, key_gain, attention_gain]
    )
    gain_count = gains.size
    projections = column_halves(query_weight, key_weight, value_weight)
    gain_rows = -(-gain_count // head_width) * 8
    gain_block = jnp.zeros((gain_rows * head_width,), BF).at[:gain_count].set(gains)
    small = jnp.concatenate(
        [gain_block.reshape(gain_rows, head_width), reorder(output_weight, to_inside).reshape(-1, head_width)]
    )
    first_own = jnp.concatenate(
        [
            cores_in_order(pick(projections, core), place.swap_core(pick(projections, 1 - core))).reshape(
                2 * rows, head_width
            ),
            small,
        ]
    )
    first_all, first_came, next_came = place.gather_chips(first_own)

    gate_weight, up_weight, down_weight, tokens, cotangent, _ = lax.optimization_barrier(
        (gate_weight, up_weight, down_weight, tokens, cotangent, first_own)
    )
    part = FF // (nx * ny)
    gate_up = jnp.stack([gate_weight, up_weight]).reshape(2, rows, nx, 2 * nw * nz, ny, -1)
    gate_up = jnp.transpose(gate_up, (2, 4, 0, 1, 3, 5)).reshape(nx, ny, 2, rows, part)
    down_own = reorder(down_weight, to_inside)
    down_full = place.gather_line(down_own)
    first_other = place.swap_core(first_all)

    def in_order(own, other):
        return jnp.where(core == 0, own, other), jnp.where(core == 0, other, own)

    first_all, first_other = (
        block.reshape(chips, first_own.shape[0], head_width) for block in (first_all, first_other)
    )
    projections = tuple(
        block[:, : 2 * rows].reshape(model, head_width) for block in (first_all, first_other)
    )
    gains_all = jnp.stack(
        in_order(*(block[:, 2 * rows, :gain_count] for block in (first_all, first_other)))
    )
    gains_all = jnp.moveaxis(gains_all.astype(F32), 0, 1)
    spans = np.cumsum([0, rows, rows, rows, query_gain.size, key_gain.size, rows])
    mixed_scale, feed_scale, final_scale, query_scale, key_scale, gain_one = (
        gains_all[:, :, a:b] for a, b in zip(spans[:-1], spans[1:])
    )
    gain_first = gain_one.reshape(model)

    def inside_order(values):
        values = values.reshape(nx, ny, nw, nz, 2, rows)
        return jnp.transpose(values, (4, 2, 3, 0, 1, 5)).reshape(-1)

    gain_one, mixed_scale, feed_scale, final_scale = (
        inside_order(g) for g in (gain_one, mixed_scale, feed_scale, final_scale)
    )

    def true_order(values):
        values = values.reshape(nx, ny, nw, nz, 2, -1)
        return jnp.transpose(values, (0, 4, 2, 3, 1, 5)).reshape(-1)

    query_scale, key_scale = true_order(query_scale), true_order(key_scale)

    tokens_in = reorder(tokens, to_inside).astype(F32)
    tokens_first = reorder(tokens, to_first).astype(F32)
    out_grad = reorder(cotangent, to_inside).astype(F32)
    factor_one = rms_factor(tokens_in)
    normed = (tokens_first * factor_one * gain_first).astype(BF)
    raw = in_order(*(matmul(normed, half) for half in projections))
    heads_half = wide // 2

    def both_halves(at, width):
        return [half[:, at : at + width] for half in raw]

    query_raw = [
        piece[:, h * HD : (h + 1) * HD]
        for piece in both_halves(0, heads_half)
        for h in range(HQ // 2)
    ]
    key_raw = jnp.concatenate(both_halves(heads_half, HD // 2), axis=1)
    value_rows = jnp.concatenate(both_halves(heads_half + HD // 2, HD // 2), axis=1).astype(BF)
    cosine, sine = angles_of(query_pos)
    key_factor = rms_factor(key_raw)
    key_rows = rotate(key_raw * key_factor * key_scale, cosine, sine).astype(BF)
    own_key_values = jnp.concatenate([key_rows, value_rows], axis=1)
    gate_up = place.deal_plane(gate_up, [first_came], next_came + [own_key_values])
    gate_own, up_own = (gate_up[:, :, i].reshape(-1, part) for i in range(2))
    gate_full, up_full = place.gather_line(gate_own), place.gather_line(up_own)
    own_key_values = after(own_key_values, gate_own, up_own, down_full)
    attention = Attention(positions, segment_ids, query_pos, query_seg)
    together = nw * nz * ny <= 8
    if together:
        key_values, queries, attended, logs = gather_attend(
            sizes,
            own_key_values,
            jnp.concatenate(query_raw, axis=1),
            query_scale.reshape(1, -1),
            cosine,
            sine,
            attention.marks,
        )
    else:
        key_values = place.gather_group(own_key_values)
        queries = jnp.concatenate(
            [
                rotate(q * rms_factor(q) * query_scale, cosine, sine).astype(BF)
                for q in query_raw
            ],
            axis=1,
        )
        attended, logs = attention.forward(queries, key_values)
    query_factor = [rms_factor(q) for q in query_raw]
    first_all, first_other, projections, query_factor = lax.optimization_barrier(
        (first_all, first_other, projections, query_factor, attended)
    )[:4]
    output_full = jnp.stack(
        in_order(*(block[:, 2 * rows + gain_rows :] for block in (first_all, first_other)))
    )
    output_full = jnp.transpose(
        output_full.reshape(2, nx, ny, nw * nz, -1, model), (1, 0, 3, 2, 4, 5)
    ).reshape(wide, model)
    projected = matmul(attended, output_full)
    factor_three = rms_factor(projected)
    mixed = tokens_in + projected * factor_three * mixed_scale
    factor_two = rms_factor(mixed)
    normed_two = (mixed * factor_two * feed_scale).astype(BF)
    near_blocks = place.gather_near(normed_two)
    def gelu_parts(value):
        scale = (2.0 / np.pi) ** 0.5
        square = value * value
        bend = jnp.tanh(scale * (value + 0.044715 * (square * value)))
        rise = 0.5 * (1.0 + bend)
        slope = 0.5 * value * (1.0 - bend * bend) * (scale * (1.0 + 3 * 0.044715 * square))
        return value * rise, rise + slope

    kept, hidden_blocks, branch_parts = [], [], []
    normed_blocks = [normed_two]
    for number in range(nx * ny):
        if number == 1:
            normed_blocks = place.gather_far(near_blocks, hidden_blocks[0])
        block = normed_blocks[number]
        gate_pre, up_pre = matmul(block, gate_full), matmul(block, up_full)
        gelu, gelu_slope = gelu_parts(gate_pre)
        kept.append(((gelu_slope * up_pre).astype(BF), gelu.astype(BF)))
        hidden_blocks.append((gelu * up_pre).astype(BF))
        branch_parts.append(matmul(hidden_blocks[-1], down_full))
    branch = place.scatter_plane(branch_parts)
    factor_four = rms_factor(branch)
    layer_out = reorder((mixed + branch * factor_four * final_scale).astype(BF), to_outside)

    branch_grad, final_term = norm_back(out_grad, branch, factor_four, final_scale)
    branch_grad = branch_grad.astype(BF)
    near_blocks = place.gather_near(branch_grad)
    branch_grad_blocks = [branch_grad]
    gate_grads, up_grads, normed_two_parts = [], [], []
    for number, factors in enumerate(kept):
        if number == 1:
            branch_grad_blocks = place.gather_far(near_blocks, normed_two_parts[0])
        block = branch_grad_blocks[number]
        hidden_grad = matmul_nt(block, down_full)
        gate_grad, up_grad = ((hidden_grad * f.astype(F32)).astype(BF) for f in factors)
        gate_grads.append(gate_grad)
        up_grads.append(up_grad)
        normed_two_parts.append(matmul_nt(gate_grad, gate_full) + matmul_nt(up_grad, up_full))
    normed_two_grad = place.scatter_plane(normed_two_parts)
    halfway = place.halfway
    normed_all = jnp.concatenate(normed_blocks)
    hidden_all = jnp.concatenate(hidden_blocks)
    down_terms = matmul_tn(
        after(hidden_all, normed_two_parts[-1]), jnp.concatenate(branch_grad_blocks)
    ).astype(BF)
    gate_terms = matmul_tn(normed_all, after(jnp.concatenate(gate_grads), *halfway)).astype(BF)
    up_terms = matmul_tn(normed_all, after(jnp.concatenate(up_grads), *halfway)).astype(BF)
    normed_two_grad = after(normed_two_grad, gate_terms, up_terms)
    down_terms = place.cores_summed(down_terms)
    gate_terms = place.cores_summed(gate_terms)
    up_terms = place.cores_summed(up_terms)
    down_rows = place.scatter_line(down_terms)
    gate_rows = place.scatter_line(gate_terms)

    mixed_part, feed_term = norm_back(normed_two_grad, mixed, factor_two, feed_scale)
    mixed_grad = out_grad + mixed_part
    projected_grad, mixed_term = norm_back(mixed_grad, projected, factor_three, mixed_scale)
    projected_grad = projected_grad.astype(BF)
    output_terms = matmul_tn(attended, projected_grad).astype(BF)
    attended_grad = matmul_nt(projected_grad, output_full).astype(BF)
    attended_grad = after(attended_grad, gate_terms, up_terms)
    delta = jnp.stack(
        [
            jnp.sum(
                attended_grad[:, h * HD : (h + 1) * HD].astype(F32)
                * attended[:, h * HD : (h + 1) * HD].astype(F32),
                axis=1,
            )
            for h in range(HQ)
        ]
    ).reshape(1, -1)
    if together:
        queries_grad, key_value_grad = attend_back(
            sizes, queries, attended_grad, logs, delta, key_values, attention.marks
        )
    else:
        queries_grad, key_value_terms = attention.backward(
            queries, attended_grad, logs, delta, key_values
        )
        key_value_grad = place.scatter_group(key_value_terms)
    output_terms = after(output_terms, key_value_grad)
    up_rows = place.scatter_line(up_terms)
    down_weight_grad = matmul(down_rows, to_outside)

    def whole_rows(own_part):
        dealt = place.deal_plane(own_part.reshape(nx, ny, rows, part))
        dealt = dealt.reshape(nx, ny, rows, 2 * nw * nz, -1)
        return jnp.transpose(dealt, (2, 0, 3, 1, 4)).reshape(rows, FF).astype(F32)

    gate_weight_grad, up_weight_grad = whole_rows(gate_rows), whole_rows(up_rows)
    key_grad_rows = key_value_grad[:, :HD]
    values_grad = key_value_grad[:, HD:].astype(BF)
    key_back = rotate(key_grad_rows, cosine, -sine)
    key_in_grad, key_term = norm_back(key_back, key_raw, key_factor, key_scale)
    key_in_grad = key_in_grad.astype(BF)
    query_in_grad, query_term = [], 0.0
    for h in range(HQ):
        query_back = rotate(queries_grad[:, h * HD : (h + 1) * HD], cosine, -sine)
        grad, term = norm_back(query_back, query_raw[h], query_factor[h], query_scale)
        query_in_grad.append(grad.astype(BF))
        query_term = query_term + term
    quarter = HD // 2
    raw_grad = []
    for c in range(2):
        raw_grad.append(
            jnp.concatenate(
                query_in_grad[c * HQ // 2 : (c + 1) * HQ // 2]
                + [
                    key_in_grad[:, c * quarter : (c + 1) * quarter],
                    values_grad[:, c * quarter : (c + 1) * quarter],
                ],
                axis=1,
            )
        )
    def chip_order(values):
        values = values.reshape(nx, 2, nw, nz, ny, -1)
        return jnp.transpose(values, (0, 4, 2, 3, 1, 5)).reshape(chips, 2, -1)

    def chip_order_inside(values):
        values = values.reshape(2, nw, nz, nx, ny, rows)
        return jnp.transpose(values, (3, 4, 1, 2, 0, 5)).reshape(chips, 2, rows)

    gain_terms = jnp.concatenate(
        [chip_order_inside(t) for t in (mixed_term, feed_term, final_term)]
        + [chip_order(query_term), chip_order(key_term)],
        axis=2,
    )
    gain_terms = jnp.moveaxis(gain_terms, 1, 0).astype(BF)
    gain_terms = jnp.pad(
        gain_terms, ((0, 0), (0, 0), (0, gain_rows * head_width - gain_terms.shape[2]))
    ).reshape(2, chips, gain_rows, head_width)
    output_terms = output_terms.reshape(nx, 2, nw * nz, ny, -1, model)
    output_terms = jnp.transpose(output_terms, (1, 0, 3, 2, 4, 5)).reshape(2, chips, -1, head_width)
    grads_pair = jnp.stack(raw_grad)

    def terms_of(which):
        return jnp.concatenate(
            [
                matmul_tn(normed, pick(grads_pair, which)).astype(BF).reshape(chips, 2 * rows, head_width),
                pick(gain_terms, which),
                pick(output_terms, which),
            ],
            axis=1,
        ).reshape(-1, head_width)

    first_terms = terms_of(core).astype(F32) + place.swap_core(terms_of(1 - core)).astype(F32)
    first_terms = after(first_terms.astype(BF), gate_rows)
    normed_grad = 0.0
    for half, grad in zip(in_order(*projections), raw_grad):
        half = matmul(inside_from_first, half).astype(BF)
        normed_grad = normed_grad + matmul_nt(after(grad, first_terms), half)
    tokens_part, _ = norm_back(normed_grad, tokens_in, factor_one, gain_one)
    tokens_grad = reorder((mixed_grad + tokens_part).astype(BF), to_outside)

    first_grad = place.scatter_chips(first_terms, up_rows)
    projection_rows = first_grad[: 2 * rows].reshape(2, rows, head_width)
    projection_rows = cores_in_order(
        pick(projection_rows, core), place.swap_core(pick(projection_rows, 1 - core))
    )

    def whole_columns(a, b):
        return jnp.moveaxis(projection_rows[:, :, a:b], 0, 1).reshape(rows, -1)

    query_weight_grad = whole_columns(0, heads_half)
    key_weight_grad = whole_columns(heads_half, heads_half + quarter)
    value_weight_grad = whole_columns(heads_half + quarter, head_width)
    gain_grad = first_grad[2 * rows : 2 * rows + gain_rows].reshape(-1)
    (
        mixed_gain_grad,
        feed_gain_grad,
        final_gain_grad,
        query_gain_grad,
        key_gain_grad,
    ) = (gain_grad[a:b] for a, b in zip(spans[:5], spans[1:6]))
    attention_gain_grad = sum(
        jnp.sum(grad * weight.astype(F32), axis=1)
        for grad, weight in (
            (query_weight_grad, query_weight),
            (key_weight_grad, key_weight),
            (value_weight_grad, value_weight),
        )
    ) / attention_gain.astype(F32)
    output_weight_grad = reorder(first_grad[2 * rows + gain_rows :].reshape(-1, model), to_outside)
    return (
        layer_out,
        tokens_grad,
        attention_gain_grad,
        query_weight_grad,
        key_weight_grad,
        value_weight_grad,
        query_gain_grad,
        key_gain_grad,
        output_weight_grad,
        mixed_gain_grad,
        feed_gain_grad,
        gate_weight_grad,
        up_weight_grad,
        down_weight_grad,
        final_gain_grad,
    )


def solution(mesh):
    sizes = grid_of(mesh)
    grid = Mesh(mesh.devices.reshape(sizes), AXES)
    matrix, vector, group = P(AXES, None), P(AXES), P(("x", "core"))
    return jax.shard_map(
        lambda *arrays: body(sizes, *arrays),
        mesh=grid,
        in_specs=(
            matrix,
            vector,
            matrix,
            matrix,
            matrix,
            vector,
            vector,
            matrix,
            vector,
            vector,
            matrix,
            matrix,
            matrix,
            vector,
            group,
            group,
            matrix,
        ),
        out_specs=(
            matrix,
            matrix,
            vector,
            matrix,
            matrix,
            matrix,
            vector,
            vector,
            matrix,
            vector,
            vector,
            matrix,
            matrix,
            matrix,
            vector,
        ),
        check_vma=False,
    )
```

```python
import functools

import jax
import jax.numpy as jnp
import numpy as np
from jax import lax
from jax.experimental import pallas as pl
from jax.experimental.pallas import tpu as pltpu
from jax.sharding import Mesh, PartitionSpec as P

FF = 6912
HQ = 4
HD = 256
EPSILON = 1e-06
THETA = 1000000.0
BF = jnp.bfloat16
F32 = jnp.float32

AXES = ("x", "core", "w", "z", "y")
CTX_GRID = {8: (1, 4, 2), 32: (2, 4, 4)}


def grid_of(mesh):
    dp, ctx = mesh.shape["dp"], mesh.shape["ctx"]
    w, z, y = CTX_GRID.get(ctx, (1, ctx, 1))
    return (dp // 2, 2, w, z, y)


class Place:
    def __init__(self, sizes):
        self.size = dict(zip(AXES, sizes))
        self.at = {a: lax.axis_index(a) for a in AXES}

    def shift(self, value, axis, by):
        n = self.size[axis]
        return lax.ppermute(value, axis, [(i, (i + by) % n) for i in range(n)])

    def shift_wz(self, value, kw, kz):
        nw, nz = self.size["w"], self.size["z"]
        pairs = [
            (w * nz + z, ((w + kw) % nw) * nz + (z + kz) % nz) for w in range(nw) for z in range(nz)
        ]
        return lax.ppermute(value, ("w", "z"), pairs)

    def swap_core(self, value):
        return lax.ppermute(value, "core", [(0, 1), (1, 0)])

    def wz_steps(self):
        return [(kw, kz) for kw in range(self.size["w"]) for kz in range(self.size["z"])]

    def gather_wz(self, own):
        return [own if kw == kz == 0 else self.shift_wz(own, kw, kz) for kw, kz in self.wz_steps()]

    def gather_line(self, own):
        return lax.all_gather(own, ("core", "w", "z"), axis=0, tiled=True)

    def cores_summed(self, full):
        full = full.reshape(2, -1, full.shape[-1])
        give = self.swap_core(lax.dynamic_index_in_dim(full, 1 - self.at["core"], 0, keepdims=False))
        keep = lax.dynamic_index_in_dim(full, self.at["core"], 0, keepdims=False)
        return (keep.astype(F32) + give.astype(F32)).astype(BF)

    def scatter_line(self, rows):
        return lax.psum_scatter(rows, ("w", "z"), scatter_dimension=0, tiled=True)

    def plane_steps(self):
        return [(dx, dy) for dx in range(self.size["x"]) for dy in range(self.size["y"])]

    def gather_near(self, own):
        blocks = {(0, 0): own}
        for dx in range(1, self.size["x"]):
            blocks[dx, 0] = self.shift(own, "x", dx)
        for dy in range(1, self.size["y"]):
            blocks[0, dy] = self.shift(own, "y", dy)
        return blocks

    def gather_far(self, near, *hold):
        blocks = {step: after(block, *hold) if hold else block for step, block in near.items()}
        cut = blocks[0, 0].shape[0] // 2
        for dx, dy in self.plane_steps():
            if dx and dy:
                top = self.shift(blocks[dx, 0][:cut], "y", dy)
                low = self.shift(blocks[0, dy][cut:], "x", dx)
                blocks[dx, dy] = jnp.concatenate([top, low])
        return [blocks[step] for step in self.plane_steps()]

    def scatter_plane(self, parts):
        parts = dict(zip(self.plane_steps(), parts))
        cut = parts[0, 0].shape[0] // 2
        tops = {d: parts[d, 0][:cut] for d in range(self.size["x"])}
        lows = {d: parts[0, d][cut:] for d in range(self.size["y"])}
        own_top, own_low = parts[0, 0][:cut], parts[0, 0][cut:]
        for dx in range(1, self.size["x"]):
            own_low = own_low + self.shift(parts[dx, 0][cut:].astype(BF), "x", -dx).astype(F32)
        for dy in range(1, self.size["y"]):
            own_top = own_top + self.shift(parts[0, dy][:cut].astype(BF), "y", -dy).astype(F32)
        for dx, dy in self.plane_steps():
            if dx and dy:
                part = parts[dx, dy].astype(BF)
                tops[dx] = tops[dx] + self.shift(part[:cut], "y", -dy).astype(F32)
                lows[dy] = lows[dy] + self.shift(part[cut:], "x", -dx).astype(F32)
        self.halfway = [tops[self.size["x"] - 1], lows[self.size["y"] - 1]]
        for dx in range(1, self.size["x"]):
            own_top = own_top + self.shift(tops[dx].astype(BF), "x", -dx).astype(F32)
        for dy in range(1, self.size["y"]):
            own_low = own_low + self.shift(lows[dy].astype(BF), "y", -dy).astype(F32)
        return jnp.concatenate([own_top, own_low])

    def deal_plane(self, pieces, hold=(), hold_end=()):
        for dim, axis in ((0, "x"), (1, "y")):
            n, here = self.size[axis], self.at[axis]
            dealt = []
            for d in range(n):
                piece = lax.dynamic_index_in_dim(pieces, (here + d) % n, dim)
                dealt.append(piece if d == 0 else self.shift(piece, axis, d))
            wait_for = hold if axis == "x" else hold_end
            if wait_for:
                dealt = [after(piece, *wait_for) for piece in dealt]
            if n == 2:
                own, other = dealt
                low = jnp.where(here == 0, own, other)
                pieces = jnp.concatenate([low, jnp.where(here == 0, other, own)], axis=dim)
            else:
                pieces = jnp.zeros_like(pieces)
                for d in range(n):
                    pieces = lax.dynamic_update_slice_in_dim(pieces, dealt[d], (here - d) % n, dim)
        return pieces

    def ctx_chip(self, spot):
        return (spot["w"] * self.size["z"] + spot["z"]) * self.size["y"] + spot["y"]

    def gather_chips(self, own):
        size, at = self.size, self.at
        rows, width = own.shape
        line = size["w"] * size["z"] * rows
        mine = jnp.zeros((line, width), own.dtype)
        for block, (kw, kz) in zip(self.gather_wz(own), self.wz_steps()):
            w, z = (at["w"] - kw) % size["w"], (at["z"] - kz) % size["z"]
            mine = lax.dynamic_update_slice(mine, block, ((w * size["z"] + z) * rows, 0))
        full = jnp.zeros((size["x"] * size["y"] * line, width), own.dtype)
        near = self.gather_near(mine)
        for block, (dx, dy) in zip(self.gather_far(near), self.plane_steps()):
            x, y = (at["x"] - dx) % size["x"], (at["y"] - dy) % size["y"]
            full = lax.dynamic_update_slice(full, block, ((x * size["y"] + y) * line, 0))
        return full, mine, list(near.values())

    def scatter_chips(self, full):
        size, at = self.size, self.at
        full = full.reshape((size["x"], size["y"], -1, full.shape[-1]))
        parts = [
            full[(at["x"] - dx) % size["x"], (at["y"] - dy) % size["y"]].astype(F32)
            for dx, dy in self.plane_steps()
        ]
        mine = self.scatter_plane(parts)
        mine = mine.reshape((size["w"], size["z"], -1, mine.shape[-1]))
        total = None
        for kw, kz in reversed(self.wz_steps()):
            part = mine[(at["w"] + kw) % size["w"], (at["z"] + kz) % size["z"]]
            if kw or kz:
                part = self.shift_wz(part.astype(BF), kw, kz).astype(F32)
            total = part if total is None else total + part
        return total

    def gather_group(self, own):
        size, at = self.size, self.at
        rows = own.shape[0]
        full = jnp.zeros((size["w"] * size["z"] * size["y"] * rows, own.shape[1]), own.dtype)
        for kw, kz in self.wz_steps():
            block = own if kw == kz == 0 else self.shift_wz(own, kw, kz)
            spot = {"w": (at["w"] - kw) % size["w"], "z": (at["z"] - kz) % size["z"]}
            for ky in range(size["y"]):
                block_y = block if ky == 0 else self.shift(block, "y", ky)
                spot["y"] = (at["y"] - ky) % size["y"]
                full = lax.dynamic_update_slice(full, block_y, (self.ctx_chip(spot) * rows, 0))
        return full

    def scatter_group(self, full):
        size, at = self.size, self.at
        full = full.reshape((size["w"], size["z"], size["y"], -1, full.shape[-1]))
        total = None
        for kw, kz in reversed(self.wz_steps()):
            part = full[(at["w"] + kw) % size["w"], (at["z"] + kz) % size["z"]]
            acc = part[at["y"]].astype(F32)
            for dy in range(1, size["y"]):
                acc = acc + self.shift(part[(at["y"] + dy) % size["y"]], "y", dy).astype(F32)
            if kw or kz:
                acc = self.shift_wz(acc.astype(BF), kw, kz).astype(F32)
            total = acc if total is None else total + acc
        return total


def after(value, *others):
    return lax.optimization_barrier((value,) + others)[0]


def rms_factor(values):
    return lax.rsqrt(jnp.mean(values * values, axis=-1, keepdims=True) + EPSILON)


def norm_back(incoming, values, factor, gain):
    scaled = incoming * gain
    gain_term = jnp.sum((incoming * values * factor).reshape(-1, values.shape[-1]), axis=0)
    inner = jnp.mean(scaled * values, axis=-1, keepdims=True)
    return (factor * scaled - values * (factor * factor * factor) * inner, gain_term)


def angles_of(position_ids):
    half_width = HD // 2
    inverse = THETA ** (-(jnp.arange(half_width, dtype=F32) * 2.0) / HD)
    angle = position_ids.astype(F32)[:, None] * inverse[None, :]
    return (jnp.cos(angle), jnp.sin(angle))


def rotate(values, cosine, sine):
    half_width = values.shape[-1] // 2
    first_half = values[..., :half_width]
    second_half = values[..., half_width:]
    return jnp.concatenate(
        [first_half * cosine - second_half * sine, second_half * cosine + first_half * sine],
        axis=-1,
    )


def matmul(left, right):
    return jnp.dot(left, right, preferred_element_type=F32)


def matmul_nt(left, right):
    return jnp.einsum("ij,kj->ik", left, right, preferred_element_type=F32)


def matmul_tn(left, right):
    return jnp.einsum("ji,jk->ik", left, right, preferred_element_type=F32)


def allowed_pairs(key_pos, key_seg, query_pos, query_seg):
    return (key_pos <= query_pos) & ((key_seg == 0) | (key_seg == query_seg))


def forward_kernel(
    live, q_ref, kv_ref, key_pos, key_seg, query_pos, query_seg, out_ref, log_ref, acc, total
):
    block = pl.program_id(0)
    local = q_ref.shape[0]

    @pl.when(block == 0)
    def _():
        acc[...] = jnp.zeros_like(acc)
        total[...] = jnp.zeros_like(total)

    @pl.when(live[block] != 0)
    def _():
        keys = kv_ref[:, :HD]
        values_t = kv_ref[:, HD:].T
        allowed = allowed_pairs(key_pos[...], key_seg[...], query_pos[...], query_seg[...])
        for head in range(HQ):
            mine = pl.ds(head * local, local)
            scores = matmul_nt(keys, q_ref[:, head * HD : (head + 1) * HD]) * HD ** (-0.5)
            weights = jnp.where(allowed, jnp.exp(scores), 0.0)
            total[:, mine] += jnp.sum(weights, axis=0, keepdims=True)
            acc[:, mine] += matmul(values_t, weights.astype(BF))

    @pl.when(block == pl.num_programs(0) - 1)
    def _():
        for head in range(HQ):
            mine = pl.ds(head * local, local)
            out_ref[:, head * HD : (head + 1) * HD] = (acc[:, mine] / total[:, mine]).T.astype(BF)
        log_ref[...] = jnp.log(total[...])


def backward_kernel(
    live,
    q_ref,
    grad_ref,
    log_ref,
    delta_ref,
    kv_ref,
    key_pos,
    key_seg,
    query_pos,
    query_seg,
    q_grad_ref,
    kv_grad_ref,
    acc,
):
    block = pl.program_id(0)
    local = q_ref.shape[0]

    @pl.when(block == 0)
    def _():
        acc[...] = jnp.zeros_like(acc)

    @pl.when(live[block] == 0)
    def _():
        kv_grad_ref[...] = jnp.zeros_like(kv_grad_ref)

    @pl.when(live[block] != 0)
    def _():
        keys = kv_ref[:, :HD]
        keys_t = keys.T
        values = kv_ref[:, HD:]
        allowed = allowed_pairs(key_pos[...], key_seg[...], query_pos[...], query_seg[...])
        key_grad = jnp.zeros(keys.shape, F32)
        value_grad = jnp.zeros(keys.shape, F32)
        for head in range(HQ):
            mine = pl.ds(head * local, local)
            queries = q_ref[:, head * HD : (head + 1) * HD]
            grads = grad_ref[:, head * HD : (head + 1) * HD]
            scores = matmul_nt(keys, queries) * HD ** (-0.5)
            probs = jnp.where(allowed, jnp.exp(scores - log_ref[:, mine]), 0.0)
            prob_grad = matmul_nt(values, grads)
            score_grad = (probs * (prob_grad - delta_ref[:, mine]) * HD ** (-0.5)).astype(BF)
            value_grad += matmul(probs.astype(BF), grads)
            key_grad += matmul(score_grad, queries)
            acc[:, mine] += matmul(keys_t, score_grad)
        kv_grad_ref[:, :HD] = key_grad.astype(BF)
        kv_grad_ref[:, HD:] = value_grad.astype(BF)

    @pl.when(block == pl.num_programs(0) - 1)
    def _():
        for head in range(HQ):
            mine = pl.ds(head * local, local)
            q_grad_ref[:, head * HD : (head + 1) * HD] = acc[:, mine].T


class Ring:
    def __init__(self, sizes):
        _, _, self.nw, self.nz, self.ny = sizes
        self.line = self.nw * self.nz
        self.w, self.z, self.y = (lax.axis_index(a) for a in ("w", "z", "y"))

    def spot(self, k, ky):
        w = lax.rem(self.w + k // self.nz + self.nw, self.nw)
        z = lax.rem(self.z + k % self.nz + self.nz, self.nz)
        return w, z, lax.rem(self.y + ky + self.ny, self.ny)

    def device(self, k, ky):
        w, z, y = self.spot(k, ky)
        return {"w": w, "z": z, "y": y}

    def block(self, k, ky):
        w, z, y = self.spot(k, ky)
        return (w * self.nz + z) * self.ny + y

    def source(self, k, ky):
        w = lax.rem(self.w - k // self.nz + self.nw, self.nw)
        z = lax.rem(self.z - k % self.nz + self.nz, self.nz)
        return (w * self.nz + z) * self.ny + lax.rem(self.y - ky + self.ny, self.ny)

    def meet(self):
        barrier = pltpu.get_barrier_semaphore()
        peers = [(k, 0) for k in range(1, self.line)] + [(0, ky) for ky in range(1, self.ny)]
        for step in peers:
            pl.semaphore_signal(
                barrier, inc=1, device_id=self.device(*step), device_id_type=pl.DeviceIdType.MESH
            )
        pl.semaphore_wait(barrier, len(peers))

    def copy(self, source, target, sems, k, ky, to):
        send, recv = sems
        return pltpu.make_async_remote_copy(
            src_ref=source,
            dst_ref=target,
            send_sem=send.at[k, ky],
            recv_sem=recv.at[k, ky],
            device_id=self.device(*to),
            device_id_type=pl.DeviceIdType.MESH,
        )


def gather_attend_kernel(
    sizes,
    own_ref,
    raw_ref,
    gain_ref,
    cos_ref,
    sin_ref,
    key_pos,
    key_seg,
    query_pos,
    query_seg,
    all_ref,
    q_ref,
    out_ref,
    log_ref,
    held,
    acc,
    total,
    send_sem,
    recv_sem,
    out_sem,
):
    ring = Ring(sizes)
    local = own_ref.shape[0]
    sems = (send_sem, recv_sem)

    def rows(block):
        return pl.ds(pl.multiple_of(block * local, local), local)

    mine = held.at[rows(ring.block(0, 0)), :]
    ring.meet()
    for ky in range(1, ring.ny):
        ring.copy(own_ref, mine, sems, 0, ky, (0, ky)).start()
    for k in range(1, ring.line):
        ring.copy(own_ref, mine, sems, k, 0, (k, 0)).start()
    held[rows(ring.block(0, 0)), :] = own_ref[...]
    acc[...] = jnp.zeros_like(acc)
    total[...] = jnp.zeros_like(total)
    for head in range(HQ):
        raw = raw_ref[:, head * HD : (head + 1) * HD]
        scaled = raw * rms_factor(raw) * gain_ref[...]
        q_ref[:, head * HD : (head + 1) * HD] = rotate(scaled, cos_ref[...], sin_ref[...]).astype(BF)

    def attend(block):
        here = rows(block)
        keys = held[here, :HD]
        values_t = held[here, HD:].T
        allowed = allowed_pairs(key_pos[here, :], key_seg[here, :], query_pos[...], query_seg[...])
        for head in range(HQ):
            place = pl.ds(head * local, local)
            scores = matmul_nt(keys, q_ref[:, head * HD : (head + 1) * HD]) * HD ** (-0.5)
            weights = jnp.where(allowed, jnp.exp(scores), 0.0)
            total[:, place] += jnp.sum(weights, axis=0, keepdims=True)
            acc[:, place] += matmul(values_t, weights.astype(BF))

    def came(k, ky):
        piece = held.at[rows(ring.source(k, ky)), :]
        ring.copy(piece, piece, sems, k, ky, (k, ky)).wait_recv()

    @pl.loop(0, ring.ny)
    def _(ky):
        @pl.when(ky > 0)
        def _():
            came(0, ky)

        attend(ring.source(0, ky))

    @pl.loop(1, ring.line)
    def _(k):
        came(k, 0)
        piece = held.at[rows(ring.source(k, 0)), :]
        for ky in range(1, ring.ny):
            ring.copy(piece, piece, sems, k, ky, (0, ky)).start()
        attend(ring.source(k, 0))

    for ky in range(1, ring.ny):

        @pl.loop(1, ring.line)
        def _(k, ky=ky):
            came(k, ky)
            attend(ring.source(k, ky))

    keep = pltpu.make_async_copy(held, all_ref, out_sem)
    keep.start()
    for head in range(HQ):
        place = pl.ds(head * local, local)
        out_ref[:, head * HD : (head + 1) * HD] = (acc[:, place] / total[:, place]).T.astype(BF)
    log_ref[...] = jnp.log(total[...])
    for ky in range(1, ring.ny):
        ring.copy(own_ref, mine, sems, 0, ky, (0, ky)).wait_send()
    for k in range(1, ring.line):
        ring.copy(own_ref, mine, sems, k, 0, (k, 0)).wait_send()
        for ky in range(1, ring.ny):
            ring.copy(own_ref, mine, sems, k, ky, (0, ky)).wait_send()
    keep.wait()


def attend_back_kernel(
    sizes,
    q_ref,
    grad_ref,
    log_ref,
    delta_ref,
    all_ref,
    key_pos,
    key_seg,
    query_pos,
    query_seg,
    q_grad_ref,
    own_grad_ref,
    acc,
    term,
    from_y,
    on_z,
    from_z,
    send_y,
    recv_y,
    send_z,
    recv_z,
):
    ring = Ring(sizes)
    local = q_ref.shape[0]
    along_y, along_z = (send_y, recv_y), (send_z, recv_z)

    def to_y(k, ky):
        return ring.copy(term.at[k, ky], from_y.at[k, ky], along_y, k, ky, (0, ky))

    def to_z(k):
        return ring.copy(on_z.at[k], from_z.at[k], along_z, k, 0, (k, 0))

    def terms(block):
        here = pl.ds(pl.multiple_of(block * local, local), local)
        keys = all_ref[here, :HD]
        keys_t = keys.T
        values = all_ref[here, HD:]
        allowed = allowed_pairs(key_pos[here, :], key_seg[here, :], query_pos[...], query_seg[...])
        key_grad = jnp.zeros(keys.shape, F32)
        value_grad = jnp.zeros(keys.shape, F32)
        for head in range(HQ):
            place = pl.ds(head * local, local)
            queries = q_ref[:, head * HD : (head + 1) * HD]
            grads = grad_ref[:, head * HD : (head + 1) * HD]
            scores = matmul_nt(keys, queries) * HD ** (-0.5)
            probs = jnp.where(allowed, jnp.exp(scores - log_ref[:, place]), 0.0)
            prob_grad = matmul_nt(values, grads)
            score_grad = (probs * (prob_grad - delta_ref[:, place]) * HD ** (-0.5)).astype(BF)
            value_grad += matmul(probs.astype(BF), grads)
            key_grad += matmul(score_grad, queries)
            acc[:, place] += matmul(keys_t, score_grad)
        return key_grad, value_grad

    def keep(ref, pair):
        ref[:, :HD] = pair[0].astype(ref.dtype)
        ref[:, HD:] = pair[1].astype(ref.dtype)

    ring.meet()
    acc[...] = jnp.zeros_like(acc)
    for ky in range(1, ring.ny):

        @pl.loop(1, ring.line)
        def _(k, ky=ky):
            keep(term.at[k, ky], terms(ring.block(k, ky)))
            to_y(k, ky).start()

    @pl.loop(1, ring.line)
    def _(k):
        keep(own_grad_ref, terms(ring.block(k, 0)))
        for ky in range(1, ring.ny):
            to_y(k, ky).wait_recv()
            own_grad_ref[...] += from_y[k, ky].astype(F32)
        on_z[k] = own_grad_ref[...].astype(BF)
        to_z(k).start()

    @pl.loop(0, ring.ny)
    def _(step):
        ky = lax.rem(step + 1, ring.ny)
        pair = terms(ring.block(0, ky))

        @pl.when(ky > 0)
        def _():
            keep(term.at[0, ky], pair)
            to_y(0, ky).start()

        @pl.when(ky == 0)
        def _():
            keep(own_grad_ref, pair)

    for head in range(HQ):
        place = pl.ds(head * local, local)
        q_grad_ref[:, head * HD : (head + 1) * HD] = acc[:, place].T
    for ky in range(1, ring.ny):
        to_y(0, ky).wait_recv()
        own_grad_ref[...] += from_y[0, ky].astype(F32)
    for k in range(1, ring.line):
        to_z(k).wait_recv()
        own_grad_ref[...] += from_z[k].astype(F32)
        to_z(k).wait_send()
    for k in range(ring.line):
        for ky in range(1, ring.ny):
            to_y(k, ky).wait_send()


IN_VMEM = pl.BlockSpec(memory_space=pltpu.VMEM)


def kernel_settings(number):
    return dict(
        compiler_params=pltpu.CompilerParams(
            collective_id=number, has_side_effects=True, vmem_limit_bytes=56 << 20
        ),
        cost_estimate=pl.CostEstimate(
            flops=5 * 10**10, bytes_accessed=16 << 20, transcendentals=0
        ),
    )


def gather_attend(sizes, own, raw, gain, cosine, sine, marks):
    local, wide = raw.shape
    _, _, nw, nz, ny = sizes
    line = nw * nz
    full = jax.ShapeDtypeStruct((line * ny * local, own.shape[1]), BF)
    return pl.pallas_call(
        functools.partial(gather_attend_kernel, sizes),
        out_shape=(
            full,
            jax.ShapeDtypeStruct((local, wide), BF),
            jax.ShapeDtypeStruct((local, wide), BF),
            jax.ShapeDtypeStruct((1, HQ * local), F32),
        ),
        in_specs=[IN_VMEM] * 9,
        out_specs=(pl.BlockSpec(memory_space=pl.ANY), IN_VMEM, IN_VMEM, IN_VMEM),
        scratch_shapes=[
            pltpu.VMEM(full.shape, BF),
            pltpu.VMEM((HD, HQ * local), F32),
            pltpu.VMEM((1, HQ * local), F32),
            pltpu.SemaphoreType.DMA((line, ny)),
            pltpu.SemaphoreType.DMA((line, ny)),
            pltpu.SemaphoreType.DMA,
        ],
        **kernel_settings(0),
    )(own, raw, gain, cosine, sine, *marks)


def attend_back(sizes, queries, grads, logs, delta, key_values, marks):
    local, wide = queries.shape
    _, _, nw, nz, ny = sizes
    line = nw * nz
    width = key_values.shape[1]
    return pl.pallas_call(
        functools.partial(attend_back_kernel, sizes),
        out_shape=(
            jax.ShapeDtypeStruct((local, wide), F32),
            jax.ShapeDtypeStruct((local, width), F32),
        ),
        in_specs=[IN_VMEM] * 9,
        out_specs=(IN_VMEM, IN_VMEM),
        scratch_shapes=[
            pltpu.VMEM((HD, HQ * local), F32),
            pltpu.VMEM((line, ny, local, width), BF),
            pltpu.VMEM((line, ny, local, width), BF),
            pltpu.VMEM((line, local, width), BF),
            pltpu.VMEM((line, local, width), BF),
            pltpu.SemaphoreType.DMA((line, ny)),
            pltpu.SemaphoreType.DMA((line, ny)),
            pltpu.SemaphoreType.DMA((line, 1)),
            pltpu.SemaphoreType.DMA((line, 1)),
        ],
        **kernel_settings(1),
    )(queries, grads, logs, delta, key_values, *marks)


class Attention:
    def __init__(self, positions, segment_ids, query_pos, query_seg):
        local = query_pos.shape[0]
        self.local = local
        self.blocks = positions.shape[0] // local
        pos = positions.reshape(self.blocks, local)
        seg = segment_ids.reshape(self.blocks, local)
        seg_low, seg_high = jnp.min(seg, axis=1), jnp.max(seg, axis=1)
        late = jnp.min(pos, axis=1) > jnp.max(query_pos)
        foreign = (seg_low > 0) & (
            (seg_low > jnp.max(query_seg)) | (seg_high < jnp.min(query_seg))
        )
        self.live = jnp.where(late | foreign, 0, 1).astype(jnp.int32)
        self.marks = (
            positions.reshape(-1, 1),
            segment_ids.reshape(-1, 1),
            query_pos.reshape(1, -1),
            query_seg.reshape(1, -1),
        )

    def specs(self):
        local = self.local
        whole = lambda *shape: pl.BlockSpec(shape, lambda j, live: (0,) * len(shape))
        rows = lambda width: pl.BlockSpec((local, width), lambda j, live: (j, 0))
        marks = [rows(1), rows(1), whole(1, local), whole(1, local)]
        return whole, rows, marks

    def forward(self, queries, key_values):
        local, wide = queries.shape
        whole, rows, marks = self.specs()
        return pl.pallas_call(
            forward_kernel,
            out_shape=(
                jax.ShapeDtypeStruct((local, wide), BF),
                jax.ShapeDtypeStruct((1, HQ * local), F32),
            ),
            grid_spec=pltpu.PrefetchScalarGridSpec(
                num_scalar_prefetch=1,
                grid=(self.blocks,),
                in_specs=[whole(local, wide), rows(2 * HD)] + marks,
                out_specs=(whole(local, wide), whole(1, HQ * local)),
                scratch_shapes=[
                    pltpu.VMEM((HD, HQ * local), F32),
                    pltpu.VMEM((1, HQ * local), F32),
                ],
            ),
            cost_estimate=pl.CostEstimate(
                flops=20 * 4 * local * local * HD, bytes_accessed=8 << 20, transcendentals=0
            ),
        )(self.live, queries, key_values, *self.marks)

    def backward(self, queries, grads, logs, delta, key_values):
        local, wide = queries.shape
        whole, rows, marks = self.specs()
        return pl.pallas_call(
            backward_kernel,
            out_shape=(
                jax.ShapeDtypeStruct((local, wide), F32),
                jax.ShapeDtypeStruct(key_values.shape, BF),
            ),
            grid_spec=pltpu.PrefetchScalarGridSpec(
                num_scalar_prefetch=1,
                grid=(self.blocks,),
                in_specs=[
                    whole(local, wide),
                    whole(local, wide),
                    whole(1, HQ * local),
                    whole(1, HQ * local),
                    rows(2 * HD),
                ]
                + marks,
                out_specs=(whole(local, wide), rows(2 * HD)),
                scratch_shapes=[pltpu.VMEM((HD, HQ * local), F32)],
            ),
            cost_estimate=pl.CostEstimate(
                flops=20 * 10 * local * local * HD, bytes_accessed=16 << 20, transcendentals=0
            ),
        )(self.live, queries, grads, logs, delta, key_values, *self.marks)


def body(
    sizes,
    tokens,
    attention_gain,
    query_weight,
    key_weight,
    value_weight,
    query_gain,
    key_gain,
    output_weight,
    mixed_gain,
    feed_gain,
    gate_weight,
    up_weight,
    down_weight,
    final_gain,
    segment_ids,
    positions,
    cotangent,
):
    place = Place(sizes)
    nx, _, nw, nz, ny = sizes
    chips = nx * nw * nz * ny
    core = place.at["core"]
    local, model = tokens.shape
    rows = query_weight.shape[0]
    wide = HQ * HD
    offset = place.ctx_chip(place.at) * local
    query_pos = lax.dynamic_slice_in_dim(positions, offset, local)
    query_seg = lax.dynamic_slice_in_dim(segment_ids, offset, local)

    def pick(pair, which):
        return lax.dynamic_index_in_dim(pair, which, 0, keepdims=False)

    def cores_in_order(own, other):
        return jnp.where(core == 0, jnp.stack([own, other]), jnp.stack([other, own]))

    outside = np.arange(model).reshape(nx, 2, nw, nz, ny, rows)
    inside = outside.transpose(1, 2, 3, 0, 4, 5).reshape(-1)
    first = outside.transpose(0, 4, 2, 3, 1, 5).reshape(-1)

    def order_change(source, target):
        at = jnp.asarray(np.argsort(source)[target], jnp.int32)
        return (lax.iota(jnp.int32, model)[:, None] == at[None, :]).astype(BF)

    outside = np.arange(model)
    to_inside = order_change(outside, inside)
    to_outside = order_change(inside, outside)
    to_first = order_change(outside, first)
    inside_from_first = order_change(inside, first)

    def reorder(values, matrix):
        if values.dtype == F32:
            return jnp.dot(values, matrix.astype(F32), precision=lax.Precision.HIGHEST)
        return matmul(values, matrix).astype(BF)

    def column_halves(query, key, value):
        cut = lambda m: m.reshape(m.shape[0], 2, -1)
        halves = jnp.concatenate([cut(query), cut(key), cut(value)], axis=2)
        return jnp.moveaxis(halves, 1, 0)

    head_width = wide // 2 + HD
    gains = jnp.concatenate(
        [mixed_gain, feed_gain, final_gain, query_gain, key_gain, attention_gain]
    )
    gain_count = gains.size
    projections = column_halves(query_weight, key_weight, value_weight)
    gain_rows = -(-gain_count // head_width) * 8
    gain_block = jnp.zeros((gain_rows * head_width,), BF).at[:gain_count].set(gains)
    small = jnp.concatenate(
        [gain_block.reshape(gain_rows, head_width), reorder(output_weight, to_inside).reshape(-1, head_width)]
    )
    first_own = jnp.concatenate(
        [
            cores_in_order(pick(projections, core), place.swap_core(pick(projections, 1 - core))).reshape(
                2 * rows, head_width
            ),
            small,
        ]
    )
    first_all, first_came, next_came = place.gather_chips(first_own)

    gate_weight, up_weight, down_weight, tokens, cotangent, _ = lax.optimization_barrier(
        (gate_weight, up_weight, down_weight, tokens, cotangent, first_own)
    )
    part = FF // (nx * ny)
    gate_up = jnp.stack([gate_weight, up_weight]).reshape(2, rows, nx, 2 * nw * nz, ny, -1)
    gate_up = jnp.transpose(gate_up, (2, 4, 0, 1, 3, 5)).reshape(nx, ny, 2, rows, part)
    down_own = reorder(down_weight, to_inside)
    down_full = place.gather_line(down_own)
    first_other = place.swap_core(first_all)

    def in_order(own, other):
        return jnp.where(core == 0, own, other), jnp.where(core == 0, other, own)

    first_all, first_other = (
        block.reshape(chips, first_own.shape[0], head_width) for block in (first_all, first_other)
    )
    projections = tuple(
        block[:, : 2 * rows].reshape(model, head_width) for block in (first_all, first_other)
    )
    gains_all = jnp.stack(
        in_order(*(block[:, 2 * rows, :gain_count] for block in (first_all, first_other)))
    )
    gains_all = jnp.moveaxis(gains_all.astype(F32), 0, 1)
    spans = np.cumsum([0, rows, rows, rows, query_gain.size, key_gain.size, rows])
    mixed_scale, feed_scale, final_scale, query_scale, key_scale, gain_one = (
        gains_all[:, :, a:b] for a, b in zip(spans[:-1], spans[1:])
    )
    gain_first = gain_one.reshape(model)

    def inside_order(values):
        values = values.reshape(nx, ny, nw, nz, 2, rows)
        return jnp.transpose(values, (4, 2, 3, 0, 1, 5)).reshape(-1)

    gain_one, mixed_scale, feed_scale, final_scale = (
        inside_order(g) for g in (gain_one, mixed_scale, feed_scale, final_scale)
    )

    def true_order(values):
        values = values.reshape(nx, ny, nw, nz, 2, -1)
        return jnp.transpose(values, (0, 4, 2, 3, 1, 5)).reshape(-1)

    query_scale, key_scale = true_order(query_scale), true_order(key_scale)

    tokens_in = reorder(tokens, to_inside).astype(F32)
    tokens_first = reorder(tokens, to_first).astype(F32)
    out_grad = reorder(cotangent, to_inside).astype(F32)
    factor_one = rms_factor(tokens_in)
    normed = (tokens_first * factor_one * gain_first).astype(BF)
    raw = in_order(*(matmul(normed, half) for half in projections))
    heads_half = wide // 2

    def both_halves(at, width):
        return [half[:, at : at + width] for half in raw]

    query_raw = [
        piece[:, h * HD : (h + 1) * HD]
        for piece in both_halves(0, heads_half)
        for h in range(HQ // 2)
    ]
    key_raw = jnp.concatenate(both_halves(heads_half, HD // 2), axis=1)
    value_rows = jnp.concatenate(both_halves(heads_half + HD // 2, HD // 2), axis=1).astype(BF)
    cosine, sine = angles_of(query_pos)
    key_factor = rms_factor(key_raw)
    key_rows = rotate(key_raw * key_factor * key_scale, cosine, sine).astype(BF)
    own_key_values = jnp.concatenate([key_rows, value_rows], axis=1)
    gate_up = place.deal_plane(gate_up, [first_came], next_came + [own_key_values])
    gate_own, up_own = (gate_up[:, :, i].reshape(-1, part) for i in range(2))
    gate_full, up_full = place.gather_line(gate_own), place.gather_line(up_own)
    own_key_values = after(own_key_values, gate_own, up_own, down_full)
    attention = Attention(positions, segment_ids, query_pos, query_seg)
    together = nw * nz * ny <= 8
    if together:
        key_values, queries, attended, logs = gather_attend(
            sizes,
            own_key_values,
            jnp.concatenate(query_raw, axis=1),
            query_scale.reshape(1, -1),
            cosine,
            sine,
            attention.marks,
        )
    else:
        key_values = place.gather_group(own_key_values)
        queries = jnp.concatenate(
            [
                rotate(q * rms_factor(q) * query_scale, cosine, sine).astype(BF)
                for q in query_raw
            ],
            axis=1,
        )
        attended, logs = attention.forward(queries, key_values)
    query_factor = [rms_factor(q) for q in query_raw]
    first_all, first_other, projections, query_factor = lax.optimization_barrier(
        (first_all, first_other, projections, query_factor, attended)
    )[:4]
    output_full = jnp.stack(
        in_order(*(block[:, 2 * rows + gain_rows :] for block in (first_all, first_other)))
    )
    output_full = jnp.transpose(
        output_full.reshape(2, nx, ny, nw * nz, -1, model), (1, 0, 3, 2, 4, 5)
    ).reshape(wide, model)
    projected = matmul(attended, output_full)
    factor_three = rms_factor(projected)
    mixed = tokens_in + projected * factor_three * mixed_scale
    factor_two = rms_factor(mixed)
    normed_two = (mixed * factor_two * feed_scale).astype(BF)
    near_blocks = place.gather_near(normed_two)
    def gelu_parts(value):
        scale = (2.0 / np.pi) ** 0.5
        square = value * value
        bend = jnp.tanh(scale * (value + 0.044715 * (square * value)))
        rise = 0.5 * (1.0 + bend)
        slope = 0.5 * value * (1.0 - bend * bend) * (scale * (1.0 + 3 * 0.044715 * square))
        return value * rise, rise + slope

    kept, hidden_blocks, branch_parts = [], [], []
    normed_blocks = [normed_two]
    for number in range(nx * ny):
        if number == 1:
            normed_blocks = place.gather_far(near_blocks, hidden_blocks[0])
        block = normed_blocks[number]
        gate_pre, up_pre = matmul(block, gate_full), matmul(block, up_full)
        gelu, gelu_slope = gelu_parts(gate_pre)
        kept.append(((gelu_slope * up_pre).astype(BF), gelu.astype(BF)))
        hidden_blocks.append((gelu * up_pre).astype(BF))
        branch_parts.append(matmul(hidden_blocks[-1], down_full))
    branch = place.scatter_plane(branch_parts)
    factor_four = rms_factor(branch)
    layer_out = reorder((mixed + branch * factor_four * final_scale).astype(BF), to_outside)

    branch_grad, final_term = norm_back(out_grad, branch, factor_four, final_scale)
    branch_grad = branch_grad.astype(BF)
    near_blocks = place.gather_near(branch_grad)
    branch_grad_blocks = [branch_grad]
    gate_grads, up_grads, normed_two_parts = [], [], []
    for number, factors in enumerate(kept):
        if number == 1:
            branch_grad_blocks = place.gather_far(near_blocks, normed_two_parts[0])
        block = branch_grad_blocks[number]
        hidden_grad = matmul_nt(block, down_full)
        gate_grad, up_grad = ((hidden_grad * f.astype(F32)).astype(BF) for f in factors)
        gate_grads.append(gate_grad)
        up_grads.append(up_grad)
        normed_two_parts.append(matmul_nt(gate_grad, gate_full) + matmul_nt(up_grad, up_full))
    normed_two_grad = place.scatter_plane(normed_two_parts)
    halfway = place.halfway
    normed_all = jnp.concatenate(normed_blocks)
    hidden_all = jnp.concatenate(hidden_blocks)
    down_terms = matmul_tn(
        after(hidden_all, normed_two_parts[-1]), jnp.concatenate(branch_grad_blocks)
    ).astype(BF)
    gate_terms = matmul_tn(normed_all, after(jnp.concatenate(gate_grads), *halfway)).astype(BF)
    up_terms = matmul_tn(normed_all, after(jnp.concatenate(up_grads), *halfway)).astype(BF)
    normed_two_grad = after(normed_two_grad, gate_terms, up_terms)
    down_terms = place.cores_summed(down_terms)
    gate_terms = place.cores_summed(gate_terms)
    up_terms = place.cores_summed(up_terms)
    down_rows = place.scatter_line(down_terms)

    mixed_part, feed_term = norm_back(normed_two_grad, mixed, factor_two, feed_scale)
    mixed_grad = out_grad + mixed_part
    projected_grad, mixed_term = norm_back(mixed_grad, projected, factor_three, mixed_scale)
    projected_grad = projected_grad.astype(BF)
    output_terms = matmul_tn(attended, projected_grad).astype(BF)
    attended_grad = matmul_nt(projected_grad, output_full).astype(BF)
    attended_grad = after(attended_grad, down_terms)
    delta = jnp.stack(
        [
            jnp.sum(
                attended_grad[:, h * HD : (h + 1) * HD].astype(F32)
                * attended[:, h * HD : (h + 1) * HD].astype(F32),
                axis=1,
            )
            for h in range(HQ)
        ]
    ).reshape(1, -1)
    if together:
        queries_grad, key_value_grad = attend_back(
            sizes, queries, attended_grad, logs, delta, key_values, attention.marks
        )
    else:
        queries_grad, key_value_terms = attention.backward(
            queries, attended_grad, logs, delta, key_values
        )
        key_value_grad = place.scatter_group(key_value_terms)
    output_terms = after(output_terms, key_value_grad)
    share = gate_terms.shape[0] // (nw * nz)
    gate_up_terms = jnp.stack(
        [t.reshape(nw * nz, share, part) for t in (gate_terms, up_terms)], axis=1
    )
    gate_up_rows = place.scatter_line(after(gate_up_terms.reshape(-1, part), key_value_grad))
    key_value_grad = after(key_value_grad, down_rows)
    gate_rows, up_rows = gate_up_rows[:share], gate_up_rows[share:]
    down_weight_grad = matmul(down_rows, to_outside)

    def whole_rows(own_part):
        dealt = place.deal_plane(own_part.reshape(nx, ny, rows, part))
        dealt = dealt.reshape(nx, ny, rows, 2 * nw * nz, -1)
        return jnp.transpose(dealt, (2, 0, 3, 1, 4)).reshape(rows, FF).astype(F32)

    gate_weight_grad, up_weight_grad = whole_rows(gate_rows), whole_rows(up_rows)
    key_grad_rows = key_value_grad[:, :HD]
    values_grad = key_value_grad[:, HD:].astype(BF)
    key_back = rotate(key_grad_rows, cosine, -sine)
    key_in_grad, key_term = norm_back(key_back, key_raw, key_factor, key_scale)
    key_in_grad = key_in_grad.astype(BF)
    query_in_grad, query_term = [], 0.0
    for h in range(HQ):
        query_back = rotate(queries_grad[:, h * HD : (h + 1) * HD], cosine, -sine)
        grad, term = norm_back(query_back, query_raw[h], query_factor[h], query_scale)
        query_in_grad.append(grad.astype(BF))
        query_term = query_term + term
    quarter = HD // 2
    raw_grad = []
    for c in range(2):
        raw_grad.append(
            jnp.concatenate(
                query_in_grad[c * HQ // 2 : (c + 1) * HQ // 2]
                + [
                    key_in_grad[:, c * quarter : (c + 1) * quarter],
                    values_grad[:, c * quarter : (c + 1) * quarter],
                ],
                axis=1,
            )
        )
    def chip_order(values):
        values = values.reshape(nx, 2, nw, nz, ny, -1)
        return jnp.transpose(values, (0, 4, 2, 3, 1, 5)).reshape(chips, 2, -1)

    def chip_order_inside(values):
        values = values.reshape(2, nw, nz, nx, ny, rows)
        return jnp.transpose(values, (3, 4, 1, 2, 0, 5)).reshape(chips, 2, rows)

    gain_terms = jnp.concatenate(
        [chip_order_inside(t) for t in (mixed_term, feed_term, final_term)]
        + [chip_order(query_term), chip_order(key_term)],
        axis=2,
    )
    gain_terms = jnp.moveaxis(gain_terms, 1, 0).astype(BF)
    gain_terms = jnp.pad(
        gain_terms, ((0, 0), (0, 0), (0, gain_rows * head_width - gain_terms.shape[2]))
    ).reshape(2, chips, gain_rows, head_width)
    output_terms = output_terms.reshape(nx, 2, nw * nz, ny, -1, model)
    output_terms = jnp.transpose(output_terms, (1, 0, 3, 2, 4, 5)).reshape(2, chips, -1, head_width)
    grads_pair = jnp.stack(raw_grad)

    def terms_of(which):
        return jnp.concatenate(
            [
                matmul_tn(normed, pick(grads_pair, which)).astype(BF).reshape(chips, 2 * rows, head_width),
                pick(gain_terms, which),
                pick(output_terms, which),
            ],
            axis=1,
        ).reshape(-1, head_width)

    first_terms = terms_of(core).astype(F32) + place.swap_core(terms_of(1 - core)).astype(F32)
    first_terms = first_terms.astype(BF)
    normed_grad = 0.0
    for half, grad in zip(in_order(*projections), raw_grad):
        half = matmul(inside_from_first, half).astype(BF)
        normed_grad = normed_grad + matmul_nt(after(grad, first_terms), half)
    tokens_part, _ = norm_back(normed_grad, tokens_in, factor_one, gain_one)
    tokens_grad = reorder((mixed_grad + tokens_part).astype(BF), to_outside)

    first_grad = place.scatter_chips(first_terms)
    projection_rows = first_grad[: 2 * rows].reshape(2, rows, head_width)
    projection_rows = cores_in_order(
        pick(projection_rows, core), place.swap_core(pick(projection_rows, 1 - core))
    )

    def whole_columns(a, b):
        return jnp.moveaxis(projection_rows[:, :, a:b], 0, 1).reshape(rows, -1)

    query_weight_grad = whole_columns(0, heads_half)
    key_weight_grad = whole_columns(heads_half, heads_half + quarter)
    value_weight_grad = whole_columns(heads_half + quarter, head_width)
    gain_grad = first_grad[2 * rows : 2 * rows + gain_rows].reshape(-1)
    (
        mixed_gain_grad,
        feed_gain_grad,
        final_gain_grad,
        query_gain_grad,
        key_gain_grad,
    ) = (gain_grad[a:b] for a, b in zip(spans[:5], spans[1:6]))
    attention_gain_grad = sum(
        jnp.sum(grad * weight.astype(F32), axis=1)
        for grad, weight in (
            (query_weight_grad, query_weight),
            (key_weight_grad, key_weight),
            (value_weight_grad, value_weight),
        )
    ) / attention_gain.astype(F32)
    output_weight_grad = reorder(first_grad[2 * rows + gain_rows :].reshape(-1, model), to_outside)
    return (
        layer_out,
        tokens_grad,
        attention_gain_grad,
        query_weight_grad,
        key_weight_grad,
        value_weight_grad,
        query_gain_grad,
        key_gain_grad,
        output_weight_grad,
        mixed_gain_grad,
        feed_gain_grad,
        gate_weight_grad,
        up_weight_grad,
        down_weight_grad,
        final_gain_grad,
    )


def solution(mesh):
    sizes = grid_of(mesh)
    grid = Mesh(mesh.devices.reshape(sizes), AXES)
    matrix, vector, group = P(AXES, None), P(AXES), P(("x", "core"))
    return jax.shard_map(
        lambda *arrays: body(sizes, *arrays),
        mesh=grid,
        in_specs=(
            matrix,
            vector,
            matrix,
            matrix,
            matrix,
            vector,
            vector,
            matrix,
            vector,
            vector,
            matrix,
            matrix,
            matrix,
            vector,
            group,
            group,
            matrix,
        ),
        out_specs=(
            matrix,
            matrix,
            vector,
            matrix,
            matrix,
            matrix,
            vector,
            vector,
            matrix,
            vector,
            vector,
            matrix,
            matrix,
            matrix,
            vector,
        ),
        check_vma=False,
    )
```

```python
import functools

import jax
import jax.numpy as jnp
import numpy as np
from jax import lax
from jax.experimental import pallas as pl
from jax.experimental.pallas import tpu as pltpu
from jax.sharding import Mesh, PartitionSpec as P

FF = 6912
HQ = 4
HD = 256
EPSILON = 1e-06
THETA = 1000000.0
BF = jnp.bfloat16
F32 = jnp.float32

AXES = ("x", "core", "w", "z", "y")
CTX_GRID = {8: (1, 4, 2), 32: (2, 4, 4)}


def grid_of(mesh):
    dp, ctx = mesh.shape["dp"], mesh.shape["ctx"]
    w, z, y = CTX_GRID.get(ctx, (1, ctx, 1))
    return (dp // 2, 2, w, z, y)


class Place:
    def __init__(self, sizes):
        self.size = dict(zip(AXES, sizes))
        self.at = {a: lax.axis_index(a) for a in AXES}

    def shift(self, value, axis, by):
        n = self.size[axis]
        return lax.ppermute(value, axis, [(i, (i + by) % n) for i in range(n)])

    def shift_wz(self, value, kw, kz):
        nw, nz = self.size["w"], self.size["z"]
        pairs = [
            (w * nz + z, ((w + kw) % nw) * nz + (z + kz) % nz) for w in range(nw) for z in range(nz)
        ]
        return lax.ppermute(value, ("w", "z"), pairs)

    def swap_core(self, value):
        return lax.ppermute(value, "core", [(0, 1), (1, 0)])

    def wz_steps(self):
        return [(kw, kz) for kw in range(self.size["w"]) for kz in range(self.size["z"])]

    def gather_wz(self, own):
        return [own if kw == kz == 0 else self.shift_wz(own, kw, kz) for kw, kz in self.wz_steps()]

    def gather_line(self, own):
        return lax.all_gather(own, ("core", "w", "z"), axis=0, tiled=True)

    def cores_summed(self, full):
        full = full.reshape(2, -1, full.shape[-1])
        give = self.swap_core(lax.dynamic_index_in_dim(full, 1 - self.at["core"], 0, keepdims=False))
        keep = lax.dynamic_index_in_dim(full, self.at["core"], 0, keepdims=False)
        return (keep.astype(F32) + give.astype(F32)).astype(BF)

    def scatter_line(self, rows):
        return lax.psum_scatter(rows, ("w", "z"), scatter_dimension=0, tiled=True)

    def plane_steps(self):
        return [(dx, dy) for dx in range(self.size["x"]) for dy in range(self.size["y"])]

    def gather_near(self, own):
        blocks = {(0, 0): own}
        for dx in range(1, self.size["x"]):
            blocks[dx, 0] = self.shift(own, "x", dx)
        for dy in range(1, self.size["y"]):
            blocks[0, dy] = self.shift(own, "y", dy)
        return blocks

    def gather_far(self, near, *hold):
        blocks = {step: after(block, *hold) if hold else block for step, block in near.items()}
        cut = blocks[0, 0].shape[0] // 2
        for dx, dy in self.plane_steps():
            if dx and dy:
                top = self.shift(blocks[dx, 0][:cut], "y", dy)
                low = self.shift(blocks[0, dy][cut:], "x", dx)
                blocks[dx, dy] = jnp.concatenate([top, low])
        return [blocks[step] for step in self.plane_steps()]

    def scatter_plane(self, parts):
        parts = dict(zip(self.plane_steps(), parts))
        cut = parts[0, 0].shape[0] // 2
        tops = {d: parts[d, 0][:cut] for d in range(self.size["x"])}
        lows = {d: parts[0, d][cut:] for d in range(self.size["y"])}
        own_top, own_low = parts[0, 0][:cut], parts[0, 0][cut:]
        for dx in range(1, self.size["x"]):
            own_low = own_low + self.shift(parts[dx, 0][cut:].astype(BF), "x", -dx).astype(F32)
        for dy in range(1, self.size["y"]):
            own_top = own_top + self.shift(parts[0, dy][:cut].astype(BF), "y", -dy).astype(F32)
        for dx, dy in self.plane_steps():
            if dx and dy:
                part = parts[dx, dy].astype(BF)
                tops[dx] = tops[dx] + self.shift(part[:cut], "y", -dy).astype(F32)
                lows[dy] = lows[dy] + self.shift(part[cut:], "x", -dx).astype(F32)
        self.halfway = [tops[self.size["x"] - 1], lows[self.size["y"] - 1]]
        for dx in range(1, self.size["x"]):
            own_top = own_top + self.shift(tops[dx].astype(BF), "x", -dx).astype(F32)
        for dy in range(1, self.size["y"]):
            own_low = own_low + self.shift(lows[dy].astype(BF), "y", -dy).astype(F32)
        return jnp.concatenate([own_top, own_low])

    def deal_plane(self, pieces, hold=(), hold_end=()):
        for dim, axis in ((0, "x"), (1, "y")):
            n, here = self.size[axis], self.at[axis]
            dealt = []
            for d in range(n):
                piece = lax.dynamic_index_in_dim(pieces, (here + d) % n, dim)
                dealt.append(piece if d == 0 else self.shift(piece, axis, d))
            wait_for = hold if axis == "x" else hold_end
            if wait_for:
                dealt = [after(piece, *wait_for) for piece in dealt]
            if n == 2:
                own, other = dealt
                low = jnp.where(here == 0, own, other)
                pieces = jnp.concatenate([low, jnp.where(here == 0, other, own)], axis=dim)
            else:
                pieces = jnp.zeros_like(pieces)
                for d in range(n):
                    pieces = lax.dynamic_update_slice_in_dim(pieces, dealt[d], (here - d) % n, dim)
        return pieces

    def ctx_chip(self, spot):
        return (spot["w"] * self.size["z"] + spot["z"]) * self.size["y"] + spot["y"]

    def gather_chips(self, own):
        size, at = self.size, self.at
        rows, width = own.shape
        line = size["w"] * size["z"] * rows
        mine = jnp.zeros((line, width), own.dtype)
        for block, (kw, kz) in zip(self.gather_wz(own), self.wz_steps()):
            w, z = (at["w"] - kw) % size["w"], (at["z"] - kz) % size["z"]
            mine = lax.dynamic_update_slice(mine, block, ((w * size["z"] + z) * rows, 0))
        full = jnp.zeros((size["x"] * size["y"] * line, width), own.dtype)
        near = self.gather_near(mine)
        for block, (dx, dy) in zip(self.gather_far(near), self.plane_steps()):
            x, y = (at["x"] - dx) % size["x"], (at["y"] - dy) % size["y"]
            full = lax.dynamic_update_slice(full, block, ((x * size["y"] + y) * line, 0))
        return full, mine, list(near.values())

    def scatter_chips(self, full):
        size, at = self.size, self.at
        full = full.reshape((size["x"], size["y"], -1, full.shape[-1]))
        parts = [
            full[(at["x"] - dx) % size["x"], (at["y"] - dy) % size["y"]].astype(F32)
            for dx, dy in self.plane_steps()
        ]
        mine = self.scatter_plane(parts)
        mine = mine.reshape((size["w"], size["z"], -1, mine.shape[-1]))
        total = None
        for kw, kz in reversed(self.wz_steps()):
            part = mine[(at["w"] + kw) % size["w"], (at["z"] + kz) % size["z"]]
            if kw or kz:
                part = self.shift_wz(part.astype(BF), kw, kz).astype(F32)
            total = part if total is None else total + part
        return total

    def gather_group(self, own):
        size, at = self.size, self.at
        rows = own.shape[0]
        full = jnp.zeros((size["w"] * size["z"] * size["y"] * rows, own.shape[1]), own.dtype)
        for kw, kz in self.wz_steps():
            block = own if kw == kz == 0 else self.shift_wz(own, kw, kz)
            spot = {"w": (at["w"] - kw) % size["w"], "z": (at["z"] - kz) % size["z"]}
            for ky in range(size["y"]):
                block_y = block if ky == 0 else self.shift(block, "y", ky)
                spot["y"] = (at["y"] - ky) % size["y"]
                full = lax.dynamic_update_slice(full, block_y, (self.ctx_chip(spot) * rows, 0))
        return full

    def scatter_group(self, full):
        size, at = self.size, self.at
        full = full.reshape((size["w"], size["z"], size["y"], -1, full.shape[-1]))
        total = None
        for kw, kz in reversed(self.wz_steps()):
            part = full[(at["w"] + kw) % size["w"], (at["z"] + kz) % size["z"]]
            acc = part[at["y"]].astype(F32)
            for dy in range(1, size["y"]):
                acc = acc + self.shift(part[(at["y"] + dy) % size["y"]], "y", dy).astype(F32)
            if kw or kz:
                acc = self.shift_wz(acc.astype(BF), kw, kz).astype(F32)
            total = acc if total is None else total + acc
        return total


def after(value, *others):
    return lax.optimization_barrier((value,) + others)[0]


def rms_factor(values):
    return lax.rsqrt(jnp.mean(values * values, axis=-1, keepdims=True) + EPSILON)


def norm_back(incoming, values, factor, gain):
    scaled = incoming * gain
    gain_term = jnp.sum((incoming * values * factor).reshape(-1, values.shape[-1]), axis=0)
    inner = jnp.mean(scaled * values, axis=-1, keepdims=True)
    return (factor * scaled - values * (factor * factor * factor) * inner, gain_term)


def angles_of(position_ids):
    half_width = HD // 2
    inverse = THETA ** (-(jnp.arange(half_width, dtype=F32) * 2.0) / HD)
    angle = position_ids.astype(F32)[:, None] * inverse[None, :]
    return (jnp.cos(angle), jnp.sin(angle))


def rotate(values, cosine, sine):
    half_width = values.shape[-1] // 2
    first_half = values[..., :half_width]
    second_half = values[..., half_width:]
    return jnp.concatenate(
        [first_half * cosine - second_half * sine, second_half * cosine + first_half * sine],
        axis=-1,
    )


def matmul(left, right):
    return jnp.dot(left, right, preferred_element_type=F32)


def matmul_nt(left, right):
    return jnp.einsum("ij,kj->ik", left, right, preferred_element_type=F32)


def matmul_tn(left, right):
    return jnp.einsum("ji,jk->ik", left, right, preferred_element_type=F32)


def allowed_pairs(key_pos, key_seg, query_pos, query_seg):
    return (key_pos <= query_pos) & ((key_seg == 0) | (key_seg == query_seg))


def forward_kernel(
    live, q_ref, kv_ref, key_pos, key_seg, query_pos, query_seg, out_ref, log_ref, acc, total
):
    block = pl.program_id(0)
    local = q_ref.shape[0]

    @pl.when(block == 0)
    def _():
        acc[...] = jnp.zeros_like(acc)
        total[...] = jnp.zeros_like(total)

    @pl.when(live[block] != 0)
    def _():
        keys = kv_ref[:, :HD]
        values_t = kv_ref[:, HD:].T
        allowed = allowed_pairs(key_pos[...], key_seg[...], query_pos[...], query_seg[...])
        for head in range(HQ):
            mine = pl.ds(head * local, local)
            scores = matmul_nt(keys, q_ref[:, head * HD : (head + 1) * HD]) * HD ** (-0.5)
            weights = jnp.where(allowed, jnp.exp(scores), 0.0)
            total[:, mine] += jnp.sum(weights, axis=0, keepdims=True)
            acc[:, mine] += matmul(values_t, weights.astype(BF))

    @pl.when(block == pl.num_programs(0) - 1)
    def _():
        for head in range(HQ):
            mine = pl.ds(head * local, local)
            out_ref[:, head * HD : (head + 1) * HD] = (acc[:, mine] / total[:, mine]).T.astype(BF)
        log_ref[...] = jnp.log(total[...])


def backward_kernel(
    live,
    q_ref,
    grad_ref,
    log_ref,
    delta_ref,
    kv_ref,
    key_pos,
    key_seg,
    query_pos,
    query_seg,
    q_grad_ref,
    kv_grad_ref,
    acc,
):
    block = pl.program_id(0)
    local = q_ref.shape[0]

    @pl.when(block == 0)
    def _():
        acc[...] = jnp.zeros_like(acc)

    @pl.when(live[block] == 0)
    def _():
        kv_grad_ref[...] = jnp.zeros_like(kv_grad_ref)

    @pl.when(live[block] != 0)
    def _():
        keys = kv_ref[:, :HD]
        keys_t = keys.T
        values = kv_ref[:, HD:]
        allowed = allowed_pairs(key_pos[...], key_seg[...], query_pos[...], query_seg[...])
        key_grad = jnp.zeros(keys.shape, F32)
        value_grad = jnp.zeros(keys.shape, F32)
        for head in range(HQ):
            mine = pl.ds(head * local, local)
            queries = q_ref[:, head * HD : (head + 1) * HD]
            grads = grad_ref[:, head * HD : (head + 1) * HD]
            scores = matmul_nt(keys, queries) * HD ** (-0.5)
            probs = jnp.where(allowed, jnp.exp(scores - log_ref[:, mine]), 0.0)
            prob_grad = matmul_nt(values, grads)
            score_grad = (probs * (prob_grad - delta_ref[:, mine]) * HD ** (-0.5)).astype(BF)
            value_grad += matmul(probs.astype(BF), grads)
            key_grad += matmul(score_grad, queries)
            acc[:, mine] += matmul(keys_t, score_grad)
        kv_grad_ref[:, :HD] = key_grad.astype(BF)
        kv_grad_ref[:, HD:] = value_grad.astype(BF)

    @pl.when(block == pl.num_programs(0) - 1)
    def _():
        for head in range(HQ):
            mine = pl.ds(head * local, local)
            q_grad_ref[:, head * HD : (head + 1) * HD] = acc[:, mine].T


class Ring:
    def __init__(self, sizes):
        _, _, self.nw, self.nz, self.ny = sizes
        self.line = self.nw * self.nz
        self.w, self.z, self.y = (lax.axis_index(a) for a in ("w", "z", "y"))

    def spot(self, k, ky):
        w = lax.rem(self.w + k // self.nz + self.nw, self.nw)
        z = lax.rem(self.z + k % self.nz + self.nz, self.nz)
        return w, z, lax.rem(self.y + ky + self.ny, self.ny)

    def device(self, k, ky):
        w, z, y = self.spot(k, ky)
        return {"w": w, "z": z, "y": y}

    def block(self, k, ky):
        w, z, y = self.spot(k, ky)
        return (w * self.nz + z) * self.ny + y

    def source(self, k, ky):
        w = lax.rem(self.w - k // self.nz + self.nw, self.nw)
        z = lax.rem(self.z - k % self.nz + self.nz, self.nz)
        return (w * self.nz + z) * self.ny + lax.rem(self.y - ky + self.ny, self.ny)

    def meet(self):
        barrier = pltpu.get_barrier_semaphore()
        peers = [(k, 0) for k in range(1, self.line)] + [(0, ky) for ky in range(1, self.ny)]
        for step in peers:
            pl.semaphore_signal(
                barrier, inc=1, device_id=self.device(*step), device_id_type=pl.DeviceIdType.MESH
            )
        pl.semaphore_wait(barrier, len(peers))

    def copy(self, source, target, sems, k, ky, to):
        send, recv = sems
        return pltpu.make_async_remote_copy(
            src_ref=source,
            dst_ref=target,
            send_sem=send.at[k, ky],
            recv_sem=recv.at[k, ky],
            device_id=self.device(*to),
            device_id_type=pl.DeviceIdType.MESH,
        )


def gather_attend_kernel(
    sizes,
    own_ref,
    raw_ref,
    gain_ref,
    cos_ref,
    sin_ref,
    key_pos,
    key_seg,
    query_pos,
    query_seg,
    all_ref,
    q_ref,
    out_ref,
    log_ref,
    held,
    acc,
    total,
    send_sem,
    recv_sem,
    out_sem,
):
    ring = Ring(sizes)
    local = own_ref.shape[0]
    sems = (send_sem, recv_sem)

    def rows(block):
        return pl.ds(pl.multiple_of(block * local, local), local)

    mine = held.at[rows(ring.block(0, 0)), :]
    ring.meet()
    for ky in range(1, ring.ny):
        ring.copy(own_ref, mine, sems, 0, ky, (0, ky)).start()
    for k in range(1, ring.line):
        ring.copy(own_ref, mine, sems, k, 0, (k, 0)).start()
    held[rows(ring.block(0, 0)), :] = own_ref[...]
    acc[...] = jnp.zeros_like(acc)
    total[...] = jnp.zeros_like(total)
    for head in range(HQ):
        raw = raw_ref[:, head * HD : (head + 1) * HD]
        scaled = raw * rms_factor(raw) * gain_ref[...]
        q_ref[:, head * HD : (head + 1) * HD] = rotate(scaled, cos_ref[...], sin_ref[...]).astype(BF)

    def attend(block):
        here = rows(block)
        keys = held[here, :HD]
        values_t = held[here, HD:].T
        allowed = allowed_pairs(key_pos[here, :], key_seg[here, :], query_pos[...], query_seg[...])
        for head in range(HQ):
            place = pl.ds(head * local, local)
            scores = matmul_nt(keys, q_ref[:, head * HD : (head + 1) * HD]) * HD ** (-0.5)
            weights = jnp.where(allowed, jnp.exp(scores), 0.0)
            total[:, place] += jnp.sum(weights, axis=0, keepdims=True)
            acc[:, place] += matmul(values_t, weights.astype(BF))

    def came(k, ky):
        piece = held.at[rows(ring.source(k, ky)), :]
        ring.copy(piece, piece, sems, k, ky, (k, ky)).wait_recv()

    @pl.loop(0, ring.ny)
    def _(ky):
        @pl.when(ky > 0)
        def _():
            came(0, ky)

        attend(ring.source(0, ky))

    @pl.loop(1, ring.line)
    def _(k):
        came(k, 0)
        piece = held.at[rows(ring.source(k, 0)), :]
        for ky in range(1, ring.ny):
            ring.copy(piece, piece, sems, k, ky, (0, ky)).start()
        attend(ring.source(k, 0))

    for ky in range(1, ring.ny):

        @pl.loop(1, ring.line)
        def _(k, ky=ky):
            came(k, ky)
            attend(ring.source(k, ky))

    keep = pltpu.make_async_copy(held, all_ref, out_sem)
    keep.start()
    for head in range(HQ):
        place = pl.ds(head * local, local)
        out_ref[:, head * HD : (head + 1) * HD] = (acc[:, place] / total[:, place]).T.astype(BF)
    log_ref[...] = jnp.log(total[...])
    for ky in range(1, ring.ny):
        ring.copy(own_ref, mine, sems, 0, ky, (0, ky)).wait_send()
    for k in range(1, ring.line):
        ring.copy(own_ref, mine, sems, k, 0, (k, 0)).wait_send()
        for ky in range(1, ring.ny):
            ring.copy(own_ref, mine, sems, k, ky, (0, ky)).wait_send()
    keep.wait()


def attend_back_kernel(
    sizes,
    q_ref,
    grad_ref,
    log_ref,
    delta_ref,
    all_ref,
    key_pos,
    key_seg,
    query_pos,
    query_seg,
    q_grad_ref,
    own_grad_ref,
    acc,
    term,
    from_y,
    on_z,
    from_z,
    send_y,
    recv_y,
    send_z,
    recv_z,
):
    ring = Ring(sizes)
    local = q_ref.shape[0]
    along_y, along_z = (send_y, recv_y), (send_z, recv_z)

    def to_y(k, ky):
        return ring.copy(term.at[k, ky], from_y.at[k, ky], along_y, k, ky, (0, ky))

    def to_z(k):
        return ring.copy(on_z.at[k], from_z.at[k], along_z, k, 0, (k, 0))

    def terms(block):
        here = pl.ds(pl.multiple_of(block * local, local), local)
        keys = all_ref[here, :HD]
        keys_t = keys.T
        values = all_ref[here, HD:]
        allowed = allowed_pairs(key_pos[here, :], key_seg[here, :], query_pos[...], query_seg[...])
        key_grad = jnp.zeros(keys.shape, F32)
        value_grad = jnp.zeros(keys.shape, F32)
        for head in range(HQ):
            place = pl.ds(head * local, local)
            queries = q_ref[:, head * HD : (head + 1) * HD]
            grads = grad_ref[:, head * HD : (head + 1) * HD]
            scores = matmul_nt(keys, queries) * HD ** (-0.5)
            probs = jnp.where(allowed, jnp.exp(scores - log_ref[:, place]), 0.0)
            prob_grad = matmul_nt(values, grads)
            score_grad = (probs * (prob_grad - delta_ref[:, place]) * HD ** (-0.5)).astype(BF)
            value_grad += matmul(probs.astype(BF), grads)
            key_grad += matmul(score_grad, queries)
            acc[:, place] += matmul(keys_t, score_grad)
        return key_grad, value_grad

    def keep(ref, pair):
        ref[:, :HD] = pair[0].astype(ref.dtype)
        ref[:, HD:] = pair[1].astype(ref.dtype)

    ring.meet()
    acc[...] = jnp.zeros_like(acc)
    for ky in range(1, ring.ny):

        @pl.loop(1, ring.line)
        def _(k, ky=ky):
            keep(term.at[k, ky], terms(ring.block(k, ky)))
            to_y(k, ky).start()

    @pl.loop(1, ring.line)
    def _(k):
        keep(own_grad_ref, terms(ring.block(k, 0)))
        for ky in range(1, ring.ny):
            to_y(k, ky).wait_recv()
            own_grad_ref[...] += from_y[k, ky].astype(F32)
        on_z[k] = own_grad_ref[...].astype(BF)
        to_z(k).start()

    @pl.loop(0, ring.ny)
    def _(step):
        ky = lax.rem(step + 1, ring.ny)
        pair = terms(ring.block(0, ky))

        @pl.when(ky > 0)
        def _():
            keep(term.at[0, ky], pair)
            to_y(0, ky).start()

        @pl.when(ky == 0)
        def _():
            keep(own_grad_ref, pair)

    for head in range(HQ):
        place = pl.ds(head * local, local)
        q_grad_ref[:, head * HD : (head + 1) * HD] = acc[:, place].T
    for ky in range(1, ring.ny):
        to_y(0, ky).wait_recv()
        own_grad_ref[...] += from_y[0, ky].astype(F32)
    for k in range(1, ring.line):
        to_z(k).wait_recv()
        own_grad_ref[...] += from_z[k].astype(F32)
        to_z(k).wait_send()
    for k in range(ring.line):
        for ky in range(1, ring.ny):
            to_y(k, ky).wait_send()


IN_VMEM = pl.BlockSpec(memory_space=pltpu.VMEM)


def kernel_settings(number):
    return dict(
        compiler_params=pltpu.CompilerParams(
            collective_id=number, has_side_effects=True, vmem_limit_bytes=56 << 20
        ),
        cost_estimate=pl.CostEstimate(
            flops=5 * 10**10, bytes_accessed=16 << 20, transcendentals=0
        ),
    )


def gather_attend(sizes, own, raw, gain, cosine, sine, marks):
    local, wide = raw.shape
    _, _, nw, nz, ny = sizes
    line = nw * nz
    full = jax.ShapeDtypeStruct((line * ny * local, own.shape[1]), BF)
    return pl.pallas_call(
        functools.partial(gather_attend_kernel, sizes),
        out_shape=(
            full,
            jax.ShapeDtypeStruct((local, wide), BF),
            jax.ShapeDtypeStruct((local, wide), BF),
            jax.ShapeDtypeStruct((1, HQ * local), F32),
        ),
        in_specs=[IN_VMEM] * 9,
        out_specs=(pl.BlockSpec(memory_space=pl.ANY), IN_VMEM, IN_VMEM, IN_VMEM),
        scratch_shapes=[
            pltpu.VMEM(full.shape, BF),
            pltpu.VMEM((HD, HQ * local), F32),
            pltpu.VMEM((1, HQ * local), F32),
            pltpu.SemaphoreType.DMA((line, ny)),
            pltpu.SemaphoreType.DMA((line, ny)),
            pltpu.SemaphoreType.DMA,
        ],
        **kernel_settings(0),
    )(own, raw, gain, cosine, sine, *marks)


def attend_back(sizes, queries, grads, logs, delta, key_values, marks):
    local, wide = queries.shape
    _, _, nw, nz, ny = sizes
    line = nw * nz
    width = key_values.shape[1]
    return pl.pallas_call(
        functools.partial(attend_back_kernel, sizes),
        out_shape=(
            jax.ShapeDtypeStruct((local, wide), F32),
            jax.ShapeDtypeStruct((local, width), F32),
        ),
        in_specs=[IN_VMEM] * 9,
        out_specs=(IN_VMEM, IN_VMEM),
        scratch_shapes=[
            pltpu.VMEM((HD, HQ * local), F32),
            pltpu.VMEM((line, ny, local, width), BF),
            pltpu.VMEM((line, ny, local, width), BF),
            pltpu.VMEM((line, local, width), BF),
            pltpu.VMEM((line, local, width), BF),
            pltpu.SemaphoreType.DMA((line, ny)),
            pltpu.SemaphoreType.DMA((line, ny)),
            pltpu.SemaphoreType.DMA((line, 1)),
            pltpu.SemaphoreType.DMA((line, 1)),
        ],
        **kernel_settings(1),
    )(queries, grads, logs, delta, key_values, *marks)


class Attention:
    def __init__(self, positions, segment_ids, query_pos, query_seg):
        local = query_pos.shape[0]
        self.local = local
        self.blocks = positions.shape[0] // local
        pos = positions.reshape(self.blocks, local)
        seg = segment_ids.reshape(self.blocks, local)
        seg_low, seg_high = jnp.min(seg, axis=1), jnp.max(seg, axis=1)
        late = jnp.min(pos, axis=1) > jnp.max(query_pos)
        foreign = (seg_low > 0) & (
            (seg_low > jnp.max(query_seg)) | (seg_high < jnp.min(query_seg))
        )
        self.live = jnp.where(late | foreign, 0, 1).astype(jnp.int32)
        self.marks = (
            positions.reshape(-1, 1),
            segment_ids.reshape(-1, 1),
            query_pos.reshape(1, -1),
            query_seg.reshape(1, -1),
        )

    def specs(self):
        local = self.local
        whole = lambda *shape: pl.BlockSpec(shape, lambda j, live: (0,) * len(shape))
        rows = lambda width: pl.BlockSpec((local, width), lambda j, live: (j, 0))
        marks = [rows(1), rows(1), whole(1, local), whole(1, local)]
        return whole, rows, marks

    def forward(self, queries, key_values):
        local, wide = queries.shape
        whole, rows, marks = self.specs()
        return pl.pallas_call(
            forward_kernel,
            out_shape=(
                jax.ShapeDtypeStruct((local, wide), BF),
                jax.ShapeDtypeStruct((1, HQ * local), F32),
            ),
            grid_spec=pltpu.PrefetchScalarGridSpec(
                num_scalar_prefetch=1,
                grid=(self.blocks,),
                in_specs=[whole(local, wide), rows(2 * HD)] + marks,
                out_specs=(whole(local, wide), whole(1, HQ * local)),
                scratch_shapes=[
                    pltpu.VMEM((HD, HQ * local), F32),
                    pltpu.VMEM((1, HQ * local), F32),
                ],
            ),
            cost_estimate=pl.CostEstimate(
                flops=20 * 4 * local * local * HD, bytes_accessed=8 << 20, transcendentals=0
            ),
        )(self.live, queries, key_values, *self.marks)

    def backward(self, queries, grads, logs, delta, key_values):
        local, wide = queries.shape
        whole, rows, marks = self.specs()
        return pl.pallas_call(
            backward_kernel,
            out_shape=(
                jax.ShapeDtypeStruct((local, wide), F32),
                jax.ShapeDtypeStruct(key_values.shape, BF),
            ),
            grid_spec=pltpu.PrefetchScalarGridSpec(
                num_scalar_prefetch=1,
                grid=(self.blocks,),
                in_specs=[
                    whole(local, wide),
                    whole(local, wide),
                    whole(1, HQ * local),
                    whole(1, HQ * local),
                    rows(2 * HD),
                ]
                + marks,
                out_specs=(whole(local, wide), rows(2 * HD)),
                scratch_shapes=[pltpu.VMEM((HD, HQ * local), F32)],
            ),
            cost_estimate=pl.CostEstimate(
                flops=20 * 10 * local * local * HD, bytes_accessed=16 << 20, transcendentals=0
            ),
        )(self.live, queries, grads, logs, delta, key_values, *self.marks)


def body(
    sizes,
    tokens,
    attention_gain,
    query_weight,
    key_weight,
    value_weight,
    query_gain,
    key_gain,
    output_weight,
    mixed_gain,
    feed_gain,
    gate_weight,
    up_weight,
    down_weight,
    final_gain,
    segment_ids,
    positions,
    cotangent,
):
    place = Place(sizes)
    nx, _, nw, nz, ny = sizes
    chips = nx * nw * nz * ny
    core = place.at["core"]
    local, model = tokens.shape
    rows = query_weight.shape[0]
    wide = HQ * HD
    offset = place.ctx_chip(place.at) * local
    query_pos = lax.dynamic_slice_in_dim(positions, offset, local)
    query_seg = lax.dynamic_slice_in_dim(segment_ids, offset, local)

    def pick(pair, which):
        return lax.dynamic_index_in_dim(pair, which, 0, keepdims=False)

    def cores_in_order(own, other):
        return jnp.where(core == 0, jnp.stack([own, other]), jnp.stack([other, own]))

    outside = np.arange(model).reshape(nx, 2, nw, nz, ny, rows)
    inside = outside.transpose(1, 2, 3, 0, 4, 5).reshape(-1)
    first = outside.transpose(0, 4, 2, 3, 1, 5).reshape(-1)

    def order_change(source, target):
        at = jnp.asarray(np.argsort(source)[target], jnp.int32)
        return (lax.iota(jnp.int32, model)[:, None] == at[None, :]).astype(BF)

    outside = np.arange(model)
    to_inside = order_change(outside, inside)
    to_outside = order_change(inside, outside)
    to_first = order_change(outside, first)
    inside_from_first = order_change(inside, first)

    def reorder(values, matrix):
        if values.dtype == F32:
            return jnp.dot(values, matrix.astype(F32), precision=lax.Precision.HIGHEST)
        return matmul(values, matrix).astype(BF)

    def column_halves(query, key, value):
        cut = lambda m: m.reshape(m.shape[0], 2, -1)
        halves = jnp.concatenate([cut(query), cut(key), cut(value)], axis=2)
        return jnp.moveaxis(halves, 1, 0)

    head_width = wide // 2 + HD
    gains = jnp.concatenate(
        [mixed_gain, feed_gain, final_gain, query_gain, key_gain, attention_gain]
    )
    gain_count = gains.size
    projections = column_halves(query_weight, key_weight, value_weight)
    gain_rows = -(-gain_count // head_width) * 8
    gain_block = jnp.zeros((gain_rows * head_width,), BF).at[:gain_count].set(gains)
    small = jnp.concatenate(
        [gain_block.reshape(gain_rows, head_width), reorder(output_weight, to_inside).reshape(-1, head_width)]
    )
    first_own = jnp.concatenate(
        [
            cores_in_order(pick(projections, core), place.swap_core(pick(projections, 1 - core))).reshape(
                2 * rows, head_width
            ),
            small,
        ]
    )
    first_all, first_came, next_came = place.gather_chips(first_own)

    gate_weight, up_weight, down_weight, tokens, cotangent, _ = lax.optimization_barrier(
        (gate_weight, up_weight, down_weight, tokens, cotangent, first_own)
    )
    part = FF // (nx * ny)
    gate_up = jnp.stack([gate_weight, up_weight]).reshape(2, rows, nx, 2 * nw * nz, ny, -1)
    gate_up = jnp.transpose(gate_up, (2, 4, 0, 1, 3, 5)).reshape(nx, ny, 2, rows, part)
    down_own = reorder(down_weight, to_inside)
    down_full = place.gather_line(down_own)
    first_other = place.swap_core(first_all)

    def in_order(own, other):
        return jnp.where(core == 0, own, other), jnp.where(core == 0, other, own)

    first_all, first_other = (
        block.reshape(chips, first_own.shape[0], head_width) for block in (first_all, first_other)
    )
    projections = tuple(
        block[:, : 2 * rows].reshape(model, head_width) for block in (first_all, first_other)
    )
    gains_all = jnp.stack(
        in_order(*(block[:, 2 * rows, :gain_count] for block in (first_all, first_other)))
    )
    gains_all = jnp.moveaxis(gains_all.astype(F32), 0, 1)
    spans = np.cumsum([0, rows, rows, rows, query_gain.size, key_gain.size, rows])
    mixed_scale, feed_scale, final_scale, query_scale, key_scale, gain_one = (
        gains_all[:, :, a:b] for a, b in zip(spans[:-1], spans[1:])
    )
    gain_first = gain_one.reshape(model)

    def inside_order(values):
        values = values.reshape(nx, ny, nw, nz, 2, rows)
        return jnp.transpose(values, (4, 2, 3, 0, 1, 5)).reshape(-1)

    gain_one, mixed_scale, feed_scale, final_scale = (
        inside_order(g) for g in (gain_one, mixed_scale, feed_scale, final_scale)
    )

    def true_order(values):
        values = values.reshape(nx, ny, nw, nz, 2, -1)
        return jnp.transpose(values, (0, 4, 2, 3, 1, 5)).reshape(-1)

    query_scale, key_scale = true_order(query_scale), true_order(key_scale)

    tokens_in = reorder(tokens, to_inside).astype(F32)
    tokens_first = reorder(tokens, to_first).astype(F32)
    out_grad = reorder(cotangent, to_inside).astype(F32)
    factor_one = rms_factor(tokens_in)
    normed = (tokens_first * factor_one * gain_first).astype(BF)
    raw = in_order(*(matmul(normed, half) for half in projections))
    heads_half = wide // 2

    def both_halves(at, width):
        return [half[:, at : at + width] for half in raw]

    query_raw = [
        piece[:, h * HD : (h + 1) * HD]
        for piece in both_halves(0, heads_half)
        for h in range(HQ // 2)
    ]
    key_raw = jnp.concatenate(both_halves(heads_half, HD // 2), axis=1)
    value_rows = jnp.concatenate(both_halves(heads_half + HD // 2, HD // 2), axis=1).astype(BF)
    cosine, sine = angles_of(query_pos)
    key_factor = rms_factor(key_raw)
    key_rows = rotate(key_raw * key_factor * key_scale, cosine, sine).astype(BF)
    own_key_values = jnp.concatenate([key_rows, value_rows], axis=1)
    gate_up = place.deal_plane(gate_up, [first_came], next_came + [own_key_values])
    gate_own, up_own = (gate_up[:, :, i].reshape(-1, part) for i in range(2))
    gate_full, up_full = place.gather_line(gate_own), place.gather_line(up_own)
    own_key_values = after(own_key_values, gate_own, up_own, down_full)
    attention = Attention(positions, segment_ids, query_pos, query_seg)
    together = nw * nz * ny <= 8
    if together:
        key_values, queries, attended, logs = gather_attend(
            sizes,
            own_key_values,
            jnp.concatenate(query_raw, axis=1),
            query_scale.reshape(1, -1),
            cosine,
            sine,
            attention.marks,
        )
    else:
        key_values = place.gather_group(own_key_values)
        queries = jnp.concatenate(
            [
                rotate(q * rms_factor(q) * query_scale, cosine, sine).astype(BF)
                for q in query_raw
            ],
            axis=1,
        )
        attended, logs = attention.forward(queries, key_values)
    query_factor = [rms_factor(q) for q in query_raw]
    first_all, first_other, projections, query_factor = lax.optimization_barrier(
        (first_all, first_other, projections, query_factor, attended)
    )[:4]
    output_full = jnp.stack(
        in_order(*(block[:, 2 * rows + gain_rows :] for block in (first_all, first_other)))
    )
    output_full = jnp.transpose(
        output_full.reshape(2, nx, ny, nw * nz, -1, model), (1, 0, 3, 2, 4, 5)
    ).reshape(wide, model)
    projected = matmul(attended, output_full)
    factor_three = rms_factor(projected)
    mixed = tokens_in + projected * factor_three * mixed_scale
    factor_two = rms_factor(mixed)
    normed_two = (mixed * factor_two * feed_scale).astype(BF)
    near_blocks = place.gather_near(normed_two)
    def gelu_parts(value):
        scale = (2.0 / np.pi) ** 0.5
        square = value * value
        bend = jnp.tanh(scale * (value + 0.044715 * (square * value)))
        rise = 0.5 * (1.0 + bend)
        slope = 0.5 * value * (1.0 - bend * bend) * (scale * (1.0 + 3 * 0.044715 * square))
        return value * rise, rise + slope

    kept, hidden_blocks, branch_parts = [], [], []
    normed_blocks = [normed_two]
    for number in range(nx * ny):
        if number == 1:
            normed_blocks = place.gather_far(near_blocks, hidden_blocks[0])
        block = normed_blocks[number]
        gate_pre, up_pre = matmul(block, gate_full), matmul(block, up_full)
        gelu, gelu_slope = gelu_parts(gate_pre)
        kept.append(((gelu_slope * up_pre).astype(BF), gelu.astype(BF)))
        hidden_blocks.append((gelu * up_pre).astype(BF))
        branch_parts.append(matmul(hidden_blocks[-1], down_full))
    branch = place.scatter_plane(branch_parts)
    factor_four = rms_factor(branch)
    layer_out = reorder((mixed + branch * factor_four * final_scale).astype(BF), to_outside)

    branch_grad, final_term = norm_back(out_grad, branch, factor_four, final_scale)
    branch_grad = branch_grad.astype(BF)
    near_blocks = place.gather_near(branch_grad)
    branch_grad_blocks = [branch_grad]
    gate_grads, up_grads, normed_two_parts = [], [], []
    for number, factors in enumerate(kept):
        if number == 1:
            branch_grad_blocks = place.gather_far(near_blocks, normed_two_parts[0])
        block = branch_grad_blocks[number]
        hidden_grad = matmul_nt(block, down_full)
        gate_grad, up_grad = ((hidden_grad * f.astype(F32)).astype(BF) for f in factors)
        gate_grads.append(gate_grad)
        up_grads.append(up_grad)
        normed_two_parts.append(matmul_nt(gate_grad, gate_full) + matmul_nt(up_grad, up_full))
    normed_two_grad = place.scatter_plane(normed_two_parts)
    halfway = place.halfway
    normed_all = jnp.concatenate(normed_blocks)
    hidden_all = jnp.concatenate(hidden_blocks)
    down_terms = matmul_tn(
        after(hidden_all, normed_two_parts[-1]), jnp.concatenate(branch_grad_blocks)
    ).astype(BF)
    gate_terms = matmul_tn(normed_all, after(jnp.concatenate(gate_grads), *halfway)).astype(BF)
    up_terms = matmul_tn(normed_all, after(jnp.concatenate(up_grads), *halfway)).astype(BF)
    normed_two_grad = after(normed_two_grad, gate_terms, up_terms)
    down_terms = place.cores_summed(down_terms)
    gate_terms = place.cores_summed(gate_terms)
    up_terms = place.cores_summed(up_terms)
    down_rows = place.scatter_line(down_terms)
    gate_rows = place.scatter_line(gate_terms)

    mixed_part, feed_term = norm_back(normed_two_grad, mixed, factor_two, feed_scale)
    mixed_grad = out_grad + mixed_part
    projected_grad, mixed_term = norm_back(mixed_grad, projected, factor_three, mixed_scale)
    projected_grad = projected_grad.astype(BF)
    output_terms = matmul_tn(attended, projected_grad).astype(BF)
    attended_grad = matmul_nt(projected_grad, output_full).astype(BF)
    attended_grad = after(attended_grad, down_terms)
    delta = jnp.stack(
        [
            jnp.sum(
                attended_grad[:, h * HD : (h + 1) * HD].astype(F32)
                * attended[:, h * HD : (h + 1) * HD].astype(F32),
                axis=1,
            )
            for h in range(HQ)
        ]
    ).reshape(1, -1)
    if together:
        queries_grad, key_value_grad = attend_back(
            sizes, queries, attended_grad, logs, delta, key_values, attention.marks
        )
    else:
        queries_grad, key_value_terms = attention.backward(
            queries, attended_grad, logs, delta, key_values
        )
        key_value_grad = place.scatter_group(key_value_terms)
    output_terms = after(output_terms, key_value_grad)
    up_rows = place.scatter_line(up_terms)
    down_weight_grad = matmul(down_rows, to_outside)

    def whole_rows(own_part):
        dealt = place.deal_plane(own_part.reshape(nx, ny, rows, part))
        dealt = dealt.reshape(nx, ny, rows, 2 * nw * nz, -1)
        return jnp.transpose(dealt, (2, 0, 3, 1, 4)).reshape(rows, FF).astype(F32)

    gate_weight_grad, up_weight_grad = whole_rows(gate_rows), whole_rows(up_rows)
    key_grad_rows = key_value_grad[:, :HD]
    values_grad = key_value_grad[:, HD:].astype(BF)
    key_back = rotate(key_grad_rows, cosine, -sine)
    key_in_grad, key_term = norm_back(key_back, key_raw, key_factor, key_scale)
    key_in_grad = key_in_grad.astype(BF)
    query_in_grad, query_term = [], 0.0
    for h in range(HQ):
        query_back = rotate(queries_grad[:, h * HD : (h + 1) * HD], cosine, -sine)
        grad, term = norm_back(query_back, query_raw[h], query_factor[h], query_scale)
        query_in_grad.append(grad.astype(BF))
        query_term = query_term + term
    quarter = HD // 2
    raw_grad = []
    for c in range(2):
        raw_grad.append(
            jnp.concatenate(
                query_in_grad[c * HQ // 2 : (c + 1) * HQ // 2]
                + [
                    key_in_grad[:, c * quarter : (c + 1) * quarter],
                    values_grad[:, c * quarter : (c + 1) * quarter],
                ],
                axis=1,
            )
        )
    def chip_order(values):
        values = values.reshape(nx, 2, nw, nz, ny, -1)
        return jnp.transpose(values, (0, 4, 2, 3, 1, 5)).reshape(chips, 2, -1)

    def chip_order_inside(values):
        values = values.reshape(2, nw, nz, nx, ny, rows)
        return jnp.transpose(values, (3, 4, 1, 2, 0, 5)).reshape(chips, 2, rows)

    gain_terms = jnp.concatenate(
        [chip_order_inside(t) for t in (mixed_term, feed_term, final_term)]
        + [chip_order(query_term), chip_order(key_term)],
        axis=2,
    )
    gain_terms = jnp.moveaxis(gain_terms, 1, 0).astype(BF)
    gain_terms = jnp.pad(
        gain_terms, ((0, 0), (0, 0), (0, gain_rows * head_width - gain_terms.shape[2]))
    ).reshape(2, chips, gain_rows, head_width)
    output_terms = output_terms.reshape(nx, 2, nw * nz, ny, -1, model)
    output_terms = jnp.transpose(output_terms, (1, 0, 3, 2, 4, 5)).reshape(2, chips, -1, head_width)
    grads_pair = jnp.stack(raw_grad)

    def terms_of(which):
        return jnp.concatenate(
            [
                matmul_tn(normed, pick(grads_pair, which)).astype(BF).reshape(chips, 2 * rows, head_width),
                pick(gain_terms, which),
                pick(output_terms, which),
            ],
            axis=1,
        ).reshape(-1, head_width)

    first_terms = terms_of(core).astype(F32) + place.swap_core(terms_of(1 - core)).astype(F32)
    first_terms = first_terms.astype(BF)
    normed_grad = 0.0
    for half, grad in zip(in_order(*projections), raw_grad):
        half = matmul(inside_from_first, half).astype(BF)
        normed_grad = normed_grad + matmul_nt(after(grad, first_terms), half)
    tokens_part, _ = norm_back(normed_grad, tokens_in, factor_one, gain_one)
    tokens_grad = reorder((mixed_grad + tokens_part).astype(BF), to_outside)

    first_grad = place.scatter_chips(first_terms)
    projection_rows = first_grad[: 2 * rows].reshape(2, rows, head_width)
    projection_rows = cores_in_order(
        pick(projection_rows, core), place.swap_core(pick(projection_rows, 1 - core))
    )

    def whole_columns(a, b):
        return jnp.moveaxis(projection_rows[:, :, a:b], 0, 1).reshape(rows, -1)

    query_weight_grad = whole_columns(0, heads_half)
    key_weight_grad = whole_columns(heads_half, heads_half + quarter)
    value_weight_grad = whole_columns(heads_half + quarter, head_width)
    gain_grad = first_grad[2 * rows : 2 * rows + gain_rows].reshape(-1)
    (
        mixed_gain_grad,
        feed_gain_grad,
        final_gain_grad,
        query_gain_grad,
        key_gain_grad,
    ) = (gain_grad[a:b] for a, b in zip(spans[:5], spans[1:6]))
    attention_gain_grad = sum(
        jnp.sum(grad * weight.astype(F32), axis=1)
        for grad, weight in (
            (query_weight_grad, query_weight),
            (key_weight_grad, key_weight),
            (value_weight_grad, value_weight),
        )
    ) / attention_gain.astype(F32)
    output_weight_grad = reorder(first_grad[2 * rows + gain_rows :].reshape(-1, model), to_outside)
    return (
        layer_out,
        tokens_grad,
        attention_gain_grad,
        query_weight_grad,
        key_weight_grad,
        value_weight_grad,
        query_gain_grad,
        key_gain_grad,
        output_weight_grad,
        mixed_gain_grad,
        feed_gain_grad,
        gate_weight_grad,
        up_weight_grad,
        down_weight_grad,
        final_gain_grad,
    )


def solution(mesh):
    sizes = grid_of(mesh)
    grid = Mesh(mesh.devices.reshape(sizes), AXES)
    matrix, vector, group = P(AXES, None), P(AXES), P(("x", "core"))
    return jax.shard_map(
        lambda *arrays: body(sizes, *arrays),
        mesh=grid,
        in_specs=(
            matrix,
            vector,
            matrix,
            matrix,
            matrix,
            vector,
            vector,
            matrix,
            vector,
            vector,
            matrix,
            matrix,
            matrix,
            vector,
            group,
            group,
            matrix,
        ),
        out_specs=(
            matrix,
            matrix,
            vector,
            matrix,
            matrix,
            matrix,
            vector,
            vector,
            matrix,
            vector,
            vector,
            matrix,
            matrix,
            matrix,
            vector,
        ),
        check_vma=False,
    )
```
